256 devices in a mesh: ifg: 8 (over x, core), rows: 32 (over y, z).
Axes of the slice: x: 4, y: 4, z: 8, core: 2. Of those that a mesh axis runs over, the one named last changes fastest.
Arguments:
- phase: bfloat16 [512, 256, 1024], P('ifg', 'rows')
- coherence: bfloat16 [512, 256, 1024], P('ifg', 'rows'), may hold values from 0.0996 to 0.95
- height: float32 [256, 1024], P('rows')
- gap_mask: int32 [512, 256], P('ifg', 'rows'), may hold values 0 or 1
- date_pairs: int32 [512, 2], replicated, may hold values from 0 to 299, as said below
Outputs:
- displacement: float32 [300, 256, 1024], P(None, 'rows', 'ifg')
- topo_slope: float32 [512], P('ifg')
The draws below stay inside these ranges and needn't reach their ends.
Inputs may be any that keep to these rules, and one draw needn't show every extreme that they name: date_pairs[i, 0] < date_pairs[i, 1] for every interferogram.
All inputs are finite; a program needn't handle non-finite values. No bound on the sum of `gap_mask` on one device may be relied on, other than what follows from the above.
Results may differ from the reference program's by a relative error of at most 0.0028.
Values may be sent and summed in bfloat16 or wider, within the bound.
No kernel may reach another device: no remote copies, remote signals or barrier semaphores. Data moves between devices by JAX's collectives and lax.ppermute only.
A program may use at most 128 MiB of HBM per device.

```python
import jax
import jax.numpy as jnp
from jax import lax

IFGS = 512
DATES = 300
R_DEV = 8
C_DEV = 128
ITERS = 3
IMG_ROWS = 256
COLS = 1024
N_ROWS = 32


def height_field(key):
    height_key = jax.random.fold_in(key, 11)
    row_ramp = 1.0 + 2.0 * jnp.arange(IMG_ROWS, dtype=jnp.float32) / IMG_ROWS
    rough = jnp.clip(jax.random.normal(height_key, (IMG_ROWS, COLS), jnp.float32), -6.0, 6.0)
    return jnp.clip(row_ramp[:, None] * rough, -18.0, 18.0)


def draw_height(key, part):
    return height_field(key)


def draw_phase(key, part):
    terrain = height_field(key)
    slopes = jax.random.uniform(jax.random.fold_in(key, 23), (IFGS,), jnp.float32, -0.5, 0.5)
    noise_key = jax.random.fold_in(key, 31)
    noise_field = jnp.clip(jax.random.normal(noise_key, (IFGS, IMG_ROWS, COLS), jnp.float32), -6.0, 6.0)
    return (noise_field + slopes[:, None, None] * terrain[None]).astype(jnp.bfloat16)


def draw_coherence(key, part):
    base_key = jax.random.fold_in(key, 51)
    shape = (IFGS, IMG_ROWS, COLS)
    base = jax.random.uniform(base_key, shape, jnp.float32)
    col_blocks = COLS // C_DEV
    order = jax.random.permutation(jax.random.fold_in(key, 53), col_blocks).astype(jnp.float32)
    col_level = -1.5 + 3.0 * order / (col_blocks - 1)
    row_level = jax.random.uniform(jax.random.fold_in(key, 57), (IMG_ROWS // R_DEV,), jnp.float32, -0.75, 0.75)
    exponent = jnp.exp(jnp.repeat(row_level, R_DEV)[:, None] + jnp.repeat(col_level, C_DEV)[None, :])
    return (0.1 + 0.85 * jnp.power(base, exponent[None])).astype(jnp.bfloat16)


def draw_date_pairs(key, part):
    earlier = jax.random.randint(jax.random.fold_in(key, 41), (IFGS,), 0, DATES - 1)
    date_gap = jax.random.randint(jax.random.fold_in(key, 43), (IFGS,), 1, 13)
    earlier = earlier.at[0].set(0)
    later = jnp.minimum(earlier + date_gap, DATES - 1)
    later = later.at[IFGS - 1].set(DATES - 1)
    return jnp.stack([earlier, later], axis=1).astype(jnp.int32)


def plant(array, stream_key, low, top_value):
    place = [jax.random.randint(jax.random.fold_in(stream_key, axis), (), 0, length) for axis, length in enumerate(array.shape)]
    longest = array.shape.index(max(array.shape))
    beside = place[:longest] + [(place[longest] + 1) % array.shape[longest]] + place[longest + 1:]
    return array.at[tuple(place)].set(low).at[tuple(beside)].set(top_value)


def setup_inputs(seed: int = 0) -> dict:
    key_list = jax.random.split(jax.random.key(seed), 6)
    phase = draw_phase(jax.random.fold_in(key_list[5], 71), 0)
    coherence = draw_coherence(jax.random.fold_in(key_list[5], 71), 0)
    height = draw_height(jax.random.fold_in(key_list[5], 71), 0)
    gap_mask = plant((jax.random.randint(key_list[3], (IFGS, IMG_ROWS), 0, 8) < 7).astype(jnp.int32), jax.random.fold_in(key_list[3], 1), 0, 1)
    date_pairs = draw_date_pairs(jax.random.fold_in(key_list[5], 71), 0)
    return {"phase": phase, "coherence": coherence, "height": height, "gap_mask": gap_mask, "date_pairs": date_pairs}


SMOOTHING_WEIGHT = 0.5
RIDGE_WEIGHT = 0.05


def box_sum(values):
    padded = jnp.pad(values, 1)
    row_sum = padded[:-2] + padded[1:-1] + padded[2:]
    return row_sum[:, :-2] + row_sum[:, 1:-1] + row_sum[:, 2:]


def reference(phase, coherence, height, gap_mask, date_pairs):
    def per_interferogram(entries):
        phase_one, coher_one, mask_one = entries
        coher_f = coher_one.astype(jnp.float32)
        top_sum = box_sum(coher_f * phase_one.astype(jnp.float32))
        low_sum = box_sum(coher_f)
        smooth = top_sum / low_sum
        mean_coh = low_sum / 9.0
        topo = jnp.sum(mean_coh * smooth * height) / jnp.sum(mean_coh * height * height)
        corrected = (smooth - topo * height).astype(jnp.bfloat16)
        weights = (mask_one.astype(jnp.float32)[:, None] * mean_coh).astype(jnp.bfloat16)
        return corrected, weights, topo

    corrected, weights, topo_slope = lax.map(per_interferogram, (phase, coherence, gap_mask))
    earlier = date_pairs[:, 0]
    later = date_pairs[:, 1]

    def slab_term(values, use_field):
        def one_slab(slab_index):
            start = (slab_index * R_DEV).astype(jnp.int32)
            weight_slab = lax.dynamic_slice_in_dim(weights, start, R_DEV, 1).astype(jnp.float32)
            if use_field:
                value_slab = lax.dynamic_slice_in_dim(values, start, R_DEV, 1)
                diffs = jnp.take(value_slab, later, axis=0) - jnp.take(value_slab, earlier, axis=0)
            else:
                diffs = lax.dynamic_slice_in_dim(corrected, start, R_DEV, 1).astype(jnp.float32)
            scaled = diffs * weight_slab
            return (jax.ops.segment_sum(scaled, later, DATES) - jax.ops.segment_sum(scaled, earlier, DATES))

        stacked = lax.map(one_slab, jnp.arange(N_ROWS, dtype=jnp.int32))
        return stacked.transpose(1, 0, 2, 3).reshape(DATES, IMG_ROWS, COLS)

    def operate(values):
        padded = jnp.pad(values, ((0, 0), (1, 1), (1, 1)))
        neighbours = padded[:, 2:, 1:-1] + padded[:, :-2, 1:-1] + padded[:, 1:-1, 2:] + padded[:, 1:-1, :-2]
        spread = 4.0 * values - neighbours
        return slab_term(values, True) + SMOOTHING_WEIGHT * spread + RIDGE_WEIGHT * values

    right_side = slab_term(None, False)
    displacement = jnp.zeros_like(right_side)
    residual, direction = right_side, right_side
    norm_now = jnp.sum(residual * residual)
    for sweep_index in range(ITERS):
        mapped = operate(direction)
        step_size = norm_now / jnp.sum(direction * mapped)
        displacement = displacement + step_size * direction
        residual = residual - step_size * mapped
        norm_next = jnp.sum(residual * residual)
        direction = residual + (norm_next / norm_now) * direction
        norm_now = norm_next
    return displacement, topo_slope
```

```python
import jax
import jax.numpy as jnp
from jax import lax
from jax.experimental import pallas as pl
from jax.experimental.pallas import tpu as pltpu
from jax.sharding import PartitionSpec as P

DATES = 300
DP = 304
SHIFT = 4.0
SMOOTHING_WEIGHT = 0.5
RIDGE_WEIGHT = 0.05
CENTRE = 4.0 * SMOOTHING_WEIGHT + RIDGE_WEIGHT - SHIFT
F32 = jnp.float32
BF16 = jnp.bfloat16
PARAMS = pltpu.CompilerParams(vmem_limit_bytes=48 * 1024 * 1024)


def sds(shape, dtype):
    return jax.ShapeDtypeStruct(shape, dtype)


def call(body, outs, *args, scratch=(), name=None):
    return pl.pallas_call(
        body,
        out_shape=outs,
        scratch_shapes=list(scratch),
        compiler_params=PARAMS,
        name=name,
    )(*args)


def dot(a, b):
    return jnp.dot(a, b, preferred_element_type=F32)


def split(values):
    high = values.astype(BF16)
    return high, (values - high.astype(F32)).astype(BF16)


def rows_first(phase, coher, phase_t, coher_t, first, last, wide):
    for part, (source, target) in enumerate(((phase, phase_t), (coher, coher_t))):
        for block in range(4):
            for tile in range(8):
                lanes = pl.ds(tile * 128, 128)
                wide[...] = source[pl.ds(block * 16, 16), :, lanes].astype(F32).reshape(128, 128)
                for row in range(8):
                    piece = wide[pl.ds(row, 16, stride=8), :].astype(BF16)
                    target[row, pl.ds(block * 16, 16), lanes] = piece
        first[pl.ds(part * 64, 64), :] = target[0]
        last[pl.ds(part * 64, 64), :] = target[7]


def shifted_sum(values, lane, last):
    left = jnp.where(lane == 0, 0.0, pltpu.roll(values, 1, 1))
    right = jnp.where(lane == last, 0.0, pltpu.roll(values, last, 1))
    return values + left + right


def regression_sums(phase_t, coher_t, height, above, below, out, box_one, box_two):
    lane = lax.broadcasted_iota(jnp.int32, (8, 1024), 1)
    sub = lax.broadcasted_iota(jnp.int32, (8, 1024), 0)
    here = height[...]
    up = jnp.where(sub == 0, above[...], pltpu.roll(here, 1, 0))
    down = jnp.where(sub == 7, below[...], pltpu.roll(here, 7, 0))
    box_one[...] = shifted_sum(here + up + down, lane, 1023)
    box_two[...] = shifted_sum(here * here + up * up + down * down, lane, 1023)
    tops, lows = [], []
    for block in range(4):
        top = jnp.zeros((16, 128), F32)
        low = jnp.zeros((16, 128), F32)
        for row in range(8):
            for tile in range(8):
                lanes = pl.ds(tile * 128, 128)
                coher = coher_t[row, pl.ds(block * 16, 16), lanes].astype(F32)
                phase = phase_t[row, pl.ds(block * 16, 16), lanes].astype(F32)
                top += coher * phase * box_one[pl.ds(row, 1), lanes]
                low += coher * box_two[pl.ds(row, 1), lanes]
        tops.append(top)
        lows.append(low)
    sums = jnp.sum(jnp.concatenate(tops + lows, axis=0).T, axis=0, keepdims=True)
    out[...] = jnp.broadcast_to(sums, out.shape)


def smoothing(phase_t, coher_t, above, below, mask, smooth, weights):
    lane = lax.broadcasted_iota(jnp.int32, (16, 1024), 1)

    def group(block, _):
        ifgs = pl.ds(pl.multiple_of(block * 16, 16), 16)
        cohers = pl.ds(pl.multiple_of(block * 16 + 64, 16), 16)
        masks = mask[ifgs, :]

        def load(row):
            if row < 0 or row > 7:
                edge = above if row < 0 else below
                coher = edge[cohers, :].astype(F32)
                return coher, coher * edge[ifgs, :].astype(F32)
            coher = coher_t[row, ifgs, :].astype(F32)
            return coher, coher * phase_t[row, ifgs, :].astype(F32)

        before, current = load(-1), load(0)
        for row in range(8):
            after = load(row + 1)
            denom = shifted_sum(before[0] + current[0] + after[0], lane, 1023)
            numer = shifted_sum(before[1] + current[1] + after[1], lane, 1023)
            smooth[row, ifgs, :] = numer / denom
            weight = (masks[:, row : row + 1] * (denom / 9.0)).astype(BF16)
            for tile in range(8):
                weights[tile, ifgs, pl.ds(row * 128, 128)] = weight[:, tile * 128 : tile * 128 + 128]
            before, current = current, after
        return 0

    lax.fori_loop(0, 4, group, 0)


def pick_blocks(source, owner, outs):
    for step, out in enumerate(outs):
        out[...] = source[(owner[0] + step) % 8]


def weight_blocks(owner, weights, *outs):
    pick_blocks(weights, owner, outs)


def correction(owner, sums, smooth, height, slope_row, *rest):
    outs, blocks = rest[:8], rest[8]
    total = sums[0] + sums[1] + sums[2] + sums[3]
    slope_row[...] = total / pltpu.roll(total, 64, 1)
    column = jnp.broadcast_to(total[0:1, :], (128, 128)).T
    slope = column[:64, :] / column[64:, :]
    for row in range(8):
        for tile in range(8):
            lanes = pl.ds(tile * 128, 128)
            value = smooth[row, :, lanes] - slope * height[pl.ds(row, 1), lanes]
            blocks[tile, :, pl.ds(row * 128, 128)] = value.astype(BF16)
    pick_blocks(blocks, owner, outs)


def column_selector():
    row = lax.broadcasted_iota(jnp.int32, (16, 1024), 0)
    pixel = lax.broadcasted_iota(jnp.int32, (16, 1024), 1)
    wanted = jnp.where(row < 8, row * 128, (row - 8) * 128 + 127)
    return (pixel == wanted).astype(BF16)


def write_edges(field, first, last, columns):
    first[...] = field[:, pl.ds(0, 128)].astype(BF16)
    last[...] = field[:, pl.ds(896, 128)].astype(BF16)
    picked = lax.dot_general(
        column_selector(), field[...].astype(BF16), (((1,), (1,)), ((), ())), preferred_element_type=F32
    )
    columns[...] = picked.astype(BF16)


def right_side(*refs):
    weight_parts, corrected_parts = refs[:8], refs[8:16]
    design_t, field, weights, first, last, columns = refs[16:]
    for part in range(8):
        weights[pl.ds(part * 64, 64), :] = weight_parts[part][...]
    for chunk in range(4):
        lanes = pl.ds(chunk * 256, 256)
        total = jnp.zeros((DP, 256), F32)
        scaled = jnp.concatenate(
            [
                weight_parts[part][:, lanes].astype(F32) * corrected_parts[part][:, lanes].astype(F32)
                for part in range(8)
            ],
            axis=0,
        )
        high, low = split(scaled)
        field[:, lanes] = dot(design_t[...], high) + dot(design_t[...], low)
    write_edges(field, first, last, columns)


def local_image(field, weights, design, design_t, chunk):
    lanes = pl.ds(chunk * 256, 256)
    high, low = split(field[:, lanes])
    scaled = (dot(design[...], high) + dot(design[...], low)) * weights[:, lanes].astype(F32)
    high, low = split(scaled)
    back = dot(design_t[...], high) + dot(design_t[...], low)
    lane = lax.broadcasted_iota(jnp.int32, (DP, 128), 1)
    parts = []
    for row in (2 * chunk, 2 * chunk + 1):
        here = field[:, pl.ds(row * 128, 128)]
        around = jnp.where(lane == 0, 0.0, pltpu.roll(here, 1, 1))
        around += jnp.where(lane == 127, 0.0, pltpu.roll(here, 127, 1))
        if row > 0:
            around += field[:, pl.ds((row - 1) * 128, 128)]
        if row < 7:
            around += field[:, pl.ds((row + 1) * 128, 128)]
        start = (row - 2 * chunk) * 128
        parts.append(back[:, start : start + 128] + CENTRE * here - SMOOTHING_WEIGHT * around)
    return parts


def fold(values):
    return jnp.sum(values.reshape(DP // 8, 8, 128), axis=0)


def apply_local(with_before, with_image, *refs):
    field, weights, design, design_t = refs[:4]
    refs = refs[4:]
    before = None
    if with_before:
        before, refs = refs[0], refs[1:]
    image = None
    if with_image:
        image, refs = refs[0], refs[1:]
    moments = refs[0]
    square = jnp.zeros((8, 128), F32)
    cross = jnp.zeros((8, 128), F32)
    ahead = jnp.zeros((8, 128), F32)
    for chunk in range(4):
        parts = local_image(field, weights, design, design_t, chunk)
        for offset, part in enumerate(parts):
            lanes = pl.ds((2 * chunk + offset) * 128, 128)
            here = field[:, lanes]
            square += fold(here * here)
            if with_before:
                cross += fold(here * before[:, lanes])
            if with_image:
                image[:, lanes] = part
            else:
                ahead += fold(here * part)
    moments[0] = square
    moments[1] = cross
    moments[2] = ahead


def spread_columns(columns, pixels):
    row = lax.broadcasted_iota(jnp.int32, (16, 128), 0)
    lane = lax.broadcasted_iota(jnp.int32, (16, 128), 1)
    wanted = jnp.where(row < 8, row, row - 8) == pixels
    place = (wanted & (lane == jnp.where(row < 8, 0, 127))).astype(BF16)
    return lax.dot_general(columns, place, (((0,), (0,)), ((), ())), preferred_element_type=F32)


def halo_part(row, above, below, columns):
    halo = spread_columns(columns, row)
    if row == 0:
        halo += above[...].astype(F32)
    if row == 7:
        halo += below[...].astype(F32)
    return halo


def join_columns(left, right):
    return jnp.concatenate([left[8:16, :], right[0:8, :]], axis=0)


def add_halo(image, above, below, left, right, field, first, last, columns):
    sides = join_columns(left, right)
    for row in range(8):
        lanes = pl.ds(row * 128, 128)
        field[:, lanes] = image[:, lanes] - SMOOTHING_WEIGHT * halo_part(row, above, below, sides)
    write_edges(field, first, last, columns)


def all_moments(field, above, below, left, right, zero, one, two, out):
    sides = join_columns(left, right)
    ahead = two[2]
    for row in range(8):
        lanes = pl.ds(row * 128, 128)
        ahead -= SMOOTHING_WEIGHT * fold(field[:, lanes] * halo_part(row, above, below, sides))
    rows = [zero[0], one[1], one[0], two[1], two[0], ahead]
    sums = [jnp.sum(values, axis=0, keepdims=True) for values in rows]
    out[...] = jnp.concatenate(sums + [jnp.zeros((2, 128), F32)], axis=0)


def combine(parts, zero, one, two, out):
    total = parts[0]
    for index in range(1, parts.shape[0]):
        total += parts[index]
    sums = jnp.sum(total, axis=1, keepdims=True)
    m0, m1, m2, m3, m4, m5 = (jnp.broadcast_to(sums[i : i + 1, :], (1, 128)) for i in range(6))
    t00, t01, t11 = m1 + SHIFT * m0, m2 + SHIFT * m1, m3 + SHIFT * m2
    t12, t22 = m4 + SHIFT * m3, m5 + SHIFT * m4
    l10, l20 = t01 / t00, t11 / t00
    pivot = t11 - l10 * t01
    off = t12 - l20 * t01
    keep = pivot > 1e-6 * t11
    safe = jnp.where(keep, pivot, 1.0)
    l21 = jnp.where(keep, off / safe, 0.0)
    last = t22 - l20 * t11 - l21 * off
    keep_last = keep & (last > 1e-6 * t22)
    y1 = m1 - l10 * m0
    y2 = m2 - l20 * m0 - l21 * y1
    c2 = jnp.where(keep_last, y2 / jnp.where(keep_last, last, 1.0), 0.0)
    c1 = jnp.where(keep, y1 / safe, 0.0) - l21 * c2
    c0 = m0 / t00 - l10 * c1 - l20 * c2
    for row in range(8):
        lanes = pl.ds(row * 128, 128)
        value = c0 * zero[:, lanes] + c1 * one[:, lanes] + c2 * two[:, lanes]
        out[pl.ds(row, DATES, stride=8), :] = value[:DATES, :]


def swap_sum(values, axis, groups, count):
    spread = jnp.broadcast_to(values[None], (count,) + values.shape)
    return lax.all_to_all(spread, axis, 0, 0, tiled=True, axis_index_groups=groups)


def per_device(phase, coherence, height, gap_mask, date_pairs):
    n_ifg, n_rows = lax.axis_size("ifg"), lax.axis_size("rows")
    me = lax.axis_index("ifg")
    owner = me.reshape(1).astype(jnp.int32)

    def forward(values, axis):
        return lax.ppermute(values, axis, [(i, i + 1) for i in range(lax.axis_size(axis) - 1)])

    def backward(values, axis):
        return lax.ppermute(values, axis, [(i + 1, i) for i in range(lax.axis_size(axis) - 1)])

    fast_groups = [[outer * 8 + inner for inner in range(8)] for outer in range(4)]
    slow_groups = [[outer * 8 + inner for outer in range(4)] for inner in range(8)]

    height_above = forward(height[7:8], "rows")
    height_below = backward(height[0:1], "rows")
    stacked = sds((8, 64, 1024), BF16)
    edge = sds((128, 1024), BF16)
    phase_t, coher_t, first, last = call(
        rows_first,
        (stacked, stacked, edge, edge),
        phase,
        coherence,
        scratch=(pltpu.VMEM((128, 128), F32),),
        name="rows_first",
    )
    above, below = forward(last, "rows"), backward(first, "rows")
    sums = call(
        regression_sums,
        sds((8, 128), F32),
        phase_t,
        coher_t,
        height,
        height_above,
        height_below,
        scratch=(pltpu.VMEM((8, 1024), F32), pltpu.VMEM((8, 1024), F32)),
        name="regression_sums",
    )
    sums = jnp.sum(swap_sum(sums, "rows", fast_groups, 8), axis=0)
    sums = swap_sum(sums[None], "rows", slow_groups, 4).reshape(4, 8, 128)

    smooth, weights = call(
        smoothing,
        (sds((8, 64, 1024), F32), stacked),
        phase_t,
        coher_t,
        above,
        below,
        gap_mask.astype(F32),
        name="smoothing",
    )
    block = sds((64, 1024), BF16)
    vmem = pl.BlockSpec(memory_space=pltpu.VMEM)
    smem = pl.BlockSpec(memory_space=pltpu.SMEM)
    weight_parts = pl.pallas_call(
        weight_blocks,
        out_shape=[block] * 8,
        in_specs=[smem, vmem],
        compiler_params=PARAMS,
        name="weight_blocks",
    )(owner, weights)
    slope_row, *corrected_parts = pl.pallas_call(
        correction,
        out_shape=[sds((8, 128), F32)] + [block] * 8,
        in_specs=[smem, vmem, vmem, vmem],
        scratch_shapes=[pltpu.VMEM((8, 64, 1024), BF16)],
        compiler_params=PARAMS,
        name="correction",
    )(owner, sums, smooth, height)

    def exchange(parts):
        return [parts[0]] + [
            lax.ppermute(parts[k], "ifg", [(i, (i + k) % n_ifg) for i in range(n_ifg)])
            for k in range(1, n_ifg)
        ]

    weight_parts, corrected_parts = exchange(weight_parts), exchange(corrected_parts)
    order = (me - jnp.arange(n_ifg)) % n_ifg
    pairs = date_pairs.reshape(n_ifg, -1, 2)[order].reshape(-1, 2)
    dates = jnp.arange(DP, dtype=jnp.int32)
    design = ((dates[None] == pairs[:, 1:2]).astype(F32) - (dates[None] == pairs[:, 0:1]).astype(F32)).astype(BF16)
    design_t = design.T

    field = sds((DP, 1024), F32)
    edges = (sds((DP, 128), BF16), sds((DP, 128), BF16), sds((16, DP), BF16))
    moments = sds((3, 8, 128), F32)
    k0, weights, *sides = call(
        right_side,
        (field, sds((512, 1024), BF16)) + edges,
        *weight_parts,
        *corrected_parts,
        design_t,
        name="right_side",
    )

    def halos(sides):
        first, last, columns = sides
        return (
            forward(last, "rows"),
            backward(first, "rows"),
            forward(columns, "ifg"),
            backward(columns, "ifg"),
        )

    def local(with_before, with_image, name, *args):
        outs = ((field,) if with_image else ()) + (moments,)
        body = lambda *refs: apply_local(with_before, with_image, *refs)
        return call(body, outs, *args, name=name)

    around = halos(sides)
    image, mom0 = local(False, True, "apply0", k0, weights, design, design_t)
    k1, *sides = call(add_halo, (field,) + edges, image, *around, name="add_halo1")
    around = halos(sides)
    image, mom1 = local(True, True, "apply1", k1, weights, design, design_t, k0)
    k2, *sides = call(add_halo, (field,) + edges, image, *around, name="add_halo2")
    around = halos(sides)
    (mom2,) = local(True, False, "apply2", k2, weights, design, design_t, k1)
    part = call(all_moments, sds((8, 128), F32), k2, *around, mom0, mom1, mom2, name="all_moments")
    for step in (1, 2, 4):
        part = part + lax.ppermute(part, "ifg", [(i, i ^ step) for i in range(n_ifg)])
    parts = swap_sum(part[None], "rows", None, n_rows).reshape(n_rows, 8, 128)
    displacement = call(combine, sds((DATES * 8, 128), F32), parts, k0, k1, k2, name="combine")
    return displacement.reshape(DATES, 8, 128), slope_row[0, :64]


def solution(mesh):
    placed = (
        P("ifg", "rows", None),
        P("ifg", "rows", None),
        P("rows", None),
        P("ifg", "rows"),
        P(),
    )
    return jax.shard_map(
        per_device,
        mesh=mesh,
        in_specs=placed,
        out_specs=(P(None, "rows", "ifg"), P("ifg")),
        check_vma=False,
    )
```

```python
import jax
import jax.numpy as jnp
from jax import lax
from jax.experimental import pallas as pl
from jax.experimental.pallas import tpu as pltpu
from jax.sharding import PartitionSpec as P

DATES = 300
DP = 304
SHIFT = 4.0
SMOOTHING_WEIGHT = 0.5
RIDGE_WEIGHT = 0.05
CENTRE = 4.0 * SMOOTHING_WEIGHT + RIDGE_WEIGHT - SHIFT
F32 = jnp.float32
BF16 = jnp.bfloat16


def sds(shape, dtype):
    return jax.ShapeDtypeStruct(shape, dtype)


def call(body, outs, *args, specs=None, scratch=(), name=None):
    places = specs or [pltpu.VMEM] * len(args)
    return pl.pallas_call(
        body,
        out_shape=outs,
        in_specs=[pl.BlockSpec(memory_space=place) for place in places],
        scratch_shapes=list(scratch),
        name=name,
    )(*args)


def dot(a, b):
    return jnp.dot(a, b, preferred_element_type=F32)


def split(values):
    high = values.astype(BF16)
    return high, (values - high.astype(F32)).astype(BF16)


def fetch(step, phase, coher, phase_in, coher_in, sems):
    ifgs = pl.ds(step * 16, 16)
    return [
        pltpu.make_async_copy(source.at[ifgs], target.at[ifgs], sems.at[part, step])
        for part, (source, target) in enumerate(((phase, phase_in), (coher, coher_in)))
    ]


def rows_first(phase, coher, phase_t, coher_t, first, last, phase_in, coher_in, wide, sems):
    copies = [fetch(step, phase, coher, phase_in, coher_in, sems) for step in range(4)]
    for pair in copies:
        for copy in pair:
            copy.start()
    for block in range(4):
        for part, (source, target) in enumerate(((phase_in, phase_t), (coher_in, coher_t))):
            copies[block][part].wait()
            for tile in range(8):
                lanes = pl.ds(tile * 128, 128)
                wide[part, tile] = source[pl.ds(block * 16, 16), :, lanes].astype(F32).reshape(128, 128)
                for row in range(8):
                    piece = wide[part, tile, pl.ds(row, 16, stride=8), :].astype(BF16)
                    target[row, pl.ds(block * 16, 16), lanes] = piece
    for part, target in enumerate((phase_t, coher_t)):
        first[pl.ds(part * 64, 64), :] = target[0]
        last[pl.ds(part * 64, 64), :] = target[7]


def shifted_sum(values, lane, last):
    left = jnp.where(lane == 0, 0.0, pltpu.roll(values, 1, 1))
    right = jnp.where(lane == last, 0.0, pltpu.roll(values, last, 1))
    return values + left + right


def fold_lanes(values):
    total = values[:, :128]
    for tile in range(1, 8):
        total += values[:, tile * 128 : tile * 128 + 128]
    return total


def smoothing(flags, owners, phase_t, coher_t, above, below, mask, height, smooth, sums, *rest):
    outs, weights, totals = rest[:8], rest[8], rest[9]
    lane = lax.broadcasted_iota(jnp.int32, (16, 1024), 1)
    edge_flag = {-1: flags[0] > 0, 8: flags[1] > 0}

    def group(block, _):
        ifgs = pl.ds(pl.multiple_of(block * 16, 16), 16)
        cohers = pl.ds(pl.multiple_of(block * 16 + 64, 16), 16)
        masks = mask[ifgs, :]

        def load(row):
            if row < 0 or row > 7:
                edge = above if row < 0 else below
                coher = jnp.where(edge_flag[row], edge[cohers, :].astype(F32), 0.0)
                return coher, coher * edge[ifgs, :].astype(F32)
            coher = coher_t[row, ifgs, :].astype(F32)
            return coher, coher * phase_t[row, ifgs, :].astype(F32)

        before, current = load(-1), load(0)
        top = jnp.zeros((16, 128), F32)
        low = jnp.zeros((16, 128), F32)
        for row in range(8):
            after = load(row + 1)
            denom = shifted_sum(before[0] + current[0] + after[0], lane, 1023)
            numer = shifted_sum(before[1] + current[1] + after[1], lane, 1023)
            terrain = height[pl.ds(row, 1), :]
            top += fold_lanes(numer * terrain)
            low += fold_lanes(denom * (terrain * terrain))
            smooth[row, ifgs, :] = numer / denom
            weight = (masks[:, row : row + 1] * (denom / 9.0)).astype(BF16)
            for tile in range(8):
                weights[tile, ifgs, pl.ds(row * 128, 128)] = weight[:, tile * 128 : tile * 128 + 128]
            before, current = current, after
        totals[ifgs, :] = top
        totals[cohers, :] = low
        return 0

    lax.fori_loop(0, 4, group, 0)
    sums[...] = jnp.broadcast_to(jnp.sum(totals[...].T, axis=0)[None, None, :], sums.shape)
    pick_blocks(weights, owners, outs)


def pick_blocks(source, owners, outs):
    for step, out in enumerate(outs):
        out[...] = source[owners[step]]


def correction(owners, sums, smooth, height, slope_row, *rest):
    outs, blocks = rest[:8], rest[8]
    total = sums[0]
    for index in range(1, sums.shape[0]):
        total += sums[index]
    slope_row[...] = total / pltpu.roll(total, 64, 1)
    column = jnp.broadcast_to(total[0:1, :], (128, 128)).T
    slope = column[:64, :] / column[64:, :]
    for row in range(8):
        for tile in range(8):
            lanes = pl.ds(tile * 128, 128)
            value = smooth[row, :, lanes] - slope * height[pl.ds(row, 1), lanes]
            blocks[tile, :, pl.ds(row * 128, 128)] = value.astype(BF16)
    pick_blocks(blocks, owners, outs)


def column_selector():
    row = lax.broadcasted_iota(jnp.int32, (16, 1024), 0)
    pixel = lax.broadcasted_iota(jnp.int32, (16, 1024), 1)
    wanted = jnp.where(row < 8, row * 128, (row - 8) * 128 + 127)
    return (pixel == wanted).astype(BF16)


def write_edges(field, first, last, columns):
    first[...] = field[:, pl.ds(0, 128)].astype(BF16)
    last[...] = field[:, pl.ds(896, 128)].astype(BF16)
    picked = lax.dot_general(
        column_selector(), field[...].astype(BF16), (((1,), (1,)), ((), ())), preferred_element_type=F32
    )
    columns[...] = picked.astype(BF16)


def right_side(*refs):
    weight_parts, corrected_parts = refs[:8], refs[8:16]
    design_t, field, weights, first, last, columns = refs[16:]
    for part in range(8):
        weights[pl.ds(part * 64, 64), :] = weight_parts[part][...]
    for chunk in range(4):
        lanes = pl.ds(chunk * 256, 256)
        total = jnp.zeros((DP, 256), F32)
        scaled = jnp.concatenate(
            [
                weight_parts[part][:, lanes].astype(F32) * corrected_parts[part][:, lanes].astype(F32)
                for part in range(8)
            ],
            axis=0,
        )
        high, low = split(scaled)
        field[:, lanes] = dot(design_t[...], high) + dot(design_t[...], low)
    write_edges(field, first, last, columns)


def local_image(field, weights, design, design_t, chunk):
    lanes = pl.ds(chunk * 256, 256)
    high, low = split(field[:, lanes])
    scaled = (dot(design[...], high) + dot(design[...], low)) * weights[:, lanes].astype(F32)
    high, low = split(scaled)
    back = dot(design_t[...], high) + dot(design_t[...], low)
    lane = lax.broadcasted_iota(jnp.int32, (DP, 128), 1)
    parts = []
    for row in (2 * chunk, 2 * chunk + 1):
        here = field[:, pl.ds(row * 128, 128)]
        around = jnp.where(lane == 0, 0.0, pltpu.roll(here, 1, 1))
        around += jnp.where(lane == 127, 0.0, pltpu.roll(here, 127, 1))
        if row > 0:
            around += field[:, pl.ds((row - 1) * 128, 128)]
        if row < 7:
            around += field[:, pl.ds((row + 1) * 128, 128)]
        start = (row - 2 * chunk) * 128
        parts.append(back[:, start : start + 128] + CENTRE * here - SMOOTHING_WEIGHT * around)
    return parts


def fold(values):
    return jnp.sum(values.reshape(DP // 8, 8, 128), axis=0)


def apply_local(with_before, with_image, *refs):
    field, weights, design, design_t = refs[:4]
    refs = refs[4:]
    before = None
    if with_before:
        before, refs = refs[0], refs[1:]
    image = None
    if with_image:
        image, refs = refs[0], refs[1:]
    moments = refs[0]
    square = jnp.zeros((8, 128), F32)
    cross = jnp.zeros((8, 128), F32)
    ahead = jnp.zeros((8, 128), F32)
    for chunk in range(4):
        parts = local_image(field, weights, design, design_t, chunk)
        for offset, part in enumerate(parts):
            lanes = pl.ds((2 * chunk + offset) * 128, 128)
            here = field[:, lanes]
            square += fold(here * here)
            if with_before:
                cross += fold(here * before[:, lanes])
            if with_image:
                image[:, lanes] = part
            else:
                ahead += fold(here * part)
    moments[0] = square
    moments[1] = cross
    moments[2] = ahead


def spread_columns(columns, pixels):
    row = lax.broadcasted_iota(jnp.int32, (16, 128), 0)
    lane = lax.broadcasted_iota(jnp.int32, (16, 128), 1)
    wanted = jnp.where(row < 8, row, row - 8) == pixels
    place = (wanted & (lane == jnp.where(row < 8, 0, 127))).astype(BF16)
    return lax.dot_general(columns, place, (((0,), (0,)), ((), ())), preferred_element_type=F32)


def keep(flag, values):
    return jnp.where(flag > 0, values.astype(F32), 0.0)


def add_halo(flags, image, above, below, left, right, field, first, last, columns):
    sides = jnp.concatenate([keep(flags[2], left[8:16, :]), keep(flags[3], right[0:8, :])], axis=0).astype(BF16)
    for row in range(8):
        lanes = pl.ds(row * 128, 128)
        halo = spread_columns(sides, row)
        if row == 0:
            halo += keep(flags[0], above[...])
        if row == 7:
            halo += keep(flags[1], below[...])
        field[:, lanes] = image[:, lanes] - SMOOTHING_WEIGHT * halo
    write_edges(field, first, last, columns)


def all_moments(flags, field, above, left, zero, one, two, out):
    sides = jnp.concatenate([keep(flags[2], left[8:16, :]), jnp.zeros((8, DP), F32)], axis=0).astype(BF16)
    ahead = two[2]
    for row in range(8):
        halo = spread_columns(sides, row)
        if row == 0:
            halo += keep(flags[0], above[...])
        ahead -= (2.0 * SMOOTHING_WEIGHT) * fold(field[:, pl.ds(row * 128, 128)] * halo)
    rows = [zero[0], one[1], one[0], two[1], two[0], ahead]
    sums = [jnp.sum(values, axis=0, keepdims=True) for values in rows]
    out[...] = jnp.concatenate(sums + [jnp.zeros((2, 128), F32)], axis=0)


def combine(parts, zero, one, two, out):
    total = parts[0]
    for index in range(1, parts.shape[0]):
        total += parts[index]
    sums = jnp.sum(total, axis=1, keepdims=True)
    m0, m1, m2, m3, m4, m5 = (jnp.broadcast_to(sums[i : i + 1, :], (1, 128)) for i in range(6))
    t00, t01, t11 = m1 + SHIFT * m0, m2 + SHIFT * m1, m3 + SHIFT * m2
    t12, t22 = m4 + SHIFT * m3, m5 + SHIFT * m4
    l10, l20 = t01 / t00, t11 / t00
    pivot = t11 - l10 * t01
    off = t12 - l20 * t01
    keep = pivot > 1e-6 * t11
    safe = jnp.where(keep, pivot, 1.0)
    l21 = jnp.where(keep, off / safe, 0.0)
    last = t22 - l20 * t11 - l21 * off
    keep_last = keep & (last > 1e-6 * t22)
    y1 = m1 - l10 * m0
    y2 = m2 - l20 * m0 - l21 * y1
    c2 = jnp.where(keep_last, y2 / jnp.where(keep_last, last, 1.0), 0.0)
    c1 = jnp.where(keep, y1 / safe, 0.0) - l21 * c2
    c0 = m0 / t00 - l10 * c1 - l20 * c2
    for row in range(8):
        lanes = pl.ds(row * 128, 128)
        value = c0 * zero[:, lanes] + c1 * one[:, lanes] + c2 * two[:, lanes]
        out[pl.ds(row, DATES, stride=8), :] = value[:DATES, :]


def per_device(phase, coherence, height, gap_mask, date_pairs):
    n_ifg, n_rows = lax.axis_size("ifg"), lax.axis_size("rows")
    n_chip = n_ifg // 2
    me, my_row = lax.axis_index("ifg"), lax.axis_index("rows")
    offsets = ((0, 0), (1, 0), (3, 0), (2, 0), (2, 1), (1, 1), (3, 1), (0, 1))

    def other(index, chips, core):
        return (index // 2 + chips) % n_chip * 2 + (index + core) % 2

    owners = jnp.stack([other(me, *offset) for offset in offsets]).astype(jnp.int32)
    flags = jnp.stack([my_row > 0, my_row < n_rows - 1, me > 0, me < n_ifg - 1]).astype(jnp.int32)

    def permute(values, axis, target):
        return lax.ppermute(values, axis, [(i, target(i)) for i in range(lax.axis_size(axis))])

    def forward(values, axis):
        return permute(values, axis, lambda i: (i + 1) % lax.axis_size(axis))

    def backward(values, axis):
        return permute(values, axis, lambda i: (i - 1) % lax.axis_size(axis))

    stacked = sds((8, 64, 1024), BF16)
    edge = sds((128, 1024), BF16)
    phase_t, coher_t, first, last = call(
        rows_first,
        (stacked, stacked, edge, edge),
        phase,
        coherence,
        specs=[pltpu.HBM] * 2,
        scratch=(
            pltpu.VMEM((64, 8, 1024), BF16),
            pltpu.VMEM((64, 8, 1024), BF16),
            pltpu.VMEM((2, 8, 128, 128), F32),
            pltpu.SemaphoreType.DMA((2, 4)),
        ),
        name="rows_first",
    )
    above, below = forward(last, "rows"), backward(first, "rows")
    block = sds((64, 1024), BF16)
    smooth, sums, *weight_parts = call(
        smoothing,
        [sds((8, 64, 1024), F32), sds((n_rows, 8, 128), F32)] + [block] * 8,
        flags,
        owners,
        phase_t,
        coher_t,
        above,
        below,
        gap_mask.astype(F32),
        height,
        specs=[pltpu.SMEM] * 2 + [pltpu.VMEM] * 6,
        scratch=(pltpu.VMEM((8, 64, 1024), BF16), pltpu.VMEM((128, 128), F32)),
        name="smoothing",
    )
    sums = lax.all_to_all(sums, "rows", 0, 0, tiled=True)

    def exchange(parts):
        return [parts[0]] + [
            permute(part, "ifg", lambda i: other(i, *offset))
            for part, offset in zip(parts[1:], offsets[1:])
        ]

    weight_parts = exchange(weight_parts)
    slope_row, *corrected_parts = call(
        correction,
        [sds((8, 128), F32)] + [block] * 8,
        owners,
        sums,
        smooth,
        height,
        specs=[pltpu.SMEM] + [pltpu.VMEM] * 3,
        scratch=(pltpu.VMEM((8, 64, 1024), BF16),),
        name="correction",
    )
    corrected_parts = exchange(corrected_parts)
    sources = jnp.stack([other(me, -chips, core) for chips, core in offsets])
    pairs = date_pairs.reshape(n_ifg, -1, 2)[sources].reshape(-1, 2)
    dates = jnp.arange(DP, dtype=jnp.int32)
    design = ((dates[None] == pairs[:, 1:2]).astype(F32) - (dates[None] == pairs[:, 0:1]).astype(F32)).astype(BF16)
    design_t = design.T

    field = sds((DP, 1024), F32)
    edges = (sds((DP, 128), BF16), sds((DP, 128), BF16), sds((16, DP), BF16))
    moments = sds((3, 8, 128), F32)
    k0, weights, first, last, columns = call(
        right_side,
        (field, sds((512, 1024), BF16)) + edges,
        *weight_parts,
        *corrected_parts,
        design_t,
        name="right_side",
    )

    def halos(first, last, columns):
        return (
            forward(last, "rows"),
            backward(first, "rows"),
            forward(columns, "ifg"),
            backward(columns, "ifg"),
        )

    def local(with_before, with_image, name, *args):
        outs = ((field,) if with_image else ()) + (moments,)
        body = lambda *refs: apply_local(with_before, with_image, *refs)
        return call(body, outs, *args, name=name)

    def joined(image, around, name):
        specs = [pltpu.SMEM] + [pltpu.VMEM] * 5
        return call(add_halo, (field,) + edges, flags, image, *around, specs=specs, name=name)

    around = halos(first, last, columns)
    image, mom0 = local(False, True, "apply0", k0, weights, design, design_t)
    k1, first, last, columns = joined(image, around, "add_halo1")
    around = halos(first, last, columns)
    image, mom1 = local(True, True, "apply1", k1, weights, design, design_t, k0)
    k2, first, last, columns = joined(image, around, "add_halo2")
    above, left = forward(last, "rows"), forward(columns, "ifg")
    (mom2,) = local(True, False, "apply2", k2, weights, design, design_t, k1)
    part = call(
        all_moments,
        sds((8, 128), F32),
        flags,
        k2,
        above,
        left,
        mom0,
        mom1,
        mom2,
        specs=[pltpu.SMEM] + [pltpu.VMEM] * 6,
        name="all_moments",
    )
    for target in (lambda i: i ^ 1, lambda i: i ^ 2, lambda i: i ^ 4):
        part = part + permute(part, "ifg", target)
    part = jnp.broadcast_to(part[None], (n_rows, 8, 128))
    parts = lax.all_to_all(part, "rows", 0, 0, tiled=True)
    displacement = call(combine, sds((DATES * 8, 128), F32), parts, k0, k1, k2, name="combine")
    return displacement.reshape(DATES, 8, 128), slope_row[0, :64]


def solution(mesh):
    placed = (
        P("ifg", "rows", None),
        P("ifg", "rows", None),
        P("rows", None),
        P("ifg", "rows"),
        P(),
    )
    return jax.shard_map(
        per_device,
        mesh=mesh,
        in_specs=placed,
        out_specs=(P(None, "rows", "ifg"), P("ifg")),
        check_vma=False,
    )
```

```python
import jax
import jax.numpy as jnp
from jax import lax
from jax.experimental import pallas as pl
from jax.experimental.pallas import tpu as pltpu
from jax.sharding import PartitionSpec as P

DATES = 300
DP = 304
SHIFT = 4.0
SMOOTHING_WEIGHT = 0.5
RIDGE_WEIGHT = 0.05
CENTRE = 4.0 * SMOOTHING_WEIGHT + RIDGE_WEIGHT - SHIFT
F32 = jnp.float32
BF16 = jnp.bfloat16


def sds(shape, dtype):
    return jax.ShapeDtypeStruct(shape, dtype)


def in_hbm(shape, dtype):
    return pltpu.HBM(shape, dtype)


def call(body, outs, *args, specs=None, out_specs=None, scratch=(), name=None):
    flat = outs if isinstance(outs, (list, tuple)) else [outs]
    places = specs or [pltpu.VMEM] * len(args)
    out_places = [pl.BlockSpec(memory_space=place) for place in out_specs or [pltpu.VMEM] * len(flat)]
    return pl.pallas_call(
        body,
        out_shape=outs,
        in_specs=[pl.BlockSpec(memory_space=place) for place in places],
        out_specs=out_places if isinstance(outs, (list, tuple)) else out_places[0],
        scratch_shapes=list(scratch),
        compiler_params=pltpu.CompilerParams(vmem_limit_bytes=16 * 1024 * 1024),
        name=name,
    )(*args)


def dot(a, b):
    return jnp.dot(a, b, preferred_element_type=F32)


def split(values):
    high = values.astype(BF16)
    return high, (values - high.astype(F32)).astype(BF16)


def rows_first(phase, coher, phase_t, coher_t, first, last, wide):
    def group(block, _):
        ifgs = pl.ds(pl.multiple_of(block * 16, 16), 16)
        for part, (source, target) in enumerate(((phase, phase_t), (coher, coher_t))):
            for tile in range(8):
                lanes = pl.ds(tile * 128, 128)
                wide[part, tile] = source[ifgs, :, lanes].astype(F32).reshape(128, 128)
                for row in range(8):
                    target[row, ifgs, lanes] = wide[part, tile, pl.ds(row, 16, stride=8), :].astype(BF16)
        return 0

    lax.fori_loop(0, 4, group, 0)
    for part, target in enumerate((phase_t, coher_t)):
        first[pl.ds(part * 64, 64), :] = target[0]
        last[pl.ds(part * 64, 64), :] = target[7]


def shifted_sum(values, lane, last):
    left = jnp.where(lane == 0, 0.0, pltpu.roll(values, 1, 1))
    right = jnp.where(lane == last, 0.0, pltpu.roll(values, last, 1))
    return values + left + right


def fold_lanes(values):
    total = values[:, :128]
    for tile in range(1, 8):
        total += values[:, tile * 128 : tile * 128 + 128]
    return total


def smoothing(flags, owners, phase_t, coher_t, above, below, mask, height, smooth_out, sums, *rest):
    outs, weights, totals, smooth, sems = rest[:8], rest[8], rest[9], rest[10], rest[11]
    lane = lax.broadcasted_iota(jnp.int32, (16, 1024), 1)
    edge_flag = {-1: flags[0] > 0, 8: flags[1] > 0}

    def copies(block):
        ifgs = pl.ds(pl.multiple_of(block * 16, 16), 16)
        return [
            pltpu.make_async_copy(weights.at[owners[step], ifgs], out.at[ifgs], sems.at[block, step])
            for step, out in enumerate(outs)
        ] + [pltpu.make_async_copy(smooth.at[:, ifgs], smooth_out.at[:, ifgs], sems.at[block, 8])]

    def group(block, _):
        ifgs = pl.ds(pl.multiple_of(block * 16, 16), 16)
        cohers = pl.ds(pl.multiple_of(block * 16 + 64, 16), 16)
        masks = mask[ifgs, :]

        def load(row):
            if row < 0 or row > 7:
                edge = above if row < 0 else below
                coher = jnp.where(edge_flag[row], edge[cohers, :].astype(F32), 0.0)
                return coher, coher * edge[ifgs, :].astype(F32)
            coher = coher_t[row, ifgs, :].astype(F32)
            return coher, coher * phase_t[row, ifgs, :].astype(F32)

        before, current = load(-1), load(0)
        top = jnp.zeros((16, 128), F32)
        low = jnp.zeros((16, 128), F32)
        for row in range(8):
            after = load(row + 1)
            denom = shifted_sum(before[0] + current[0] + after[0], lane, 1023)
            numer = shifted_sum(before[1] + current[1] + after[1], lane, 1023)
            terrain = height[pl.ds(row, 1), :]
            top += fold_lanes(numer * terrain)
            low += fold_lanes(denom * (terrain * terrain))
            smooth[row, ifgs, :] = numer / denom
            weight = (masks[:, row : row + 1] * (denom / 9.0)).astype(BF16)
            for tile in range(8):
                weights[tile, ifgs, pl.ds(row * 128, 128)] = weight[:, tile * 128 : tile * 128 + 128]
            before, current = current, after
        totals[ifgs, :] = top
        totals[cohers, :] = low
        for copy in copies(block):
            copy.start()
        return 0

    lax.fori_loop(0, 4, group, 0)
    sums[...] = jnp.broadcast_to(jnp.sum(totals[...].T, axis=0, keepdims=True), sums.shape)
    for block in range(4):
        for copy in copies(block):
            copy.wait()


def pick_blocks(source, owners, outs):
    for step, out in enumerate(outs):
        out[...] = source[owners[step]]


def correction(owners, sums, smooth, height, slope_row, *rest):
    outs, blocks = rest[:8], rest[8]
    total = sums[...]
    slope_row[...] = total / pltpu.roll(total, 64, 1)
    column = jnp.broadcast_to(total[0:1, :], (128, 128)).T
    slope = column[:64, :] / column[64:, :]

    def one_tile(tile, _):
        lanes = pl.ds(pl.multiple_of(tile * 128, 128), 128)
        for row in range(8):
            value = smooth[row, :, lanes] - slope * height[pl.ds(row, 1), lanes]
            blocks[tile, :, pl.ds(row * 128, 128)] = value.astype(BF16)
        return 0

    lax.fori_loop(0, 8, one_tile, 0)
    pick_blocks(blocks, owners, outs)


def column_selector():
    row = lax.broadcasted_iota(jnp.int32, (16, 1024), 0)
    pixel = lax.broadcasted_iota(jnp.int32, (16, 1024), 1)
    wanted = jnp.where(row < 8, row * 128, (row - 8) * 128 + 127)
    return (pixel == wanted).astype(BF16)


def write_edges(field, first, last, columns):
    first[...] = field[:, pl.ds(0, 128)].astype(BF16)
    last[...] = field[:, pl.ds(896, 128)].astype(BF16)
    picked = lax.dot_general(
        column_selector(), field[...].astype(BF16), (((1,), (1,)), ((), ())), preferred_element_type=F32
    )
    columns[...] = picked.astype(BF16)


def right_side(*refs):
    weight_parts, corrected_parts = refs[:8], refs[8:16]
    design_t, field, weights, first, last, columns = refs[16:]
    for part in range(8):
        weights[pl.ds(part * 64, 64), :] = weight_parts[part][...]

    def one_chunk(chunk, _):
        lanes = pl.ds(pl.multiple_of(chunk * 256, 256), 256)
        scaled = jnp.concatenate(
            [
                weight_parts[part][:, lanes].astype(F32) * corrected_parts[part][:, lanes].astype(F32)
                for part in range(8)
            ],
            axis=0,
        )
        high, low = split(scaled)
        field[:, lanes] = dot(design_t[...], high) + dot(design_t[...], low)
        return 0

    lax.fori_loop(0, 4, one_chunk, 0)
    write_edges(field, first, last, columns)


def row_lanes(row):
    return pl.ds(pl.multiple_of(row * 128, 128), 128)


def local_image(field, weights, design, design_t, chunk):
    lanes = pl.ds(pl.multiple_of(chunk * 256, 256), 256)
    high, low = split(field[:, lanes])
    scaled = (dot(design[...], high) + dot(design[...], low)) * weights[:, lanes].astype(F32)
    high, low = split(scaled)
    back = dot(design_t[...], high) + dot(design_t[...], low)
    lane = lax.broadcasted_iota(jnp.int32, (DP, 128), 1)
    parts = []
    for offset in range(2):
        row = 2 * chunk + offset
        here = field[:, row_lanes(row)]
        around = jnp.where(lane == 0, 0.0, pltpu.roll(here, 1, 1))
        around += jnp.where(lane == 127, 0.0, pltpu.roll(here, 127, 1))
        around += jnp.where(row > 0, field[:, row_lanes(jnp.maximum(row - 1, 0))], 0.0)
        around += jnp.where(row < 7, field[:, row_lanes(jnp.minimum(row + 1, 7))], 0.0)
        part = back[:, offset * 128 : offset * 128 + 128] + CENTRE * here - SMOOTHING_WEIGHT * around
        parts.append((row, part))
    return parts


def fold(values):
    return jnp.sum(values.reshape(DP // 8, 8, 128), axis=0)


def apply_local(with_before, with_image, *refs):
    field, weights, design, design_t = refs[:4]
    refs = refs[4:]
    before = None
    if with_before:
        before, refs = refs[0], refs[1:]
    image = None
    if with_image:
        image, refs = refs[0], refs[1:]
    moments = refs[0]

    def one_chunk(chunk, totals):
        square, cross, ahead = totals
        for row, part in local_image(field, weights, design, design_t, chunk):
            here = field[:, row_lanes(row)]
            square += fold(here * here)
            if with_before:
                cross += fold(here * before[:, row_lanes(row)])
            if with_image:
                image[:, row_lanes(row)] = part
            else:
                ahead += fold(here * part)
        return square, cross, ahead

    zero = jnp.zeros((8, 128), F32)
    totals = lax.fori_loop(0, 4, one_chunk, (zero, zero, zero))
    for index in range(3):
        moments[index] = totals[index]


def spread_columns(columns, pixels):
    row = lax.broadcasted_iota(jnp.int32, (16, 128), 0)
    lane = lax.broadcasted_iota(jnp.int32, (16, 128), 1)
    wanted = jnp.where(row < 8, row, row - 8) == pixels
    place = (wanted & (lane == jnp.where(row < 8, 0, 127))).astype(BF16)
    return lax.dot_general(columns, place, (((0,), (0,)), ((), ())), preferred_element_type=F32)


def keep(flag, values):
    return jnp.where(flag > 0, values.astype(F32), 0.0)


def add_halo(flags, image, above, below, left, right, field, first, last, columns):
    sides = jnp.concatenate([keep(flags[2], left[8:16, :]), keep(flags[3], right[0:8, :])], axis=0).astype(BF16)
    for row in range(8):
        lanes = pl.ds(row * 128, 128)
        halo = spread_columns(sides, row)
        if row == 0:
            halo += keep(flags[0], above[...])
        if row == 7:
            halo += keep(flags[1], below[...])
        field[:, lanes] = image[:, lanes] - SMOOTHING_WEIGHT * halo
    write_edges(field, first, last, columns)


def all_moments(flags, field, above, left, zero, one, two, out):
    sides = jnp.concatenate([keep(flags[2], left[8:16, :]), jnp.zeros((8, DP), F32)], axis=0).astype(BF16)
    ahead = two[2]
    for row in range(8):
        halo = spread_columns(sides, row)
        if row == 0:
            halo += keep(flags[0], above[...])
        ahead -= (2.0 * SMOOTHING_WEIGHT) * fold(field[:, pl.ds(row * 128, 128)] * halo)
    rows = [zero[0], one[1], one[0], two[1], two[0], ahead]
    sums = [jnp.sum(values, axis=0, keepdims=True) for values in rows]
    out[...] = jnp.concatenate(sums + [jnp.zeros((2, 128), F32)], axis=0)


def combine(total, zero, one, two, out):
    sums = jnp.sum(total[...], axis=1, keepdims=True)
    m0, m1, m2, m3, m4, m5 = (jnp.broadcast_to(sums[i : i + 1, :], (1, 128)) for i in range(6))
    t00, t01, t11 = m1 + SHIFT * m0, m2 + SHIFT * m1, m3 + SHIFT * m2
    t12, t22 = m4 + SHIFT * m3, m5 + SHIFT * m4
    l10, l20 = t01 / t00, t11 / t00
    pivot = t11 - l10 * t01
    off = t12 - l20 * t01
    keep = pivot > 1e-6 * t11
    safe = jnp.where(keep, pivot, 1.0)
    l21 = jnp.where(keep, off / safe, 0.0)
    last = t22 - l20 * t11 - l21 * off
    keep_last = keep & (last > 1e-6 * t22)
    y1 = m1 - l10 * m0
    y2 = m2 - l20 * m0 - l21 * y1
    c2 = jnp.where(keep_last, y2 / jnp.where(keep_last, last, 1.0), 0.0)
    c1 = jnp.where(keep, y1 / safe, 0.0) - l21 * c2
    c0 = m0 / t00 - l10 * c1 - l20 * c2
    for row in range(8):
        lanes = pl.ds(row * 128, 128)
        value = c0 * zero[:, lanes] + c1 * one[:, lanes] + c2 * two[:, lanes]
        out[pl.ds(row, DATES, stride=8), :] = value[:DATES, :]


def per_device(phase, coherence, height, gap_mask, date_pairs):
    n_ifg, n_rows = lax.axis_size("ifg"), lax.axis_size("rows")
    n_chip = n_ifg // 2
    me, my_row = lax.axis_index("ifg"), lax.axis_index("rows")
    offsets = ((0, 0), (1, 0), (3, 0), (2, 0), (2, 1), (1, 1), (3, 1), (0, 1))

    def other(index, chips, core):
        return (((index >> 1) + chips) & (n_chip - 1)) * 2 + ((index & 1) ^ core)

    owners = jnp.stack([other(me, *offset) for offset in offsets]).astype(jnp.int32)
    flags = jnp.stack([my_row > 0, my_row < n_rows - 1, me > 0, me < n_ifg - 1]).astype(jnp.int32)

    def permute(values, axis, target):
        return lax.ppermute(values, axis, [(i, target(i)) for i in range(lax.axis_size(axis))])

    def forward(values, axis):
        return permute(values, axis, lambda i: (i + 1) % lax.axis_size(axis))

    def backward(values, axis):
        return permute(values, axis, lambda i: (i - 1) % lax.axis_size(axis))

    def ring_of_four(values, axis, target):
        moved = [permute(values, axis, lambda i: target(i, k)) for k in (1, 2, 3)]
        return (values + moved[1]) + (moved[0] + moved[2])

    def sum_rows(values):
        values = ring_of_four(values, "rows", lambda i, k: (i + 8 * k) % n_rows)
        values = values + permute(values, "rows", lambda i: i ^ 1)
        return ring_of_four(values, "rows", lambda i, k: i // 8 * 8 + (i + 2 * k) % 8)

    stacked = sds((8, 64, 1024), BF16)
    edge = sds((128, 1024), BF16)
    phase_t, coher_t, first, last = call(
        rows_first,
        (stacked, stacked, edge, edge),
        phase,
        coherence,
        scratch=(pltpu.VMEM((2, 8, 128, 128), F32),),
        name="rows_first",
    )
    above, below = forward(last, "rows"), backward(first, "rows")
    block = sds((64, 1024), BF16)
    smooth, sums, *weight_parts = call(
        smoothing,
        [in_hbm((8, 64, 1024), F32), sds((8, 128), F32)] + [in_hbm((64, 1024), BF16)] * 8,
        flags,
        owners,
        phase_t,
        coher_t,
        above,
        below,
        gap_mask.astype(F32),
        height,
        specs=[pltpu.SMEM] * 2 + [pltpu.VMEM] * 6,
        out_specs=[pltpu.HBM, pltpu.VMEM] + [pltpu.HBM] * 8,
        scratch=(
            pltpu.VMEM((8, 64, 1024), BF16),
            pltpu.VMEM((128, 128), F32),
            pltpu.VMEM((8, 64, 1024), F32),
            pltpu.SemaphoreType.DMA((4, 9)),
        ),
        name="smoothing",
    )
    sums = sum_rows(sums)

    def exchange(parts):
        return [parts[0]] + [
            permute(part, "ifg", lambda i: other(i, *offset))
            for part, offset in zip(parts[1:], offsets[1:])
        ]

    weight_parts = exchange(weight_parts)
    slope_row, *corrected_parts = call(
        correction,
        [sds((8, 128), F32)] + [block] * 8,
        owners,
        sums,
        smooth,
        height,
        specs=[pltpu.SMEM] + [pltpu.VMEM] * 3,
        scratch=(pltpu.VMEM((8, 64, 1024), BF16),),
        name="correction",
    )
    corrected_parts = exchange(corrected_parts)
    sources = jnp.stack([other(me, n_chip - chips, core) for chips, core in offsets])
    pairs = date_pairs.reshape(n_ifg, -1, 2)[sources].reshape(-1, 2)
    dates = jnp.arange(DP, dtype=jnp.int32)
    design = ((dates[None] == pairs[:, 1:2]).astype(F32) - (dates[None] == pairs[:, 0:1]).astype(F32)).astype(BF16)
    design_t = design.T

    field = sds((DP, 1024), F32)
    edges = (sds((DP, 128), BF16), sds((DP, 128), BF16), sds((16, DP), BF16))
    moments = sds((3, 8, 128), F32)
    k0, weights, first, last, columns = call(
        right_side,
        (field, sds((512, 1024), BF16)) + edges,
        *weight_parts,
        *corrected_parts,
        design_t,
        name="right_side",
    )

    def halos(first, last, columns):
        return (
            forward(last, "rows"),
            backward(first, "rows"),
            forward(columns, "ifg"),
            backward(columns, "ifg"),
        )

    def local(with_before, with_image, name, *args):
        outs = ((field,) if with_image else ()) + (moments,)
        body = lambda *refs: apply_local(with_before, with_image, *refs)
        return call(body, outs, *args, name=name)

    def joined(image, around, name):
        specs = [pltpu.SMEM] + [pltpu.VMEM] * 5
        return call(add_halo, (field,) + edges, flags, image, *around, specs=specs, name=name)

    around = halos(first, last, columns)
    image, mom0 = local(False, True, "apply0", k0, weights, design, design_t)
    k1, first, last, columns = joined(image, around, "add_halo1")
    around = halos(first, last, columns)
    image, mom1 = local(True, True, "apply1", k1, weights, design, design_t, k0)
    k2, first, last, columns = joined(image, around, "add_halo2")
    above, left = forward(last, "rows"), forward(columns, "ifg")
    (mom2,) = local(True, False, "apply2", k2, weights, design, design_t, k1)
    part = call(
        all_moments,
        sds((8, 128), F32),
        flags,
        k2,
        above,
        left,
        mom0,
        mom1,
        mom2,
        specs=[pltpu.SMEM] + [pltpu.VMEM] * 6,
        name="all_moments",
    )
    part = part + permute(part, "ifg", lambda i: i ^ 1)
    part = sum_rows(ring_of_four(part, "ifg", lambda i, k: (i + 2 * k) % n_ifg))
    displacement = call(combine, sds((DATES * 8, 128), F32), part, k0, k1, k2, name="combine")
    return displacement.reshape(DATES, 8, 128), slope_row[0, :64]


def solution(mesh):
    placed = (
        P("ifg", "rows", None),
        P("ifg", "rows", None),
        P("rows", None),
        P("ifg", "rows"),
        P(),
    )
    return jax.shard_map(
        per_device,
        mesh=mesh,
        in_specs=placed,
        out_specs=(P(None, "rows", "ifg"), P("ifg")),
        check_vma=False,
    )
```

```python
import jax
import jax.numpy as jnp
from jax import lax
from jax.experimental import pallas as pl
from jax.experimental.pallas import tpu as pltpu
from jax.sharding import PartitionSpec as P

DATES = 300
DP = 304
SHIFT = 4.0
SMOOTHING_WEIGHT = 0.5
RIDGE_WEIGHT = 0.05
CENTRE = 4.0 * SMOOTHING_WEIGHT + RIDGE_WEIGHT - SHIFT
F32 = jnp.float32
BF16 = jnp.bfloat16


def sds(shape, dtype):
    return jax.ShapeDtypeStruct(shape, dtype)


def in_hbm(shape, dtype):
    return pltpu.HBM(shape, dtype)


def call(body, outs, *args, specs=None, out_specs=None, scratch=(), aliases=None, name=None):
    flat = outs if isinstance(outs, (list, tuple)) else [outs]
    places = specs or [pltpu.VMEM] * len(args)
    out_places = [pl.BlockSpec(memory_space=place) for place in out_specs or [pltpu.VMEM] * len(flat)]
    return pl.pallas_call(
        body,
        out_shape=outs,
        in_specs=[pl.BlockSpec(memory_space=place) for place in places],
        out_specs=out_places if isinstance(outs, (list, tuple)) else out_places[0],
        scratch_shapes=list(scratch),
        input_output_aliases=aliases or {},
        compiler_params=pltpu.CompilerParams(vmem_limit_bytes=16 * 1024 * 1024),
        name=name,
    )(*args)


def dot(a, b):
    return jnp.dot(a, b, preferred_element_type=F32)


def split(values):
    high = values.astype(BF16)
    return high, (values - high.astype(F32)).astype(BF16)


def rows_first(phase, coher, phase_t, coher_t, first, last, wide):
    def group(block, _):
        ifgs = pl.ds(pl.multiple_of(block * 16, 16), 16)
        for part, (source, target) in enumerate(((phase, phase_t), (coher, coher_t))):
            for tile in range(8):
                lanes = pl.ds(tile * 128, 128)
                wide[part, tile] = source[ifgs, :, lanes].astype(F32).reshape(128, 128)
                for row in range(8):
                    target[row, ifgs, lanes] = wide[part, tile, pl.ds(row, 16, stride=8), :].astype(BF16)
        return 0

    lax.fori_loop(0, 4, group, 0)
    for part, target in enumerate((phase_t, coher_t)):
        first[pl.ds(part * 64, 64), :] = target[0]
        last[pl.ds(part * 64, 64), :] = target[7]


def shifted_sum(values, lane, last):
    left = jnp.where(lane == 0, 0.0, pltpu.roll(values, 1, 1))
    right = jnp.where(lane == last, 0.0, pltpu.roll(values, last, 1))
    return values + left + right


def fold_lanes(values):
    total = values[:, :128]
    for tile in range(1, 8):
        total += values[:, tile * 128 : tile * 128 + 128]
    return total


OFFSETS = ((0, 0), (1, 0), (3, 0), (2, 0), (2, 1), (1, 1), (3, 1), (0, 1))


def other(index, chips, core):
    return (((index >> 1) + chips) & 3) * 2 + ((index & 1) ^ core)


def owner(step):
    return other(lax.axis_index("ifg"), *OFFSETS[step])


def smooth_row(rows, lane, mask, terrain):
    denom = shifted_sum(rows[0][0] + rows[1][0] + rows[2][0], lane, 1023)
    numer = shifted_sum(rows[0][1] + rows[1][1] + rows[2][1], lane, 1023)
    top = fold_lanes(numer * terrain)
    low = fold_lanes(denom * (terrain * terrain))
    return numer / denom, (mask * (denom / 9.0)).astype(BF16), top, low


def load_row(phase_t, coher_t, row, ifgs):
    coher = coher_t[row, ifgs, :].astype(F32)
    return coher, coher * phase_t[row, ifgs, :].astype(F32)


def block_of(block):
    return pl.ds(pl.multiple_of(block * 16, 16), 16), pl.ds(pl.multiple_of(block * 16 + 64, 16), 16)


def inner_rows(phase_t, coher_t, mask, height, smooth_out, totals, *rest):
    outs, weights, smooth, sems = rest[:8], rest[8], rest[9], rest[10]
    lane = lax.broadcasted_iota(jnp.int32, (16, 1024), 1)

    def copies(block):
        ifgs, _ = block_of(block)
        return [
            pltpu.make_async_copy(
                weights.at[owner(step), ifgs], out.at[ifgs, pl.ds(128, 768)], sems.at[block, step]
            )
            for step, out in enumerate(outs)
        ] + [pltpu.make_async_copy(smooth.at[:, ifgs], smooth_out.at[pl.ds(1, 6), ifgs], sems.at[block, 8])]

    def group(block, _):
        ifgs, lows = block_of(block)
        masks = mask[ifgs, :]
        rows = [load_row(phase_t, coher_t, row, ifgs) for row in (0, 1)]
        top = jnp.zeros((16, 128), F32)
        low = jnp.zeros((16, 128), F32)
        for row in range(1, 7):
            rows.append(load_row(phase_t, coher_t, row + 1, ifgs))
            value, weight, more_top, more_low = smooth_row(
                rows, lane, masks[:, row : row + 1], height[pl.ds(row, 1), :]
            )
            rows = rows[1:]
            top += more_top
            low += more_low
            smooth[row - 1, ifgs, :] = value
            for tile in range(8):
                weights[tile, ifgs, pl.ds((row - 1) * 128, 128)] = weight[:, tile * 128 : tile * 128 + 128]
        totals[ifgs, :] = top
        totals[lows, :] = low
        for copy in copies(block):
            copy.start()
        return 0

    lax.fori_loop(0, 4, group, 0)
    for block in range(4):
        for copy in copies(block):
            copy.wait()


def border_rows(phase_t, coher_t, above, below, mask, height, totals, *rest):
    smooth_out, sums, outs = rest[9], rest[10], rest[11:19]
    weights, smooth, added, sems = rest[19:]
    lane = lax.broadcasted_iota(jnp.int32, (16, 1024), 1)
    my_row = lax.axis_index("rows")
    valid = (my_row > 0, my_row < lax.axis_size("rows") - 1)

    def group(block, _):
        ifgs, lows = block_of(block)
        masks = mask[ifgs, :]
        top = totals[ifgs, :]
        low = totals[lows, :]
        for side, (edge, row) in enumerate(((above, 0), (below, 7))):
            coher = jnp.where(valid[side], edge[lows, :].astype(F32), 0.0)
            rows = [(coher, coher * edge[ifgs, :].astype(F32))]
            rows += [load_row(phase_t, coher_t, near, ifgs) for near in (row, 1 if row == 0 else 6)]
            value, weight, more_top, more_low = smooth_row(
                rows, lane, masks[:, row : row + 1], height[pl.ds(row, 1), :]
            )
            top += more_top
            low += more_low
            smooth[side, ifgs, :] = value
            for tile in range(8):
                weights[side, tile, ifgs, :] = weight[:, tile * 128 : tile * 128 + 128]
        added[ifgs, :] = top
        added[lows, :] = low
        return 0

    lax.fori_loop(0, 4, group, 0)
    copies = []
    for side, row in ((0, 0), (1, 7)):
        copies.append(pltpu.make_async_copy(smooth.at[side], smooth_out.at[row], sems.at[side, 8]))
        for step, out in enumerate(outs):
            lanes = pl.ds(row * 128, 128)
            copies.append(
                pltpu.make_async_copy(weights.at[side, owner(step)], out.at[:, lanes], sems.at[side, step])
            )
    for copy in copies:
        copy.start()
    sums[...] = jnp.broadcast_to(jnp.sum(added[...].T, axis=0)[None, None, :], sums.shape)
    for copy in copies:
        copy.wait()


def correction(sums, smooth, height, slope_row, *rest):
    outs, blocks = rest[:8], rest[8]
    total = sums[0]
    for index in range(1, sums.shape[0]):
        total += sums[index]
    slope_row[...] = total / pltpu.roll(total, 64, 1)
    column = jnp.broadcast_to(total[0:1, :], (128, 128)).T
    slope = column[:64, :] / column[64:, :]

    def one_tile(tile, _):
        lanes = pl.ds(pl.multiple_of(tile * 128, 128), 128)
        for row in range(8):
            value = smooth[row, :, lanes] - slope * height[pl.ds(row, 1), lanes]
            blocks[tile, :, pl.ds(row * 128, 128)] = value.astype(BF16)
        return 0

    lax.fori_loop(0, 8, one_tile, 0)
    for step, out in enumerate(outs):
        out[...] = blocks[owner(step)]


def column_selector():
    row = lax.broadcasted_iota(jnp.int32, (16, 1024), 0)
    pixel = lax.broadcasted_iota(jnp.int32, (16, 1024), 1)
    wanted = jnp.where(row < 8, row * 128, (row - 8) * 128 + 127)
    return (pixel == wanted).astype(BF16)


def write_edges(field, first, last, columns):
    first[...] = field[:, pl.ds(0, 128)].astype(BF16)
    last[...] = field[:, pl.ds(896, 128)].astype(BF16)
    picked = lax.dot_general(
        column_selector(), field[...].astype(BF16), (((1,), (1,)), ((), ())), preferred_element_type=F32
    )
    columns[...] = picked.astype(BF16)


def right_side(*refs):
    weight_parts, corrected_parts = refs[:8], refs[8:16]
    design_t, field, weights, first, last, columns = refs[16:]
    for part in range(8):
        weights[pl.ds(part * 64, 64), :] = weight_parts[part][...]

    def one_chunk(chunk, _):
        lanes = pl.ds(pl.multiple_of(chunk * 256, 256), 256)
        scaled = jnp.concatenate(
            [
                weight_parts[part][:, lanes].astype(F32) * corrected_parts[part][:, lanes].astype(F32)
                for part in range(8)
            ],
            axis=0,
        )
        high, low = split(scaled)
        field[:, lanes] = dot(design_t[...], high) + dot(design_t[...], low)
        return 0

    lax.fori_loop(0, 4, one_chunk, 0)
    write_edges(field, first, last, columns)


def row_lanes(row):
    return pl.ds(pl.multiple_of(row * 128, 128), 128)


def local_image(field, weights, design, design_t, chunk):
    lanes = pl.ds(pl.multiple_of(chunk * 256, 256), 256)
    high, low = split(field[:, lanes])
    scaled = (dot(design[...], high) + dot(design[...], low)) * weights[:, lanes].astype(F32)
    high, low = split(scaled)
    back = dot(design_t[...], high) + dot(design_t[...], low)
    lane = lax.broadcasted_iota(jnp.int32, (DP, 128), 1)
    parts = []
    for offset in range(2):
        row = 2 * chunk + offset
        here = field[:, row_lanes(row)]
        around = jnp.where(lane == 0, 0.0, pltpu.roll(here, 1, 1))
        around += jnp.where(lane == 127, 0.0, pltpu.roll(here, 127, 1))
        around += jnp.where(row > 0, field[:, row_lanes(jnp.maximum(row - 1, 0))], 0.0)
        around += jnp.where(row < 7, field[:, row_lanes(jnp.minimum(row + 1, 7))], 0.0)
        part = back[:, offset * 128 : offset * 128 + 128] + CENTRE * here - SMOOTHING_WEIGHT * around
        parts.append((row, part))
    return parts


def fold(values):
    return jnp.sum(values.reshape(DP // 8, 8, 128), axis=0)


def apply_local(with_before, with_image, *refs):
    field, weights, design, design_t = refs[:4]
    refs = refs[4:]
    before = None
    if with_before:
        before, refs = refs[0], refs[1:]
    image = None
    if with_image:
        image, refs = refs[0], refs[1:]
    moments = refs[0]

    def one_chunk(chunk, totals):
        square, cross, ahead = totals
        for row, part in local_image(field, weights, design, design_t, chunk):
            here = field[:, row_lanes(row)]
            square += fold(here * here)
            if with_before:
                cross += fold(here * before[:, row_lanes(row)])
            if with_image:
                image[:, row_lanes(row)] = part
            else:
                ahead += fold(here * part)
        return square, cross, ahead

    zero = jnp.zeros((8, 128), F32)
    totals = lax.fori_loop(0, 4, one_chunk, (zero, zero, zero))
    for index in range(3):
        moments[index] = totals[index]


def spread_columns(columns, pixels):
    row = lax.broadcasted_iota(jnp.int32, (16, 128), 0)
    lane = lax.broadcasted_iota(jnp.int32, (16, 128), 1)
    wanted = jnp.where(row < 8, row, row - 8) == pixels
    place = (wanted & (lane == jnp.where(row < 8, 0, 127))).astype(BF16)
    return lax.dot_general(columns, place, (((0,), (0,)), ((), ())), preferred_element_type=F32)


def keep(flag, values):
    return jnp.where(flag, values.astype(F32), 0.0)


def inside():
    row, col = lax.axis_index("rows"), lax.axis_index("ifg")
    return row > 0, row < lax.axis_size("rows") - 1, col > 0, col < lax.axis_size("ifg") - 1


def add_halo(image, above, below, left, right, field, first, last, columns):
    flags = inside()
    sides = jnp.concatenate([keep(flags[2], left[8:16, :]), keep(flags[3], right[0:8, :])], axis=0).astype(BF16)
    for row in range(8):
        lanes = pl.ds(row * 128, 128)
        halo = spread_columns(sides, row)
        if row == 0:
            halo += keep(flags[0], above[...])
        if row == 7:
            halo += keep(flags[1], below[...])
        field[:, lanes] = image[:, lanes] - SMOOTHING_WEIGHT * halo
    write_edges(field, first, last, columns)


def all_moments(field, above, left, zero, one, two, out):
    flags = inside()
    sides = jnp.concatenate([keep(flags[2], left[8:16, :]), jnp.zeros((8, DP), F32)], axis=0).astype(BF16)
    ahead = two[2]
    for row in range(8):
        halo = spread_columns(sides, row)
        if row == 0:
            halo += keep(flags[0], above[...])
        ahead -= (2.0 * SMOOTHING_WEIGHT) * fold(field[:, pl.ds(row * 128, 128)] * halo)
    rows = [zero[0], one[1], one[0], two[1], two[0], ahead]
    sums = [jnp.sum(values, axis=0, keepdims=True) for values in rows]
    out[...] = jnp.concatenate(sums + [jnp.zeros((2, 128), F32)], axis=0)


def add_and_spread(one, two, out):
    out[...] = jnp.broadcast_to((one[...] + two[...])[None], out.shape)


def combine(parts, zero, one, two, out):
    total = parts[0]
    for index in range(1, parts.shape[0]):
        total += parts[index]
    sums = jnp.sum(total, axis=1, keepdims=True)
    m0, m1, m2, m3, m4, m5 = (jnp.broadcast_to(sums[i : i + 1, :], (1, 128)) for i in range(6))
    t00, t01, t11 = m1 + SHIFT * m0, m2 + SHIFT * m1, m3 + SHIFT * m2
    t12, t22 = m4 + SHIFT * m3, m5 + SHIFT * m4
    l10, l20 = t01 / t00, t11 / t00
    pivot = t11 - l10 * t01
    off = t12 - l20 * t01
    keep = pivot > 1e-6 * t11
    safe = jnp.where(keep, pivot, 1.0)
    l21 = jnp.where(keep, off / safe, 0.0)
    last = t22 - l20 * t11 - l21 * off
    keep_last = keep & (last > 1e-6 * t22)
    y1 = m1 - l10 * m0
    y2 = m2 - l20 * m0 - l21 * y1
    c2 = jnp.where(keep_last, y2 / jnp.where(keep_last, last, 1.0), 0.0)
    c1 = jnp.where(keep, y1 / safe, 0.0) - l21 * c2
    c0 = m0 / t00 - l10 * c1 - l20 * c2
    for row in range(8):
        lanes = pl.ds(row * 128, 128)
        value = c0 * zero[:, lanes] + c1 * one[:, lanes] + c2 * two[:, lanes]
        out[pl.ds(row, DATES, stride=8), :] = value[:DATES, :]


def per_device(phase, coherence, height, gap_mask, date_pairs):
    n_ifg, n_rows = lax.axis_size("ifg"), lax.axis_size("rows")
    me = lax.axis_index("ifg")

    def permute(values, axis, target):
        return lax.ppermute(values, axis, [(i, target(i)) for i in range(lax.axis_size(axis))])

    def forward(values, axis):
        return permute(values, axis, lambda i: (i + 1) % lax.axis_size(axis))

    def backward(values, axis):
        return permute(values, axis, lambda i: (i - 1) % lax.axis_size(axis))

    stacked = sds((8, 64, 1024), BF16)
    edge = sds((128, 1024), BF16)
    phase_t, coher_t, first, last = call(
        rows_first,
        (stacked, stacked, edge, edge),
        phase,
        coherence,
        scratch=(pltpu.VMEM((2, 8, 128, 128), F32),),
        name="rows_first",
    )
    above, below = forward(last, "rows"), backward(first, "rows")
    block = sds((64, 1024), BF16)
    mask = gap_mask.astype(F32)
    pieces = [in_hbm((64, 1024), BF16)] * 8
    smooth, totals, *weight_parts = call(
        inner_rows,
        [in_hbm((8, 64, 1024), F32), sds((128, 128), F32)] + pieces,
        phase_t,
        coher_t,
        mask,
        height,
        out_specs=[pltpu.HBM, pltpu.VMEM] + [pltpu.HBM] * 8,
        scratch=(
            pltpu.VMEM((8, 64, 768), BF16),
            pltpu.VMEM((6, 64, 1024), F32),
            pltpu.SemaphoreType.DMA((4, 9)),
        ),
        name="inner_rows",
    )
    smooth, sums, *weight_parts = call(
        border_rows,
        [in_hbm((8, 64, 1024), F32), sds((n_rows, 8, 128), F32)] + pieces,
        phase_t,
        coher_t,
        above,
        below,
        mask,
        height,
        totals,
        smooth,
        *weight_parts,
        specs=[pltpu.VMEM] * 7 + [pltpu.HBM] * 9,
        out_specs=[pltpu.HBM, pltpu.VMEM] + [pltpu.HBM] * 8,
        scratch=(
            pltpu.VMEM((2, 8, 64, 128), BF16),
            pltpu.VMEM((2, 64, 1024), F32),
            pltpu.VMEM((128, 128), F32),
            pltpu.SemaphoreType.DMA((2, 9)),
        ),
        aliases={7: 0, **{8 + step: 2 + step for step in range(8)}},
        name="border_rows",
    )

    def exchange(parts):
        return [parts[0]] + [
            permute(part, "ifg", lambda i: other(i, *offset))
            for part, offset in zip(parts[1:], OFFSETS[1:])
        ]

    weight_parts = exchange(weight_parts)
    sums, weight_parts[7] = lax.optimization_barrier((sums, weight_parts[7]))
    sums = lax.all_to_all(sums, "rows", 0, 0, tiled=True)
    slope_row, *corrected_parts = call(
        correction,
        [sds((8, 128), F32)] + [block] * 8,
        sums,
        smooth,
        height,
        scratch=(pltpu.VMEM((8, 64, 1024), BF16),),
        name="correction",
    )
    corrected_parts = exchange(corrected_parts)
    sources = jnp.stack([other(me, 4 - chips, core) for chips, core in OFFSETS])
    pairs = date_pairs.reshape(n_ifg, -1, 2)[sources].reshape(-1, 2)
    dates = jnp.arange(DP, dtype=jnp.int32)
    design = ((dates[None] == pairs[:, 1:2]).astype(F32) - (dates[None] == pairs[:, 0:1]).astype(F32)).astype(BF16)
    design_t = design.T

    field = sds((DP, 1024), F32)
    edges = (sds((DP, 128), BF16), sds((DP, 128), BF16), sds((16, DP), BF16))
    moments = sds((3, 8, 128), F32)
    k0, weights, first, last, columns = call(
        right_side,
        (field, sds((512, 1024), BF16)) + edges,
        *weight_parts,
        *corrected_parts,
        design_t,
        name="right_side",
    )

    def halos(first, last, columns):
        return (
            forward(last, "rows"),
            backward(first, "rows"),
            forward(columns, "ifg"),
            backward(columns, "ifg"),
        )

    def local(with_before, with_image, name, *args):
        outs = ((field,) if with_image else ()) + (moments,)
        body = lambda *refs: apply_local(with_before, with_image, *refs)
        return call(body, outs, *args, name=name)

    def joined(image, around, name):
        return call(add_halo, (field,) + edges, image, *around, name=name)

    around = halos(first, last, columns)
    image, mom0 = local(False, True, "apply0", k0, weights, design, design_t)
    k1, first, last, columns = joined(image, around, "add_halo1")
    around = halos(first, last, columns)
    image, mom1 = local(True, True, "apply1", k1, weights, design, design_t, k0)
    k2, first, last, columns = joined(image, around, "add_halo2")
    above, left = forward(last, "rows"), forward(columns, "ifg")
    (mom2,) = local(True, False, "apply2", k2, weights, design, design_t, k1)
    part = call(
        all_moments,
        sds((8, 128), F32),
        k2,
        above,
        left,
        mom0,
        mom1,
        mom2,
        name="all_moments",
    )
    for step in (1, 2):
        part = part + permute(part, "ifg", lambda i: i ^ step)
    parts = call(
        add_and_spread,
        sds((n_rows, 8, 128), F32),
        part,
        permute(part, "ifg", lambda i: i ^ 4),
        name="add_and_spread",
    )
    parts = lax.all_to_all(parts, "rows", 0, 0, tiled=True)
    displacement = call(combine, sds((DATES * 8, 128), F32), parts, k0, k1, k2, name="combine")
    return displacement.reshape(DATES, 8, 128), slope_row[0, :64]


def solution(mesh):
    placed = (
        P("ifg", "rows", None),
        P("ifg", "rows", None),
        P("rows", None),
        P("ifg", "rows"),
        P(),
    )
    return jax.shard_map(
        per_device,
        mesh=mesh,
        in_specs=placed,
        out_specs=(P(None, "rows", "ifg"), P("ifg")),
        check_vma=False,
    )
```

```python
import jax
import jax.numpy as jnp
from jax import lax
from jax.experimental import pallas as pl
from jax.experimental.pallas import tpu as pltpu
from jax.sharding import PartitionSpec as P

DATES = 300
DP = 304
SHIFT = 4.0
SMOOTHING_WEIGHT = 0.5
RIDGE_WEIGHT = 0.05
CENTRE = 4.0 * SMOOTHING_WEIGHT + RIDGE_WEIGHT - SHIFT
F32 = jnp.float32
BF16 = jnp.bfloat16


def sds(shape, dtype):
    return jax.ShapeDtypeStruct(shape, dtype)


def in_hbm(shape, dtype):
    return pltpu.HBM(shape, dtype)


def call(body, outs, *args, specs=None, out_specs=None, scratch=(), aliases=None, name=None):
    flat = outs if isinstance(outs, (list, tuple)) else [outs]
    places = specs or [pltpu.VMEM] * len(args)
    out_places = [pl.BlockSpec(memory_space=place) for place in out_specs or [pltpu.VMEM] * len(flat)]
    return pl.pallas_call(
        body,
        out_shape=outs,
        in_specs=[pl.BlockSpec(memory_space=place) for place in places],
        out_specs=out_places if isinstance(outs, (list, tuple)) else out_places[0],
        scratch_shapes=list(scratch),
        input_output_aliases=aliases or {},
        compiler_params=pltpu.CompilerParams(vmem_limit_bytes=16 * 1024 * 1024),
        name=name,
    )(*args)


def dot(a, b):
    return jnp.dot(a, b, preferred_element_type=F32)


def split(values):
    high = values.astype(BF16)
    return high, (values - high.astype(F32)).astype(BF16)


def rows_first(phase, coher, phase_t, coher_t, first, last, phase_in, coher_in, wide, sems):
    pairs = ((phase, phase_in, phase_t), (coher, coher_in, coher_t))

    def fetch(part, block):
        ifgs, _ = block_of(block)
        return pltpu.make_async_copy(pairs[part][0].at[ifgs], pairs[part][1].at[ifgs], sems.at[part, block])

    for block in range(4):
        for part in range(2):
            fetch(part, block).start()

    def group(block, _):
        ifgs, _ = block_of(block)
        for part, (_, source, target) in enumerate(pairs):
            fetch(part, block).wait()
            for tile in range(8):
                lanes = pl.ds(tile * 128, 128)
                wide[part, tile] = source[ifgs, :, lanes].astype(F32).reshape(128, 128)
                for row in range(8):
                    target[row, ifgs, lanes] = wide[part, tile, pl.ds(row, 16, stride=8), :].astype(BF16)
        return 0

    lax.fori_loop(0, 4, group, 0)
    for part, target in enumerate((phase_t, coher_t)):
        first[pl.ds(part * 64, 64), :] = target[0]
        last[pl.ds(part * 64, 64), :] = target[7]


def shifted_sum(values, lane, last):
    left = jnp.where(lane == 0, 0.0, pltpu.roll(values, 1, 1))
    right = jnp.where(lane == last, 0.0, pltpu.roll(values, last, 1))
    return values + left + right


def fold_lanes(values):
    total = values[:, :128]
    for tile in range(1, 8):
        total += values[:, tile * 128 : tile * 128 + 128]
    return total


OFFSETS = ((0, 0), (1, 0), (3, 0), (2, 0), (2, 1), (1, 1), (3, 1), (0, 1))


def other(index, chips, core):
    return (((index >> 1) + chips) & 3) * 2 + ((index & 1) ^ core)


def owner(step):
    return other(lax.axis_index("ifg"), *OFFSETS[step])


def pieces_of(outs):
    return [*outs[:3], outs[3].at[0], outs[3].at[1], *outs[4:]]


def smooth_row(rows, lane, mask, terrain):
    denom = shifted_sum(rows[0][0] + rows[1][0] + rows[2][0], lane, 1023)
    numer = shifted_sum(rows[0][1] + rows[1][1] + rows[2][1], lane, 1023)
    top = fold_lanes(numer * terrain)
    low = fold_lanes(denom * (terrain * terrain))
    return numer / denom, (mask * (denom / 9.0)).astype(BF16), top, low


def load_row(phase_t, coher_t, row, ifgs):
    coher = coher_t[row, ifgs, :].astype(F32)
    return coher, coher * phase_t[row, ifgs, :].astype(F32)


def block_of(block):
    return pl.ds(pl.multiple_of(block * 16, 16), 16), pl.ds(pl.multiple_of(block * 16 + 64, 16), 16)


def inner_rows(phase_t, coher_t, mask, height, smooth_out, totals, *rest):
    outs, weights, smooth, sems = pieces_of(rest[:7]), *rest[7:]
    lane = lax.broadcasted_iota(jnp.int32, (16, 1024), 1)

    def copies(block):
        ifgs, _ = block_of(block)
        return [
            pltpu.make_async_copy(
                weights.at[owner(step), ifgs], out.at[ifgs, pl.ds(128, 768)], sems.at[block, step]
            )
            for step, out in enumerate(outs)
        ] + [pltpu.make_async_copy(smooth.at[:, ifgs], smooth_out.at[pl.ds(1, 6), ifgs], sems.at[block, 8])]

    def group(block, _):
        ifgs, lows = block_of(block)
        masks = mask[ifgs, :]
        rows = [load_row(phase_t, coher_t, row, ifgs) for row in (0, 1)]
        top = jnp.zeros((16, 128), F32)
        low = jnp.zeros((16, 128), F32)
        for row in range(1, 7):
            rows.append(load_row(phase_t, coher_t, row + 1, ifgs))
            value, weight, more_top, more_low = smooth_row(
                rows, lane, masks[:, row : row + 1], height[pl.ds(row, 1), :]
            )
            rows = rows[1:]
            top += more_top
            low += more_low
            smooth[row - 1, ifgs, :] = value
            for tile in range(8):
                weights[tile, ifgs, pl.ds((row - 1) * 128, 128)] = weight[:, tile * 128 : tile * 128 + 128]
        totals[ifgs, :] = top
        totals[lows, :] = low
        for copy in copies(block):
            copy.start()
        return 0

    lax.fori_loop(0, 4, group, 0)
    for block in range(4):
        for copy in copies(block):
            copy.wait()


def border_rows(phase_t, coher_t, above, below, mask, height, totals, *rest):
    smooth_out, sums, outs = rest[8], rest[9], pieces_of(rest[10:17])
    weights, smooth, added, sems = rest[17:]
    lane = lax.broadcasted_iota(jnp.int32, (16, 1024), 1)
    my_row = lax.axis_index("rows")
    valid = (my_row > 0, my_row < lax.axis_size("rows") - 1)

    def group(block, _):
        ifgs, lows = block_of(block)
        masks = mask[ifgs, :]
        top = totals[ifgs, :]
        low = totals[lows, :]
        for side, (edge, row) in enumerate(((above, 0), (below, 7))):
            coher = jnp.where(valid[side], edge[lows, :].astype(F32), 0.0)
            rows = [(coher, coher * edge[ifgs, :].astype(F32))]
            rows += [load_row(phase_t, coher_t, near, ifgs) for near in (row, 1 if row == 0 else 6)]
            value, weight, more_top, more_low = smooth_row(
                rows, lane, masks[:, row : row + 1], height[pl.ds(row, 1), :]
            )
            top += more_top
            low += more_low
            smooth[side, ifgs, :] = value
            for tile in range(8):
                weights[side, tile, ifgs, :] = weight[:, tile * 128 : tile * 128 + 128]
        added[ifgs, :] = top
        added[lows, :] = low
        return 0

    lax.fori_loop(0, 4, group, 0)
    copies = []
    for side, row in ((0, 0), (1, 7)):
        copies.append(pltpu.make_async_copy(smooth.at[side], smooth_out.at[row], sems.at[side, 8]))
        for step, out in enumerate(outs):
            lanes = pl.ds(row * 128, 128)
            copies.append(
                pltpu.make_async_copy(weights.at[side, owner(step)], out.at[:, lanes], sems.at[side, step])
            )
    for copy in copies:
        copy.start()
    sums[...] = jnp.broadcast_to(jnp.sum(added[...].T, axis=0)[None, None, :], sums.shape)
    for copy in copies:
        copy.wait()


def correction(sums, smooth, height, slope_row, *rest):
    outs, blocks = pieces_of(rest[:7]), rest[7]
    total = sums[0]
    for index in range(1, sums.shape[0]):
        total += sums[index]
    slope_row[...] = total / pltpu.roll(total, 64, 1)
    column = jnp.broadcast_to(total[0:1, :], (128, 128)).T
    slope = column[:64, :] / column[64:, :]

    def one_tile(tile, _):
        lanes = pl.ds(pl.multiple_of(tile * 128, 128), 128)
        for row in range(8):
            value = smooth[row, :, lanes] - slope * height[pl.ds(row, 1), lanes]
            blocks[tile, :, pl.ds(row * 128, 128)] = value.astype(BF16)
        return 0

    lax.fori_loop(0, 8, one_tile, 0)
    for step, out in enumerate(outs):
        out[...] = blocks[owner(step)]


def column_selector():
    row = lax.broadcasted_iota(jnp.int32, (16, 1024), 0)
    pixel = lax.broadcasted_iota(jnp.int32, (16, 1024), 1)
    wanted = jnp.where(row < 8, row * 128, (row - 8) * 128 + 127)
    return (pixel == wanted).astype(BF16)


def write_edges(field, first, last, columns):
    first[...] = field[:, pl.ds(0, 128)].astype(BF16)
    last[...] = field[:, pl.ds(896, 128)].astype(BF16)
    picked = lax.dot_general(
        column_selector(), field[...].astype(BF16), (((1,), (1,)), ((), ())), preferred_element_type=F32
    )
    columns[...] = picked.astype(BF16)


def right_side(*refs):
    weight_parts, corrected_parts = refs[:8], refs[8:16]
    design_t, field, weights, first, last, columns = refs[16:]
    for part in range(8):
        weights[pl.ds(part * 64, 64), :] = weight_parts[part][...]

    def one_chunk(chunk, _):
        lanes = pl.ds(pl.multiple_of(chunk * 256, 256), 256)
        scaled = jnp.concatenate(
            [
                weight_parts[part][:, lanes].astype(F32) * corrected_parts[part][:, lanes].astype(F32)
                for part in range(8)
            ],
            axis=0,
        )
        high, low = split(scaled)
        field[:, lanes] = dot(design_t[...], high) + dot(design_t[...], low)
        return 0

    lax.fori_loop(0, 4, one_chunk, 0)
    write_edges(field, first, last, columns)


def row_lanes(row):
    return pl.ds(pl.multiple_of(row * 128, 128), 128)


def local_image(field, weights, design, design_t, chunk):
    lanes = pl.ds(pl.multiple_of(chunk * 256, 256), 256)
    high, low = split(field[:, lanes])
    scaled = dot(design[...], jnp.concatenate([high, low], axis=0)) * weights[:, lanes].astype(F32)
    high, low = split(scaled)
    back = dot(design_t[...], high) + dot(design_t[...], low)
    lane = lax.broadcasted_iota(jnp.int32, (DP, 128), 1)
    parts = []
    for offset in range(2):
        row = 2 * chunk + offset
        here = field[:, row_lanes(row)]
        around = jnp.where(lane == 0, 0.0, pltpu.roll(here, 1, 1))
        around += jnp.where(lane == 127, 0.0, pltpu.roll(here, 127, 1))
        around += jnp.where(row > 0, field[:, row_lanes(jnp.maximum(row - 1, 0))], 0.0)
        around += jnp.where(row < 7, field[:, row_lanes(jnp.minimum(row + 1, 7))], 0.0)
        part = back[:, offset * 128 : offset * 128 + 128] + CENTRE * here - SMOOTHING_WEIGHT * around
        parts.append((row, part))
    return parts


def fold(values):
    return jnp.sum(values.reshape(DP // 8, 8, 128), axis=0)


def apply_local(with_before, with_image, *refs):
    field, weights, design, design_t = refs[:4]
    refs = refs[4:]
    before = None
    if with_before:
        before, refs = refs[0], refs[1:]
    image = None
    if with_image:
        image, refs = refs[0], refs[1:]
    moments = refs[0]

    def one_chunk(chunk, totals):
        square, cross, ahead = totals
        for row, part in local_image(field, weights, design, design_t, chunk):
            here = field[:, row_lanes(row)]
            square += fold(here * here)
            if with_before:
                cross += fold(here * before[:, row_lanes(row)])
            if with_image:
                image[:, row_lanes(row)] = part
            else:
                ahead += fold(here * part)
        return square, cross, ahead

    zero = jnp.zeros((8, 128), F32)
    totals = lax.fori_loop(0, 4, one_chunk, (zero, zero, zero))
    for index in range(3):
        moments[index] = totals[index]


def spread_columns(columns, pixels):
    row = lax.broadcasted_iota(jnp.int32, (16, 128), 0)
    lane = lax.broadcasted_iota(jnp.int32, (16, 128), 1)
    wanted = jnp.where(row < 8, row, row - 8) == pixels
    place = (wanted & (lane == jnp.where(row < 8, 0, 127))).astype(BF16)
    return lax.dot_general(columns, place, (((0,), (0,)), ((), ())), preferred_element_type=F32)


def keep(flag, values):
    return jnp.where(flag, values.astype(F32), 0.0)


def inside():
    row, col = lax.axis_index("rows"), lax.axis_index("ifg")
    return row > 0, row < lax.axis_size("rows") - 1, col > 0, col < lax.axis_size("ifg") - 1


def add_halo(image, above, below, left, right, field, first, last, columns):
    flags = inside()
    sides = jnp.concatenate([keep(flags[2], left[8:16, :]), keep(flags[3], right[0:8, :])], axis=0).astype(BF16)
    for row in range(8):
        lanes = pl.ds(row * 128, 128)
        halo = spread_columns(sides, row)
        if row == 0:
            halo += keep(flags[0], above[...])
        if row == 7:
            halo += keep(flags[1], below[...])
        field[:, lanes] = image[:, lanes] - SMOOTHING_WEIGHT * halo
    write_edges(field, first, last, columns)


def all_moments(field, above, left, zero, one, two, out):
    flags = inside()
    sides = jnp.concatenate([keep(flags[2], left[8:16, :]), jnp.zeros((8, DP), F32)], axis=0).astype(BF16)
    ahead = two[2]
    for row in range(8):
        halo = spread_columns(sides, row)
        if row == 0:
            halo += keep(flags[0], above[...])
        ahead -= (2.0 * SMOOTHING_WEIGHT) * fold(field[:, pl.ds(row * 128, 128)] * halo)
    rows = [zero[0], one[1], one[0], two[1], two[0], ahead]
    sums = [jnp.sum(values, axis=0, keepdims=True) for values in rows]
    out[...] = jnp.concatenate(sums + [jnp.zeros((2, 128), F32)], axis=0)


def add_and_spread(one, two, basis, out):
    out[...] = jnp.broadcast_to((one[...] + two[...])[None], out.shape)


def combine(parts, zero, one, two, out):
    total = parts[0]
    for index in range(1, parts.shape[0]):
        total += parts[index]
    sums = jnp.sum(total, axis=1, keepdims=True)
    m0, m1, m2, m3, m4, m5 = (jnp.broadcast_to(sums[i : i + 1, :], (1, 128)) for i in range(6))
    t00, t01, t11 = m1 + SHIFT * m0, m2 + SHIFT * m1, m3 + SHIFT * m2
    t12, t22 = m4 + SHIFT * m3, m5 + SHIFT * m4
    l10, l20 = t01 / t00, t11 / t00
    pivot = t11 - l10 * t01
    off = t12 - l20 * t01
    keep = pivot > 1e-6 * t11
    safe = jnp.where(keep, pivot, 1.0)
    l21 = jnp.where(keep, off / safe, 0.0)
    last = t22 - l20 * t11 - l21 * off
    keep_last = keep & (last > 1e-6 * t22)
    y1 = m1 - l10 * m0
    y2 = m2 - l20 * m0 - l21 * y1
    c2 = jnp.where(keep_last, y2 / jnp.where(keep_last, last, 1.0), 0.0)
    c1 = jnp.where(keep, y1 / safe, 0.0) - l21 * c2
    c0 = m0 / t00 - l10 * c1 - l20 * c2
    for row in range(8):
        lanes = pl.ds(row * 128, 128)
        value = c0 * zero[:, lanes] + c1 * one[:, lanes] + c2 * two[:, lanes]
        out[pl.ds(row, DATES, stride=8), :] = value[:DATES, :]


def per_device(phase, coherence, height, gap_mask, date_pairs):
    n_ifg, n_rows = lax.axis_size("ifg"), lax.axis_size("rows")
    me = lax.axis_index("ifg")

    def permute(values, axis, target):
        return lax.ppermute(values, axis, [(i, target(i)) for i in range(lax.axis_size(axis))])

    def forward(values, axis):
        return permute(values, axis, lambda i: (i + 1) % lax.axis_size(axis))

    def backward(values, axis):
        return permute(values, axis, lambda i: (i - 1) % lax.axis_size(axis))

    stacked = sds((8, 64, 1024), BF16)
    edge = sds((128, 1024), BF16)
    phase_t, coher_t, first, last = call(
        rows_first,
        (stacked, stacked, edge, edge),
        pltpu.with_memory_space_constraint(phase, pltpu.HBM),
        pltpu.with_memory_space_constraint(coherence, pltpu.HBM),
        specs=[pltpu.HBM] * 2,
        scratch=(
            pltpu.VMEM((64, 8, 1024), BF16),
            pltpu.VMEM((64, 8, 1024), BF16),
            pltpu.VMEM((2, 8, 128, 128), F32),
            pltpu.SemaphoreType.DMA((2, 4)),
        ),
        name="rows_first",
    )
    above, below = forward(last, "rows"), backward(first, "rows")
    mask = gap_mask.astype(F32)
    pieces = [in_hbm((2, 64, 1024) if step == 3 else (64, 1024), BF16) for step in range(7)]
    smooth, totals, *weight_parts = call(
        inner_rows,
        [in_hbm((8, 64, 1024), F32), sds((128, 128), F32)] + pieces,
        phase_t,
        coher_t,
        mask,
        height,
        out_specs=[pltpu.HBM, pltpu.VMEM] + [pltpu.HBM] * 7,
        scratch=(
            pltpu.VMEM((8, 64, 768), BF16),
            pltpu.VMEM((6, 64, 1024), F32),
            pltpu.SemaphoreType.DMA((4, 9)),
        ),
        name="inner_rows",
    )
    smooth, sums, *weight_parts = call(
        border_rows,
        [in_hbm((8, 64, 1024), F32), sds((n_rows, 8, 128), F32)] + pieces,
        phase_t,
        coher_t,
        above,
        below,
        mask,
        height,
        totals,
        smooth,
        *weight_parts,
        specs=[pltpu.VMEM] * 7 + [pltpu.HBM] * 8,
        out_specs=[pltpu.HBM, pltpu.VMEM] + [pltpu.HBM] * 7,
        scratch=(
            pltpu.VMEM((2, 8, 64, 128), BF16),
            pltpu.VMEM((2, 64, 1024), F32),
            pltpu.VMEM((128, 128), F32),
            pltpu.SemaphoreType.DMA((2, 9)),
        ),
        aliases={7: 0, **{8 + step: 2 + step for step in range(7)}},
        name="border_rows",
    )

    def exchange(parts):
        def far(i):
            return other(i, 3, 0) if i & 1 else other(i, 2, 0)

        def near(i, core):
            return other(i, 3, core) if i & 1 else other(i, 0, core)

        def offset(values, chips, core):
            return permute(values, "ifg", lambda i: other(i, chips, core))

        own, up, down, twice, up_other, down_other, pair = parts
        twice = permute(twice, "ifg", far)
        up, down = offset(up, 1, 0), offset(down, 3, 0)
        up_other, down_other = offset(up_other, 1, 1), offset(down_other, 3, 1)
        pair = offset(pair, 0, 1)
        twice, twice_other = (permute(twice[core], "ifg", lambda i: near(i, core)) for core in (0, 1))
        return [own, up, down, twice, twice_other, up_other, down_other, pair]

    weight_parts = exchange(weight_parts)
    sums, weight_parts[7] = lax.optimization_barrier((sums, weight_parts[7]))
    sums = lax.all_to_all(sums, "rows", 0, 0, tiled=True)
    sums, weight_parts = lax.optimization_barrier((sums, weight_parts))
    slope_row, *corrected_parts = call(
        correction,
        [sds((8, 128), F32)] + [sds(piece.shape, BF16) for piece in pieces],
        sums,
        smooth,
        height,
        scratch=(pltpu.VMEM((8, 64, 1024), BF16),),
        name="correction",
    )
    slope, corrected_parts[0] = lax.optimization_barrier((slope_row[0, :64], corrected_parts[0]))
    corrected_parts = exchange(corrected_parts)
    sources = jnp.stack([other(me, 4 - chips, core) for chips, core in OFFSETS])
    pairs = date_pairs.reshape(n_ifg, -1, 2)[sources].reshape(-1, 2)
    dates = jnp.arange(DP, dtype=jnp.int32)
    design = ((dates[None] == pairs[:, 1:2]).astype(F32) - (dates[None] == pairs[:, 0:1]).astype(F32)).astype(BF16)
    design_t = design.T
    design = jnp.concatenate([design, design], axis=1)

    field = sds((DP, 1024), F32)
    edges = (sds((DP, 128), BF16), sds((DP, 128), BF16), sds((16, DP), BF16))
    moments = sds((3, 8, 128), F32)
    k0, weights, first, last, columns = call(
        right_side,
        (field, sds((512, 1024), BF16)) + edges,
        *weight_parts,
        *corrected_parts,
        design_t,
        name="right_side",
    )

    def halos(first, last, columns):
        return (
            forward(last, "rows"),
            backward(first, "rows"),
            forward(columns, "ifg"),
            backward(columns, "ifg"),
        )

    def local(with_before, with_image, name, *args):
        outs = ((field,) if with_image else ()) + (moments,)
        body = lambda *refs: apply_local(with_before, with_image, *refs)
        return call(body, outs, *args, name=name)

    def joined(image, around, name):
        return call(add_halo, (field,) + edges, image, *around, name=name)

    around = halos(first, last, columns)
    image, mom0 = local(False, True, "apply0", k0, weights, design, design_t)
    k1, first, last, columns = joined(image, around, "add_halo1")
    around = halos(first, last, columns)
    image, mom1 = local(True, True, "apply1", k1, weights, design, design_t, k0)
    k2, first, last, columns = joined(image, around, "add_halo2")
    above, left = forward(last, "rows"), forward(columns, "ifg")
    (mom2,) = local(True, False, "apply2", k2, weights, design, design_t, k1)
    part = call(
        all_moments,
        sds((8, 128), F32),
        k2,
        above,
        left,
        mom0,
        mom1,
        mom2,
        name="all_moments",
    )
    for step in (1, 2):
        part = part + permute(part, "ifg", lambda i: i ^ step)
    parts = call(
        add_and_spread,
        sds((n_rows, 8, 128), F32),
        part,
        permute(part, "ifg", lambda i: i ^ 4),
        k0,
        name="add_and_spread",
    )
    parts = lax.all_to_all(parts, "rows", 0, 0, tiled=True)
    displacement = call(combine, sds((DATES * 8, 128), F32), parts, k0, k1, k2, name="combine")
    return displacement.reshape(DATES, 8, 128), slope


def solution(mesh):
    placed = (
        P("ifg", "rows", None),
        P("ifg", "rows", None),
        P("rows", None),
        P("ifg", "rows"),
        P(),
    )
    return jax.shard_map(
        per_device,
        mesh=mesh,
        in_specs=placed,
        out_specs=(P(None, "rows", "ifg"), P("ifg")),
        check_vma=False,
    )
```

```python
import jax
import jax.numpy as jnp
from jax import lax
from jax.experimental import pallas as pl
from jax.experimental.pallas import tpu as pltpu
from jax.sharding import PartitionSpec as P

DATES = 300
DP = 304
SHIFT = 4.0
SMOOTHING_WEIGHT = 0.5
RIDGE_WEIGHT = 0.05
CENTRE = 4.0 * SMOOTHING_WEIGHT + RIDGE_WEIGHT - SHIFT
F32 = jnp.float32
BF16 = jnp.bfloat16


def sds(shape, dtype):
    return jax.ShapeDtypeStruct(shape, dtype)


def in_hbm(shape, dtype):
    return pltpu.HBM(shape, dtype)


def call(body, outs, *args, specs=None, out_specs=None, scratch=(), aliases=None, name=None):
    flat = outs if isinstance(outs, (list, tuple)) else [outs]
    places = specs or [pltpu.VMEM] * len(args)
    out_places = [pl.BlockSpec(memory_space=place) for place in out_specs or [pltpu.VMEM] * len(flat)]
    return pl.pallas_call(
        body,
        out_shape=outs,
        in_specs=[pl.BlockSpec(memory_space=place) for place in places],
        out_specs=out_places if isinstance(outs, (list, tuple)) else out_places[0],
        scratch_shapes=list(scratch),
        input_output_aliases=aliases or {},
        compiler_params=pltpu.CompilerParams(vmem_limit_bytes=16 * 1024 * 1024),
        name=name,
    )(*args)


def dot(a, b):
    return jnp.dot(a, b, preferred_element_type=F32)


def split(values):
    high = values.astype(BF16)
    return high, (values - high.astype(F32)).astype(BF16)


def rows_first(phase, coher, phase_t, coher_t, first, last, phase_in, coher_in, wide, sems):
    pairs = ((phase, phase_in, phase_t), (coher, coher_in, coher_t))

    def fetch(part, block):
        ifgs, _ = block_of(block)
        return pltpu.make_async_copy(pairs[part][0].at[ifgs], pairs[part][1].at[ifgs], sems.at[part, block])

    for block in range(4):
        for part in range(2):
            fetch(part, block).start()

    def group(block, _):
        ifgs, _ = block_of(block)
        for part, (_, source, target) in enumerate(pairs):
            fetch(part, block).wait()
            for tile in range(8):
                lanes = pl.ds(tile * 128, 128)
                wide[part, tile] = source[ifgs, :, lanes].astype(F32).reshape(128, 128)
                for row in range(8):
                    target[row, ifgs, lanes] = wide[part, tile, pl.ds(row, 16, stride=8), :].astype(BF16)
        return 0

    lax.fori_loop(0, 4, group, 0)
    for part, target in enumerate((phase_t, coher_t)):
        first[pl.ds(part * 64, 64), :] = target[0]
        last[pl.ds(part * 64, 64), :] = target[7]


def shifted_sum(values, lane, last):
    left = jnp.where(lane == 0, 0.0, pltpu.roll(values, 1, 1))
    right = jnp.where(lane == last, 0.0, pltpu.roll(values, last, 1))
    return values + left + right


def fold_lanes(values):
    total = values[:, :128]
    for tile in range(1, 8):
        total += values[:, tile * 128 : tile * 128 + 128]
    return total


OFFSETS = ((0, 0), (1, 0), (3, 0), (2, 0), (2, 1), (1, 1), (3, 1), (0, 1))


def other(index, chips, core):
    return (((index >> 1) + chips) & 3) * 2 + ((index & 1) ^ core)


def owner(step):
    return other(lax.axis_index("ifg"), *OFFSETS[step])


def smooth_row(rows, lane, mask, terrain):
    denom = shifted_sum(rows[0][0] + rows[1][0] + rows[2][0], lane, 1023)
    numer = shifted_sum(rows[0][1] + rows[1][1] + rows[2][1], lane, 1023)
    top = fold_lanes(numer * terrain)
    low = fold_lanes(denom * (terrain * terrain))
    return numer / denom, (mask * (denom / 9.0)).astype(BF16), top, low


def load_row(phase_t, coher_t, row, ifgs):
    coher = coher_t[row, ifgs, :].astype(F32)
    return coher, coher * phase_t[row, ifgs, :].astype(F32)


def block_of(block):
    return pl.ds(pl.multiple_of(block * 16, 16), 16), pl.ds(pl.multiple_of(block * 16 + 64, 16), 16)


def inner_rows(phase_t, coher_t, mask, height, smooth_out, totals, *rest):
    outs, weights, smooth, sems = rest[:8], *rest[8:]
    lane = lax.broadcasted_iota(jnp.int32, (16, 1024), 1)

    def copies(block):
        ifgs, _ = block_of(block)
        return [
            pltpu.make_async_copy(
                weights.at[owner(step), ifgs], out.at[ifgs, pl.ds(128, 768)], sems.at[block, step]
            )
            for step, out in enumerate(outs)
        ] + [pltpu.make_async_copy(smooth.at[:, ifgs], smooth_out.at[pl.ds(1, 6), ifgs], sems.at[block, 8])]

    def group(block, _):
        ifgs, lows = block_of(block)
        masks = mask[ifgs, :]
        rows = [load_row(phase_t, coher_t, row, ifgs) for row in (0, 1)]
        top = jnp.zeros((16, 128), F32)
        low = jnp.zeros((16, 128), F32)
        for row in range(1, 7):
            rows.append(load_row(phase_t, coher_t, row + 1, ifgs))
            value, weight, more_top, more_low = smooth_row(
                rows, lane, masks[:, row : row + 1], height[pl.ds(row, 1), :]
            )
            rows = rows[1:]
            top += more_top
            low += more_low
            smooth[row - 1, ifgs, :] = value
            for tile in range(8):
                weights[tile, ifgs, pl.ds((row - 1) * 128, 128)] = weight[:, tile * 128 : tile * 128 + 128]
        totals[ifgs, :] = top
        totals[lows, :] = low
        for copy in copies(block):
            copy.start()
        return 0

    lax.fori_loop(0, 4, group, 0)
    for block in range(4):
        for copy in copies(block):
            copy.wait()


def border_rows(phase_t, coher_t, above, below, mask, height, totals, *rest):
    smooth_out, sums, outs = rest[9], rest[10], rest[11:19]
    weights, smooth, added, sems = rest[19:]
    lane = lax.broadcasted_iota(jnp.int32, (16, 1024), 1)
    my_row = lax.axis_index("rows")
    valid = (my_row > 0, my_row < lax.axis_size("rows") - 1)

    def group(block, _):
        ifgs, lows = block_of(block)
        masks = mask[ifgs, :]
        top = totals[ifgs, :]
        low = totals[lows, :]
        for side, (edge, row) in enumerate(((above, 0), (below, 7))):
            coher = jnp.where(valid[side], edge[lows, :].astype(F32), 0.0)
            rows = [(coher, coher * edge[ifgs, :].astype(F32))]
            rows += [load_row(phase_t, coher_t, near, ifgs) for near in (row, 1 if row == 0 else 6)]
            value, weight, more_top, more_low = smooth_row(
                rows, lane, masks[:, row : row + 1], height[pl.ds(row, 1), :]
            )
            top += more_top
            low += more_low
            smooth[side, ifgs, :] = value
            for tile in range(8):
                weights[side, tile, ifgs, :] = weight[:, tile * 128 : tile * 128 + 128]
        added[ifgs, :] = top
        added[lows, :] = low
        return 0

    lax.fori_loop(0, 4, group, 0)
    copies = []
    for side, row in ((0, 0), (1, 7)):
        copies.append(pltpu.make_async_copy(smooth.at[side], smooth_out.at[row], sems.at[side, 8]))
        for step, out in enumerate(outs):
            lanes = pl.ds(row * 128, 128)
            copies.append(
                pltpu.make_async_copy(weights.at[side, owner(step)], out.at[:, lanes], sems.at[side, step])
            )
    for copy in copies:
        copy.start()
    sums[...] = jnp.broadcast_to(jnp.sum(added[...].T, axis=0)[None, None, :], sums.shape)
    for copy in copies:
        copy.wait()


def stage(source, out, sems):
    copies = [
        pltpu.make_async_copy(source.at[pl.ds(part * 2, 2)], out.at[pl.ds(part * 2, 2)], sems.at[part])
        for part in range(4)
    ]
    for copy in copies:
        copy.start()
    for copy in copies:
        copy.wait()


def correction(sums, smooth, height, slope_row, *rest):
    outs, blocks = rest[:8], rest[8]
    total = sums[0]
    for index in range(1, sums.shape[0]):
        total += sums[index]
    slope_row[...] = total / pltpu.roll(total, 64, 1)
    column = jnp.broadcast_to(total, (128, 128)).T
    slope = column[:64, :] / column[64:, :]

    def one_tile(tile, _):
        lanes = pl.ds(pl.multiple_of(tile * 128, 128), 128)
        for row in range(8):
            value = smooth[row, :, lanes] - slope * height[pl.ds(row, 1), lanes]
            blocks[tile, :, pl.ds(row * 128, 128)] = value.astype(BF16)
        return 0

    lax.fori_loop(0, 8, one_tile, 0)
    for step, out in enumerate(outs):
        out[...] = blocks[owner(step)]


def column_selector():
    row = lax.broadcasted_iota(jnp.int32, (16, 1024), 0)
    pixel = lax.broadcasted_iota(jnp.int32, (16, 1024), 1)
    wanted = jnp.where(row < 8, row * 128, (row - 8) * 128 + 127)
    return (pixel == wanted).astype(BF16)


def write_edges(field, first, last, columns):
    first[...] = field[:, pl.ds(0, 128)].astype(BF16)
    last[...] = field[:, pl.ds(896, 128)].astype(BF16)
    picked = lax.dot_general(
        column_selector(), field[...].astype(BF16), (((1,), (1,)), ((), ())), preferred_element_type=F32
    )
    columns[...] = picked.astype(BF16)


def right_side(*refs):
    weight_parts, corrected_parts = refs[:8], refs[8:16]
    design_t, field, weights, first, last, columns = refs[16:]
    for part in range(8):
        weights[pl.ds(part * 64, 64), :] = weight_parts[part][...]

    def one_chunk(chunk, _):
        lanes = pl.ds(pl.multiple_of(chunk * 256, 256), 256)
        scaled = jnp.concatenate(
            [
                weight_parts[part][:, lanes].astype(F32) * corrected_parts[part][:, lanes].astype(F32)
                for part in range(8)
            ],
            axis=0,
        )
        high, low = split(scaled)
        field[:, lanes] = dot(design_t[...], high) + dot(design_t[...], low)
        return 0

    lax.fori_loop(0, 4, one_chunk, 0)
    write_edges(field, first, last, columns)


def row_lanes(row):
    return pl.ds(pl.multiple_of(row * 128, 128), 128)


def local_image(field, weights, design, design_t, chunk):
    lanes = pl.ds(pl.multiple_of(chunk * 256, 256), 256)
    high, low = split(field[:, lanes])
    scaled = dot(design[...], jnp.concatenate([high, low], axis=0)) * weights[:, lanes].astype(F32)
    high, low = split(scaled)
    back = dot(design_t[...], high) + dot(design_t[...], low)
    lane = lax.broadcasted_iota(jnp.int32, (DP, 128), 1)
    parts = []
    for offset in range(2):
        row = 2 * chunk + offset
        here = field[:, row_lanes(row)]
        around = jnp.where(lane == 0, 0.0, pltpu.roll(here, 1, 1))
        around += jnp.where(lane == 127, 0.0, pltpu.roll(here, 127, 1))
        around += jnp.where(row > 0, field[:, row_lanes(jnp.maximum(row - 1, 0))], 0.0)
        around += jnp.where(row < 7, field[:, row_lanes(jnp.minimum(row + 1, 7))], 0.0)
        part = back[:, offset * 128 : offset * 128 + 128] + CENTRE * here - SMOOTHING_WEIGHT * around
        parts.append((row, part))
    return parts


def fold(values):
    return jnp.sum(values.reshape(DP // 8, 8, 128), axis=0)


def apply_local(with_before, with_image, *refs):
    field, weights, design, design_t = refs[:4]
    refs = refs[4:]
    before = None
    if with_before:
        before, refs = refs[0], refs[1:]
    image = None
    if with_image:
        image, refs = refs[0], refs[1:]
    moments = refs[0]

    def one_chunk(chunk, totals):
        square, cross, ahead = totals
        for row, part in local_image(field, weights, design, design_t, chunk):
            here = field[:, row_lanes(row)]
            square += fold(here * here)
            if with_before:
                cross += fold(here * before[:, row_lanes(row)])
            if with_image:
                image[:, row_lanes(row)] = part
            else:
                ahead += fold(here * part)
        return square, cross, ahead

    zero = jnp.zeros((8, 128), F32)
    totals = lax.fori_loop(0, 4, one_chunk, (zero, zero, zero), unroll=True)
    for index in range(3):
        moments[index] = totals[index]


def spread_columns(columns, pixels):
    row = lax.broadcasted_iota(jnp.int32, (16, 128), 0)
    lane = lax.broadcasted_iota(jnp.int32, (16, 128), 1)
    wanted = jnp.where(row < 8, row, row - 8) == pixels
    place = (wanted & (lane == jnp.where(row < 8, 0, 127))).astype(BF16)
    return lax.dot_general(columns, place, (((0,), (0,)), ((), ())), preferred_element_type=F32)


def keep(flag, values):
    return jnp.where(flag, values.astype(F32), 0.0)


def inside():
    row, col = lax.axis_index("rows"), lax.axis_index("ifg")
    return row > 0, row < lax.axis_size("rows") - 1, col > 0, col < lax.axis_size("ifg") - 1


def add_halo(image, above, below, left, right, field, first, last, columns):
    flags = inside()
    sides = jnp.concatenate([keep(flags[2], left[8:16, :]), keep(flags[3], right[0:8, :])], axis=0).astype(BF16)
    for row in range(8):
        lanes = pl.ds(row * 128, 128)
        halo = spread_columns(sides, row)
        if row == 0:
            halo += keep(flags[0], above[...])
        if row == 7:
            halo += keep(flags[1], below[...])
        field[:, lanes] = image[:, lanes] - SMOOTHING_WEIGHT * halo
    write_edges(field, first, last, columns)


def all_moments(field, above, left, zero, one, two, out):
    flags = inside()
    sides = jnp.concatenate([keep(flags[2], left[8:16, :]), jnp.zeros((8, DP), F32)], axis=0).astype(BF16)
    ahead = two[2]
    for row in range(8):
        halo = spread_columns(sides, row)
        if row == 0:
            halo += keep(flags[0], above[...])
        ahead -= (2.0 * SMOOTHING_WEIGHT) * fold(field[:, pl.ds(row * 128, 128)] * halo)
    rows = [zero[0], one[1], one[0], two[1], two[0], ahead]
    lane = lax.broadcasted_iota(jnp.int32, (1, 128), 1)
    total = jnp.zeros((1, 128), F32)
    for index, values in enumerate(rows):
        line = jnp.sum(values, axis=0, keepdims=True)
        total += jnp.where(lane == index, jnp.sum(line, axis=1, keepdims=True), 0.0)
    out[...] = total


def add_and_spread(one, two, basis, out):
    out[...] = jnp.broadcast_to((one[...] + two[...])[None], out.shape)


def combine(parts, zero, one, two, out, field, sems):
    total = parts[0]
    for index in range(1, parts.shape[0]):
        total += parts[index]
    m0, m1, m2, m3, m4, m5 = (jnp.broadcast_to(total[:, i : i + 1], (1, 128)) for i in range(6))
    t00, t01, t11 = m1 + SHIFT * m0, m2 + SHIFT * m1, m3 + SHIFT * m2
    t12, t22 = m4 + SHIFT * m3, m5 + SHIFT * m4
    l10, l20 = t01 / t00, t11 / t00
    pivot = t11 - l10 * t01
    off = t12 - l20 * t01
    keep = pivot > 1e-6 * t11
    safe = jnp.where(keep, pivot, 1.0)
    l21 = jnp.where(keep, off / safe, 0.0)
    last = t22 - l20 * t11 - l21 * off
    keep_last = keep & (last > 1e-6 * t22)
    y1 = m1 - l10 * m0
    y2 = m2 - l20 * m0 - l21 * y1
    c2 = jnp.where(keep_last, y2 / jnp.where(keep_last, last, 1.0), 0.0)
    c1 = jnp.where(keep, y1 / safe, 0.0) - l21 * c2
    c0 = m0 / t00 - l10 * c1 - l20 * c2
    copies = []
    for part in range(4):
        count = min(80, DATES - part * 80)
        dates = pl.ds(part * 80, (count + 7) // 8 * 8)
        for row in range(8):
            lanes = pl.ds(row * 128, 128)
            value = c0 * zero[dates, lanes] + c1 * one[dates, lanes] + c2 * two[dates, lanes]
            field[pl.ds(part * 640 + row, count, stride=8), :] = value[:count, :]
        lines = pl.ds(part * 640, count * 8)
        copies.append(pltpu.make_async_copy(field.at[lines], out.at[lines], sems.at[part]))
        copies[-1].start()
    for copy in copies:
        copy.wait()


def per_device(phase, coherence, height, gap_mask, date_pairs):
    n_ifg, n_rows = lax.axis_size("ifg"), lax.axis_size("rows")
    me = lax.axis_index("ifg")

    def permute(values, axis, target):
        return lax.ppermute(values, axis, [(i, target(i)) for i in range(lax.axis_size(axis))])

    def forward(values, axis):
        return permute(values, axis, lambda i: (i + 1) % lax.axis_size(axis))

    def backward(values, axis):
        return permute(values, axis, lambda i: (i - 1) % lax.axis_size(axis))

    stacked = sds((8, 64, 1024), BF16)
    edge = sds((128, 1024), BF16)
    phase_t, coher_t, first, last = call(
        rows_first,
        (stacked, stacked, edge, edge),
        pltpu.with_memory_space_constraint(phase, pltpu.HBM),
        pltpu.with_memory_space_constraint(coherence, pltpu.HBM),
        specs=[pltpu.HBM] * 2,
        scratch=(
            pltpu.VMEM((64, 8, 1024), BF16),
            pltpu.VMEM((64, 8, 1024), BF16),
            pltpu.VMEM((2, 8, 128, 128), F32),
            pltpu.SemaphoreType.DMA((2, 4)),
        ),
        name="rows_first",
    )
    above, below = forward(last, "rows"), backward(first, "rows")
    mask = gap_mask.astype(F32)
    pieces = [in_hbm((64, 1024), BF16)] * 8
    smooth, totals, *weight_parts = call(
        inner_rows,
        [in_hbm((8, 64, 1024), F32), sds((128, 128), F32)] + pieces,
        phase_t,
        coher_t,
        mask,
        height,
        out_specs=[pltpu.HBM, pltpu.VMEM] + [pltpu.HBM] * 8,
        scratch=(
            pltpu.VMEM((8, 64, 768), BF16),
            pltpu.VMEM((6, 64, 1024), F32),
            pltpu.SemaphoreType.DMA((4, 9)),
        ),
        name="inner_rows",
    )
    smooth, sums, *weight_parts = call(
        border_rows,
        [in_hbm((8, 64, 1024), F32), sds((n_rows, 1, 128), F32)] + pieces,
        phase_t,
        coher_t,
        above,
        below,
        mask,
        height,
        totals,
        smooth,
        *weight_parts,
        specs=[pltpu.VMEM] * 7 + [pltpu.HBM] * 9,
        out_specs=[pltpu.HBM, pltpu.VMEM] + [pltpu.HBM] * 8,
        scratch=(
            pltpu.VMEM((2, 8, 64, 128), BF16),
            pltpu.VMEM((2, 64, 1024), F32),
            pltpu.VMEM((128, 128), F32),
            pltpu.SemaphoreType.DMA((2, 9)),
        ),
        aliases={7: 0, **{8 + step: 2 + step for step in range(8)}},
        name="border_rows",
    )

    def exchange(parts):
        return [parts[0]] + [
            permute(part, "ifg", lambda i: other(i, *offset))
            for part, offset in zip(parts[1:], OFFSETS[1:])
        ]

    weight_parts = exchange(weight_parts)
    sums, weight_parts[7] = lax.optimization_barrier((sums, weight_parts[7]))
    sums = lax.all_to_all(sums, "rows", 0, 0, tiled=True)
    smooth = call(
        stage,
        sds((8, 64, 1024), F32),
        pltpu.with_memory_space_constraint(smooth, pltpu.HBM),
        specs=[pltpu.HBM],
        scratch=(pltpu.SemaphoreType.DMA((4,)),),
        name="stage",
    )
    slope_row, *corrected_parts = call(
        correction,
        [sds((1, 128), F32)] + [sds((64, 1024), BF16)] * 8,
        sums,
        smooth,
        height,
        scratch=(pltpu.VMEM((8, 64, 1024), BF16),),
        name="correction",
    )
    slope, corrected_parts[0] = lax.optimization_barrier((slope_row[0, :64], corrected_parts[0]))
    corrected_parts = exchange(corrected_parts)
    sources = jnp.stack([other(me, 4 - chips, core) for chips, core in OFFSETS])
    pairs = date_pairs.reshape(n_ifg, -1, 2)[sources].reshape(-1, 2)
    dates = jnp.arange(DP, dtype=jnp.int32)
    design = ((dates[None] == pairs[:, 1:2]).astype(F32) - (dates[None] == pairs[:, 0:1]).astype(F32)).astype(BF16)
    design_t = design.T
    design = jnp.concatenate([design, design], axis=1)

    field = sds((DP, 1024), F32)
    edges = (sds((DP, 128), BF16), sds((DP, 128), BF16), sds((16, DP), BF16))
    moments = sds((3, 8, 128), F32)
    k0, weights, first, last, columns = call(
        right_side,
        (field, sds((512, 1024), BF16)) + edges,
        *weight_parts,
        *corrected_parts,
        design_t,
        name="right_side",
    )

    def halos(first, last, columns):
        return (
            forward(last, "rows"),
            backward(first, "rows"),
            forward(columns, "ifg"),
            backward(columns, "ifg"),
        )

    def local(with_before, with_image, name, *args):
        outs = ((field,) if with_image else ()) + (moments,)
        body = lambda *refs: apply_local(with_before, with_image, *refs)
        return call(body, outs, *args, name=name)

    def joined(image, around, name):
        return call(add_halo, (field,) + edges, image, *around, name=name)

    around = halos(first, last, columns)
    image, mom0 = local(False, True, "apply0", k0, weights, design, design_t)
    k1, first, last, columns = joined(image, around, "add_halo1")
    around = halos(first, last, columns)
    image, mom1 = local(True, True, "apply1", k1, weights, design, design_t, k0)
    k2, first, last, columns = joined(image, around, "add_halo2")
    above, left = forward(last, "rows"), forward(columns, "ifg")
    (mom2,) = local(True, False, "apply2", k2, weights, design, design_t, k1)
    part = call(
        all_moments,
        sds((1, 128), F32),
        k2,
        above,
        left,
        mom0,
        mom1,
        mom2,
        name="all_moments",
    )
    for step in (1, 2):
        part = part + permute(part, "ifg", lambda i: i ^ step)
    parts = call(
        add_and_spread,
        sds((n_rows, 1, 128), F32),
        part,
        permute(part, "ifg", lambda i: i ^ 4),
        k0,
        name="add_and_spread",
    )
    parts = lax.all_to_all(parts, "rows", 0, 0, tiled=True)
    displacement = call(
        combine,
        sds((DATES * 8, 128), F32),
        parts,
        k0,
        k1,
        k2,
        out_specs=[pltpu.HBM],
        scratch=(pltpu.VMEM((DATES * 8, 128), F32), pltpu.SemaphoreType.DMA((4,))),
        name="combine",
    )
    return displacement.reshape(DATES, 8, 128), slope


def solution(mesh):
    placed = (
        P("ifg", "rows", None),
        P("ifg", "rows", None),
        P("rows", None),
        P("ifg", "rows"),
        P(),
    )
    return jax.shard_map(
        per_device,
        mesh=mesh,
        in_specs=placed,
        out_specs=(P(None, "rows", "ifg"), P("ifg")),
        check_vma=False,
    )
```

```python
import jax
import jax.numpy as jnp
from jax import lax
from jax.experimental import pallas as pl
from jax.experimental.pallas import tpu as pltpu
from jax.sharding import PartitionSpec as P

DATES = 300
DP = 304
SHIFT = 4.0
SMOOTHING_WEIGHT = 0.5
RIDGE_WEIGHT = 0.05
CENTRE = 4.0 * SMOOTHING_WEIGHT + RIDGE_WEIGHT - SHIFT
F32 = jnp.float32
BF16 = jnp.bfloat16


def sds(shape, dtype):
    return jax.ShapeDtypeStruct(shape, dtype)


def in_hbm(shape, dtype):
    return pltpu.HBM(shape, dtype)


def call(body, outs, *args, specs=None, out_specs=None, scratch=(), aliases=None, name=None):
    flat = outs if isinstance(outs, (list, tuple)) else [outs]
    places = specs or [pltpu.VMEM] * len(args)
    out_places = [pl.BlockSpec(memory_space=place) for place in out_specs or [pltpu.VMEM] * len(flat)]
    return pl.pallas_call(
        body,
        out_shape=outs,
        in_specs=[pl.BlockSpec(memory_space=place) for place in places],
        out_specs=out_places if isinstance(outs, (list, tuple)) else out_places[0],
        scratch_shapes=list(scratch),
        input_output_aliases=aliases or {},
        compiler_params=pltpu.CompilerParams(vmem_limit_bytes=16 * 1024 * 1024),
        name=name,
    )(*args)


def dot(a, b):
    return jnp.dot(a, b, preferred_element_type=F32)


def split(values):
    high = values.astype(BF16)
    return high, (values - high.astype(F32)).astype(BF16)


def rows_first(phase, coher, phase_t, coher_t, first, last, phase_in, coher_in, wide, sems):
    pairs = ((phase, phase_in, phase_t), (coher, coher_in, coher_t))

    def fetch(part, block):
        ifgs, _ = block_of(block)
        return pltpu.make_async_copy(pairs[part][0].at[ifgs], pairs[part][1].at[ifgs], sems.at[part, block])

    for block in range(4):
        for part in range(2):
            fetch(part, block).start()

    def group(block, _):
        ifgs, _ = block_of(block)
        for part, (_, source, target) in enumerate(pairs):
            fetch(part, block).wait()
            for tile in range(8):
                lanes = pl.ds(tile * 128, 128)
                wide[part, tile] = source[ifgs, :, lanes].astype(F32).reshape(128, 128)
                for row in range(8):
                    target[row, ifgs, lanes] = wide[part, tile, pl.ds(row, 16, stride=8), :].astype(BF16)
        return 0

    lax.fori_loop(0, 4, group, 0)
    for part, target in enumerate((phase_t, coher_t)):
        first[pl.ds(part * 64, 64), :] = target[0]
        last[pl.ds(part * 64, 64), :] = target[7]


def shifted_sum(values, lane, last):
    left = jnp.where(lane == 0, 0.0, pltpu.roll(values, 1, 1))
    right = jnp.where(lane == last, 0.0, pltpu.roll(values, last, 1))
    return values + left + right


def fold_lanes(values):
    total = values[:, :128]
    for tile in range(1, 8):
        total += values[:, tile * 128 : tile * 128 + 128]
    return total


OFFSETS = ((0, 0), (1, 0), (3, 0), (2, 0), (2, 1), (1, 1), (3, 1), (0, 1))


def other(index, chips, core):
    return (((index >> 1) + chips) & 3) * 2 + ((index & 1) ^ core)


def owner(step):
    return other(lax.axis_index("ifg"), *OFFSETS[step])


def pieces_of(outs):
    own, up, down, twice, pair = outs
    return [own, up.at[0], down.at[0], twice.at[0], twice.at[1], up.at[1], down.at[1], pair]


def smooth_row(rows, lane, mask, terrain):
    denom = shifted_sum(rows[0][0] + rows[1][0] + rows[2][0], lane, 1023)
    numer = shifted_sum(rows[0][1] + rows[1][1] + rows[2][1], lane, 1023)
    top = fold_lanes(numer * terrain)
    low = fold_lanes(denom * (terrain * terrain))
    return numer / denom, (mask * (denom / 9.0)).astype(BF16), top, low


def load_row(phase_t, coher_t, row, ifgs):
    coher = coher_t[row, ifgs, :].astype(F32)
    return coher, coher * phase_t[row, ifgs, :].astype(F32)


def block_of(block):
    return pl.ds(pl.multiple_of(block * 16, 16), 16), pl.ds(pl.multiple_of(block * 16 + 64, 16), 16)


def inner_rows(phase_t, coher_t, mask, height, smooth_out, totals, *rest):
    outs, weights, smooth, sems = pieces_of(rest[:5]), *rest[5:]
    lane = lax.broadcasted_iota(jnp.int32, (16, 1024), 1)

    def copies(block):
        ifgs, _ = block_of(block)
        return [
            pltpu.make_async_copy(
                weights.at[owner(step), ifgs], out.at[ifgs, pl.ds(128, 768)], sems.at[block, step]
            )
            for step, out in enumerate(outs)
        ] + [pltpu.make_async_copy(smooth.at[:, ifgs], smooth_out.at[pl.ds(1, 6), ifgs], sems.at[block, 8])]

    def group(block, _):
        ifgs, lows = block_of(block)
        masks = mask[ifgs, :]
        rows = [load_row(phase_t, coher_t, row, ifgs) for row in (0, 1)]
        top = jnp.zeros((16, 128), F32)
        low = jnp.zeros((16, 128), F32)
        for row in range(1, 7):
            rows.append(load_row(phase_t, coher_t, row + 1, ifgs))
            value, weight, more_top, more_low = smooth_row(
                rows, lane, masks[:, row : row + 1], height[pl.ds(row, 1), :]
            )
            rows = rows[1:]
            top += more_top
            low += more_low
            smooth[row - 1, ifgs, :] = value
            for tile in range(8):
                weights[tile, ifgs, pl.ds((row - 1) * 128, 128)] = weight[:, tile * 128 : tile * 128 + 128]
        totals[ifgs, :] = top
        totals[lows, :] = low
        for copy in copies(block):
            copy.start()
        return 0

    lax.fori_loop(0, 4, group, 0)
    for block in range(4):
        for copy in copies(block):
            copy.wait()


def border_rows(phase_t, coher_t, above, below, mask, height, totals, *rest):
    smooth_out, sums, outs = rest[6], rest[7], pieces_of(rest[8:13])
    weights, smooth, added, sems = rest[13:]
    lane = lax.broadcasted_iota(jnp.int32, (16, 1024), 1)
    my_row = lax.axis_index("rows")
    valid = (my_row > 0, my_row < lax.axis_size("rows") - 1)

    def group(block, _):
        ifgs, lows = block_of(block)
        masks = mask[ifgs, :]
        top = totals[ifgs, :]
        low = totals[lows, :]
        for side, (edge, row) in enumerate(((above, 0), (below, 7))):
            coher = jnp.where(valid[side], edge[lows, :].astype(F32), 0.0)
            rows = [(coher, coher * edge[ifgs, :].astype(F32))]
            rows += [load_row(phase_t, coher_t, near, ifgs) for near in (row, 1 if row == 0 else 6)]
            value, weight, more_top, more_low = smooth_row(
                rows, lane, masks[:, row : row + 1], height[pl.ds(row, 1), :]
            )
            top += more_top
            low += more_low
            smooth[side, ifgs, :] = value
            for tile in range(8):
                weights[side, tile, ifgs, :] = weight[:, tile * 128 : tile * 128 + 128]
        added[ifgs, :] = top
        added[lows, :] = low
        return 0

    lax.fori_loop(0, 4, group, 0)
    copies = []
    for side, row in ((0, 0), (1, 7)):
        copies.append(pltpu.make_async_copy(smooth.at[side], smooth_out.at[row], sems.at[side, 8]))
        for step, out in enumerate(outs):
            lanes = pl.ds(row * 128, 128)
            copies.append(
                pltpu.make_async_copy(weights.at[side, owner(step)], out.at[:, lanes], sems.at[side, step])
            )
    for copy in copies:
        copy.start()
    sums[...] = jnp.broadcast_to(jnp.sum(added[...].T, axis=0, keepdims=True), sums.shape)
    for copy in copies:
        copy.wait()


def stage(source, out, sems):
    copies = [
        pltpu.make_async_copy(source.at[pl.ds(part * 2, 2)], out.at[pl.ds(part * 2, 2)], sems.at[part])
        for part in range(4)
    ]
    for copy in copies:
        copy.start()
    for copy in copies:
        copy.wait()


def correction(sums, smooth, height, slope_row, *rest):
    outs, blocks = rest[:8], rest[8]
    total = sums[0]
    for index in range(1, sums.shape[0]):
        total += sums[index]
    slope_row[...] = total / pltpu.roll(total, 64, 1)
    column = jnp.broadcast_to(total, (128, 128)).T
    slope = column[:64, :] / column[64:, :]

    def one_tile(tile, _):
        lanes = pl.ds(pl.multiple_of(tile * 128, 128), 128)
        for row in range(8):
            value = smooth[row, :, lanes] - slope * height[pl.ds(row, 1), lanes]
            blocks[tile, :, pl.ds(row * 128, 128)] = value.astype(BF16)
        return 0

    lax.fori_loop(0, 8, one_tile, 0)
    for step, out in enumerate(outs):
        out[...] = blocks[owner(step)]


def column_selector():
    row = lax.broadcasted_iota(jnp.int32, (16, 1024), 0)
    pixel = lax.broadcasted_iota(jnp.int32, (16, 1024), 1)
    wanted = jnp.where(row < 8, row * 128, (row - 8) * 128 + 127)
    return (pixel == wanted).astype(BF16)


def write_edges(field, last, columns, first=None):
    if first is not None:
        first[...] = field[:, pl.ds(0, 128)].astype(BF16)
    last[...] = field[:, pl.ds(896, 128)].astype(BF16)
    picked = lax.dot_general(
        column_selector(), field[...].astype(BF16), (((1,), (1,)), ((), ())), preferred_element_type=F32
    )
    columns[...] = picked.astype(BF16)


def right_side(*refs):
    own, up, down, twice, swap = refs[:5]
    weight_parts = [own, up.at[0], down.at[0], twice.at[0]] + [swap.at[part] for part in range(4)]
    corrected_parts = refs[5:13]
    design_t, field, weights, *edges = refs[13:]
    for part in range(8):
        weights[pl.ds(part * 64, 64), :] = weight_parts[part][...]

    def one_chunk(chunk, _):
        lanes = pl.ds(pl.multiple_of(chunk * 256, 256), 256)
        scaled = jnp.concatenate(
            [
                weight_parts[part][:, lanes].astype(F32) * corrected_parts[part][:, lanes].astype(F32)
                for part in range(8)
            ],
            axis=0,
        )
        high, low = split(scaled)
        field[:, lanes] = dot(design_t[...], high) + dot(design_t[...], low)
        return 0

    lax.fori_loop(0, 4, one_chunk, 0)
    write_edges(field, *edges)


def row_lanes(row):
    return pl.ds(pl.multiple_of(row * 128, 128), 128)


def local_image(field, weights, design, design_t, chunk):
    lanes = pl.ds(pl.multiple_of(chunk * 256, 256), 256)
    high, low = split(field[:, lanes])
    scaled = dot(design[...], jnp.concatenate([high, low], axis=0)) * weights[:, lanes].astype(F32)
    high, low = split(scaled)
    back = dot(design_t[...], high) + dot(design_t[...], low)
    lane = lax.broadcasted_iota(jnp.int32, (DP, 128), 1)
    parts = []
    for offset in range(2):
        row = 2 * chunk + offset
        here = field[:, row_lanes(row)]
        around = jnp.where(lane == 0, 0.0, pltpu.roll(here, 1, 1))
        around += jnp.where(lane == 127, 0.0, pltpu.roll(here, 127, 1))
        around += jnp.where(row > 0, field[:, row_lanes(jnp.maximum(row - 1, 0))], 0.0)
        around += jnp.where(row < 7, field[:, row_lanes(jnp.minimum(row + 1, 7))], 0.0)
        part = back[:, offset * 128 : offset * 128 + 128] + CENTRE * here - SMOOTHING_WEIGHT * around
        parts.append((row, part))
    return parts


def fold(values):
    return jnp.sum(values.reshape(DP // 8, 8, 128), axis=0)


def apply_local(with_before, with_image, *refs):
    field, weights, design, design_t = refs[:4]
    refs = refs[4:]
    before = None
    if with_before:
        before, refs = refs[0], refs[1:]
    image = None
    if with_image:
        image, refs = refs[0], refs[1:]
    moments = refs[0]

    def one_chunk(chunk, totals):
        square, cross, ahead = totals
        for row, part in local_image(field, weights, design, design_t, chunk):
            here = field[:, row_lanes(row)]
            square += fold(here * here)
            if with_before:
                cross += fold(here * before[:, row_lanes(row)])
            if with_image:
                image[:, row_lanes(row)] = part
            else:
                ahead += fold(here * part)
        return square, cross, ahead

    zero = jnp.zeros((8, 128), F32)
    totals = lax.fori_loop(0, 4, one_chunk, (zero, zero, zero), unroll=True)
    for index in range(3):
        moments[index] = totals[index]


def spread_columns(columns, pixels):
    row = lax.broadcasted_iota(jnp.int32, (16, 128), 0)
    lane = lax.broadcasted_iota(jnp.int32, (16, 128), 1)
    wanted = jnp.where(row < 8, row, row - 8) == pixels
    place = (wanted & (lane == jnp.where(row < 8, 0, 127))).astype(BF16)
    return lax.dot_general(columns, place, (((0,), (0,)), ((), ())), preferred_element_type=F32)


def keep(flag, values):
    return jnp.where(flag, values.astype(F32), 0.0)


def inside():
    row, col = lax.axis_index("rows"), lax.axis_index("ifg")
    return row > 0, row < lax.axis_size("rows") - 1, col > 0, col < lax.axis_size("ifg") - 1


def add_halo(image, above, below, left, right, field, *edges):
    flags = inside()
    sides = jnp.concatenate([keep(flags[2], left[8:16, :]), keep(flags[3], right[0:8, :])], axis=0).astype(BF16)
    for row in range(8):
        lanes = pl.ds(row * 128, 128)
        halo = spread_columns(sides, row)
        if row == 0:
            halo += keep(flags[0], above[...])
        if row == 7:
            halo += keep(flags[1], below[...])
        field[:, lanes] = image[:, lanes] - SMOOTHING_WEIGHT * halo
    write_edges(field, *edges)


def all_moments(field, above, left, zero, one, two, out):
    flags = inside()
    sides = jnp.concatenate([keep(flags[2], left[8:16, :]), jnp.zeros((8, DP), F32)], axis=0).astype(BF16)
    ahead = two[2]
    for row in range(8):
        halo = spread_columns(sides, row)
        if row == 0:
            halo += keep(flags[0], above[...])
        ahead -= (2.0 * SMOOTHING_WEIGHT) * fold(field[:, pl.ds(row * 128, 128)] * halo)
    rows = [zero[0], one[1], one[0], two[1], two[0], ahead]
    lane = lax.broadcasted_iota(jnp.int32, (1, 128), 1)
    total = jnp.zeros((1, 128), F32)
    for index, values in enumerate(rows):
        line = jnp.sum(values, axis=0, keepdims=True)
        total += jnp.where(lane == index, jnp.sum(line, axis=1, keepdims=True), 0.0)
    out[...] = total


def add_and_spread(one, two, *rest):
    out = rest[-1]
    out[...] = jnp.broadcast_to((one[...] + two[...])[None], out.shape)


def combine(parts, zero, one, two, out, field, sems):
    total = parts[0]
    for index in range(1, parts.shape[0]):
        total += parts[index]
    m0, m1, m2, m3, m4, m5 = (jnp.broadcast_to(total[:, i : i + 1], (1, 128)) for i in range(6))
    t00, t01, t11 = m1 + SHIFT * m0, m2 + SHIFT * m1, m3 + SHIFT * m2
    t12, t22 = m4 + SHIFT * m3, m5 + SHIFT * m4
    l10, l20 = t01 / t00, t11 / t00
    pivot = t11 - l10 * t01
    off = t12 - l20 * t01
    keep = pivot > 1e-6 * t11
    safe = jnp.where(keep, pivot, 1.0)
    l21 = jnp.where(keep, off / safe, 0.0)
    last = t22 - l20 * t11 - l21 * off
    keep_last = keep & (last > 1e-6 * t22)
    y1 = m1 - l10 * m0
    y2 = m2 - l20 * m0 - l21 * y1
    c2 = jnp.where(keep_last, y2 / jnp.where(keep_last, last, 1.0), 0.0)
    c1 = jnp.where(keep, y1 / safe, 0.0) - l21 * c2
    c0 = m0 / t00 - l10 * c1 - l20 * c2
    copies = []
    for part in range(4):
        count = min(80, DATES - part * 80)
        dates = pl.ds(part * 80, (count + 7) // 8 * 8)
        for row in range(8):
            lanes = pl.ds(row * 128, 128)
            value = c0 * zero[dates, lanes] + c1 * one[dates, lanes] + c2 * two[dates, lanes]
            field[pl.ds(part * 640 + row, count, stride=8), :] = value[:count, :]
        lines = pl.ds(part * 640, count * 8)
        copies.append(pltpu.make_async_copy(field.at[lines], out.at[lines], sems.at[part]))
        copies[-1].start()
    for copy in copies:
        copy.wait()


def per_device(phase, coherence, height, gap_mask, date_pairs):
    n_ifg, n_rows = lax.axis_size("ifg"), lax.axis_size("rows")
    me = lax.axis_index("ifg")

    def permute(values, axis, target):
        return lax.ppermute(values, axis, [(i, target(i)) for i in range(lax.axis_size(axis))])

    def forward(values, axis):
        return permute(values, axis, lambda i: (i + 1) % lax.axis_size(axis))

    def backward(values, axis):
        return permute(values, axis, lambda i: (i - 1) % lax.axis_size(axis))

    stacked = sds((8, 64, 1024), BF16)
    edge = sds((128, 1024), BF16)
    phase_t, coher_t, first, last = call(
        rows_first,
        (stacked, stacked, edge, edge),
        pltpu.with_memory_space_constraint(phase, pltpu.HBM),
        pltpu.with_memory_space_constraint(coherence, pltpu.HBM),
        specs=[pltpu.HBM] * 2,
        scratch=(
            pltpu.VMEM((64, 8, 1024), BF16),
            pltpu.VMEM((64, 8, 1024), BF16),
            pltpu.VMEM((2, 8, 128, 128), F32),
            pltpu.SemaphoreType.DMA((2, 4)),
        ),
        name="rows_first",
    )
    above, below = forward(last, "rows"), backward(first, "rows")
    mask = gap_mask.astype(F32)
    single, double = in_hbm((64, 1024), BF16), in_hbm((2, 64, 1024), BF16)
    pieces = [single, double, double, double, single]
    smooth, totals, *weight_parts = call(
        inner_rows,
        [in_hbm((8, 64, 1024), F32), sds((128, 128), F32)] + pieces,
        phase_t,
        coher_t,
        mask,
        height,
        out_specs=[pltpu.HBM, pltpu.VMEM] + [pltpu.HBM] * 5,
        scratch=(
            pltpu.VMEM((8, 64, 768), BF16),
            pltpu.VMEM((6, 64, 1024), F32),
            pltpu.SemaphoreType.DMA((4, 9)),
        ),
        name="inner_rows",
    )
    smooth, sums, *weight_parts = call(
        border_rows,
        [in_hbm((8, 64, 1024), F32), sds((1, 128), F32)] + pieces,
        phase_t,
        coher_t,
        above,
        below,
        mask,
        height,
        totals,
        smooth,
        *weight_parts,
        specs=[pltpu.VMEM] * 7 + [pltpu.HBM] * 6,
        out_specs=[pltpu.HBM, pltpu.VMEM] + [pltpu.HBM] * 5,
        scratch=(
            pltpu.VMEM((2, 8, 64, 128), BF16),
            pltpu.VMEM((2, 64, 1024), F32),
            pltpu.VMEM((128, 128), F32),
            pltpu.SemaphoreType.DMA((2, 9)),
        ),
        aliases={7: 0, **{8 + step: 2 + step for step in range(5)}},
        name="border_rows",
    )

    def offset(values, chips, core):
        return permute(values, "ifg", lambda i: other(i, chips, core))

    groups = [[8 * y + 2 * z + half for y in range(4) for z in range(4)] for half in range(2)]

    def gather_rows(values, *after):
        spread = call(
            add_and_spread,
            sds((n_rows // 2, 1, 128), F32),
            values,
            permute(values, "rows", lambda i: i ^ 1),
            *after,
            name="add_and_spread",
        )
        return lax.all_to_all(spread, "rows", 0, 0, tiled=True, axis_index_groups=groups)

    sums = gather_rows(sums)
    own, up, down, twice, pair = weight_parts
    twice, up, down = offset(twice, 2, 0), offset(up, 1, 0), offset(down, 3, 0)
    swap = offset(jnp.stack([twice[1], up[1], down[1], pair]), 0, 1)
    smooth = call(
        stage,
        sds((8, 64, 1024), F32),
        pltpu.with_memory_space_constraint(smooth, pltpu.HBM),
        specs=[pltpu.HBM],
        scratch=(pltpu.SemaphoreType.DMA((4,)),),
        name="stage",
    )
    slope_row, *corrected_parts = call(
        correction,
        [sds((1, 128), F32)] + [sds((64, 1024), BF16)] * 8,
        sums,
        smooth,
        height,
        scratch=(pltpu.VMEM((8, 64, 1024), BF16),),
        name="correction",
    )
    slope, corrected_parts[0] = lax.optimization_barrier((slope_row[0, :64], corrected_parts[0]))
    corrected_parts = corrected_parts[:1] + [
        offset(part, *where) for part, where in zip(corrected_parts[1:], OFFSETS[1:])
    ]
    sources = jnp.stack([other(me, 4 - chips, core) for chips, core in OFFSETS])
    pairs = date_pairs.reshape(n_ifg, -1, 2)[sources].reshape(-1, 2)
    dates = jnp.arange(DP, dtype=jnp.int32)
    design = ((dates[None] == pairs[:, 1:2]).astype(F32) - (dates[None] == pairs[:, 0:1]).astype(F32)).astype(BF16)
    design_t = design.T
    design = jnp.concatenate([design, design], axis=1)

    field = sds((DP, 1024), F32)
    edges = (sds((DP, 128), BF16), sds((16, DP), BF16), sds((DP, 128), BF16))
    moments = sds((3, 8, 128), F32)
    k0, weights, *sides = call(
        right_side,
        (field, sds((512, 1024), BF16)) + edges,
        own,
        up,
        down,
        twice,
        swap,
        *corrected_parts,
        design_t,
        name="right_side",
    )

    def halos(last, columns, first):
        return (
            forward(last, "rows"),
            backward(first, "rows"),
            forward(columns, "ifg"),
            backward(columns, "ifg"),
        )

    def local(with_before, with_image, name, *args):
        outs = ((field,) if with_image else ()) + (moments,)
        body = lambda *refs: apply_local(with_before, with_image, *refs)
        return call(body, outs, *args, name=name)

    def joined(image, around, count, name):
        return call(add_halo, (field,) + edges[:count], image, *around, name=name)

    around = halos(*sides)
    image, mom0 = local(False, True, "apply0", k0, weights, design, design_t)
    k1, *sides = joined(image, around, 3, "add_halo1")
    around = halos(*sides)
    image, mom1 = local(True, True, "apply1", k1, weights, design, design_t, k0)
    k2, last, columns = joined(image, around, 2, "add_halo2")
    above, left = forward(last, "rows"), forward(columns, "ifg")
    (mom2,) = local(True, False, "apply2", k2, weights, design, design_t, k1)
    part = call(
        all_moments,
        sds((1, 128), F32),
        k2,
        above,
        left,
        mom0,
        mom1,
        mom2,
        name="all_moments",
    )
    for step in (1, 2, 4):
        part = part + permute(part, "ifg", lambda i: i ^ step)
    parts = gather_rows(part, k0)
    displacement = call(
        combine,
        sds((DATES * 8, 128), F32),
        parts,
        k0,
        k1,
        k2,
        out_specs=[pltpu.HBM],
        scratch=(pltpu.VMEM((DATES * 8, 128), F32), pltpu.SemaphoreType.DMA((4,))),
        name="combine",
    )
    return displacement.reshape(DATES, 8, 128), slope


def solution(mesh):
    placed = (
        P("ifg", "rows", None),
        P("ifg", "rows", None),
        P("rows", None),
        P("ifg", "rows"),
        P(),
    )
    return jax.shard_map(
        per_device,
        mesh=mesh,
        in_specs=placed,
        out_specs=(P(None, "rows", "ifg"), P("ifg")),
        check_vma=False,
    )
```

```python
import jax
import jax.numpy as jnp
from jax import lax
from jax.experimental import pallas as pl
from jax.experimental.pallas import tpu as pltpu
from jax.sharding import PartitionSpec as P

DATES = 300
DP = 304
SHIFT = 4.0
SMOOTHING_WEIGHT = 0.5
RIDGE_WEIGHT = 0.05
CENTRE = 4.0 * SMOOTHING_WEIGHT + RIDGE_WEIGHT - SHIFT
F32 = jnp.float32
BF16 = jnp.bfloat16


def sds(shape, dtype):
    return jax.ShapeDtypeStruct(shape, dtype)


def in_hbm(shape, dtype):
    return pltpu.HBM(shape, dtype)


def call(body, outs, *args, specs=None, out_specs=None, scratch=(), aliases=None, name=None):
    flat = outs if isinstance(outs, (list, tuple)) else [outs]
    places = specs or [pltpu.VMEM] * len(args)
    out_places = [pl.BlockSpec(memory_space=place) for place in out_specs or [pltpu.VMEM] * len(flat)]
    return pl.pallas_call(
        body,
        out_shape=outs,
        in_specs=[pl.BlockSpec(memory_space=place) for place in places],
        out_specs=out_places if isinstance(outs, (list, tuple)) else out_places[0],
        scratch_shapes=list(scratch),
        input_output_aliases=aliases or {},
        compiler_params=pltpu.CompilerParams(vmem_limit_bytes=16 * 1024 * 1024),
        name=name,
    )(*args)


def dot(a, b):
    return jnp.dot(a, b, preferred_element_type=F32)


def split(values):
    high = values.astype(BF16)
    return high, (values - high.astype(F32)).astype(BF16)


def rows_first(phase, coher, phase_t, coher_t, first, last, phase_in, coher_in, wide, sems):
    pairs = ((phase, phase_in, phase_t), (coher, coher_in, coher_t))

    def fetch(part, block):
        ifgs, _ = block_of(block)
        return pltpu.make_async_copy(pairs[part][0].at[ifgs], pairs[part][1].at[ifgs], sems.at[part, block])

    for block in range(4):
        for part in range(2):
            fetch(part, block).start()

    def group(block, _):
        ifgs, _ = block_of(block)
        for part, (_, source, target) in enumerate(pairs):
            fetch(part, block).wait()
            for tile in range(8):
                lanes = pl.ds(tile * 128, 128)
                wide[part, tile] = source[ifgs, :, lanes].astype(F32).reshape(128, 128)
                for row in range(8):
                    target[row, ifgs, lanes] = wide[part, tile, pl.ds(row, 16, stride=8), :].astype(BF16)
        return 0

    lax.fori_loop(0, 4, group, 0)
    for part, target in enumerate((phase_t, coher_t)):
        first[pl.ds(part * 64, 64), :] = target[0]
        last[pl.ds(part * 64, 64), :] = target[7]


def shifted_sum(values, lane, last):
    left = jnp.where(lane == 0, 0.0, pltpu.roll(values, 1, 1))
    right = jnp.where(lane == last, 0.0, pltpu.roll(values, last, 1))
    return values + left + right


def fold_lanes(values):
    total = values[:, :128]
    for tile in range(1, 8):
        total += values[:, tile * 128 : tile * 128 + 128]
    return total


OFFSETS = ((0, 0), (0, 1), (2, 0), (2, 1), (1, 0), (1, 1), (3, 0), (3, 1))


def other(index, chips, core):
    return (((index >> 1) + chips) & 3) * 2 + ((index & 1) ^ core)


def owner(step):
    return other(lax.axis_index("ifg"), *OFFSETS[step])


def smooth_row(rows, lane, mask, terrain):
    denom = shifted_sum(rows[0][0] + rows[1][0] + rows[2][0], lane, 1023)
    numer = shifted_sum(rows[0][1] + rows[1][1] + rows[2][1], lane, 1023)
    top = fold_lanes(numer * terrain)
    low = fold_lanes(denom * (terrain * terrain))
    return numer / denom, (mask * (denom / 9.0)).astype(BF16), top, low


def load_row(phase_t, coher_t, row, ifgs):
    coher = coher_t[row, ifgs, :].astype(F32)
    return coher, coher * phase_t[row, ifgs, :].astype(F32)


def block_of(block):
    return pl.ds(pl.multiple_of(block * 16, 16), 16), pl.ds(pl.multiple_of(block * 16 + 64, 16), 16)


def inner_rows(phase_t, coher_t, mask, height, smooth_out, totals, *rest):
    outs, weights, smooth, sems = rest[:8], *rest[8:]
    lane = lax.broadcasted_iota(jnp.int32, (16, 1024), 1)

    def copies(block):
        ifgs, _ = block_of(block)
        return [
            pltpu.make_async_copy(
                weights.at[owner(step), ifgs], out.at[ifgs, pl.ds(128, 768)], sems.at[block, step]
            )
            for step, out in enumerate(outs)
        ] + [pltpu.make_async_copy(smooth.at[:, ifgs], smooth_out.at[pl.ds(1, 6), ifgs], sems.at[block, 8])]

    def group(block, _):
        ifgs, lows = block_of(block)
        masks = mask[ifgs, :]
        rows = [load_row(phase_t, coher_t, row, ifgs) for row in (0, 1)]
        top = jnp.zeros((16, 128), F32)
        low = jnp.zeros((16, 128), F32)
        for row in range(1, 7):
            rows.append(load_row(phase_t, coher_t, row + 1, ifgs))
            value, weight, more_top, more_low = smooth_row(
                rows, lane, masks[:, row : row + 1], height[pl.ds(row, 1), :]
            )
            rows = rows[1:]
            top += more_top
            low += more_low
            smooth[row - 1, ifgs, :] = value
            for tile in range(8):
                weights[tile, ifgs, pl.ds((row - 1) * 128, 128)] = weight[:, tile * 128 : tile * 128 + 128]
        totals[ifgs, :] = top
        totals[lows, :] = low
        for copy in copies(block):
            copy.start()
        return 0

    lax.fori_loop(0, 4, group, 0)
    for block in range(4):
        for copy in copies(block):
            copy.wait()


def border_rows(phase_t, coher_t, above, below, mask, height, totals, *rest):
    smooth_out, sums, outs = rest[9], rest[10], rest[11:19]
    weights, smooth, added, sems = rest[19:]
    lane = lax.broadcasted_iota(jnp.int32, (16, 1024), 1)
    my_row = lax.axis_index("rows")
    valid = (my_row > 0, my_row < lax.axis_size("rows") - 1)

    def group(block, _):
        ifgs, lows = block_of(block)
        masks = mask[ifgs, :]
        top = totals[ifgs, :]
        low = totals[lows, :]
        for side, (edge, row) in enumerate(((above, 0), (below, 7))):
            coher = jnp.where(valid[side], edge[lows, :].astype(F32), 0.0)
            rows = [(coher, coher * edge[ifgs, :].astype(F32))]
            rows += [load_row(phase_t, coher_t, near, ifgs) for near in (row, 1 if row == 0 else 6)]
            value, weight, more_top, more_low = smooth_row(
                rows, lane, masks[:, row : row + 1], height[pl.ds(row, 1), :]
            )
            top += more_top
            low += more_low
            smooth[side, ifgs, :] = value
            for tile in range(8):
                weights[side, tile, ifgs, :] = weight[:, tile * 128 : tile * 128 + 128]
        added[ifgs, :] = top
        added[lows, :] = low
        return 0

    lax.fori_loop(0, 4, group, 0)
    copies = []
    for side, row in ((0, 0), (1, 7)):
        copies.append(pltpu.make_async_copy(smooth.at[side], smooth_out.at[row], sems.at[side, 8]))
        for step, out in enumerate(outs):
            lanes = pl.ds(row * 128, 128)
            copies.append(
                pltpu.make_async_copy(weights.at[side, owner(step)], out.at[:, lanes], sems.at[side, step])
            )
    for copy in copies:
        copy.start()
    sums[...] = jnp.broadcast_to(jnp.sum(added[...].T, axis=0)[None, None, :], sums.shape)
    for copy in copies:
        copy.wait()


def stage(source, out, sems):
    copies = [
        pltpu.make_async_copy(source.at[pl.ds(part * 2, 2)], out.at[pl.ds(part * 2, 2)], sems.at[part])
        for part in range(4)
    ]
    for copy in copies:
        copy.start()
    for copy in copies:
        copy.wait()


def correction(sums, smooth, height, slope_row, *rest):
    outs, blocks = rest[:8], rest[8]
    total = sums[0]
    for index in range(1, sums.shape[0]):
        total += sums[index]
    slope_row[...] = total / pltpu.roll(total, 64, 1)
    column = jnp.broadcast_to(total, (128, 128)).T
    slope = column[:64, :] / column[64:, :]

    def one_tile(tile, _):
        lanes = pl.ds(pl.multiple_of(tile * 128, 128), 128)
        for row in range(8):
            value = smooth[row, :, lanes] - slope * height[pl.ds(row, 1), lanes]
            blocks[tile, :, pl.ds(row * 128, 128)] = value.astype(BF16)
        return 0

    lax.fori_loop(0, 8, one_tile, 0)
    for step, out in enumerate(outs):
        out[...] = blocks[owner(step)]


def column_selector():
    row = lax.broadcasted_iota(jnp.int32, (16, 1024), 0)
    pixel = lax.broadcasted_iota(jnp.int32, (16, 1024), 1)
    wanted = jnp.where(row < 8, row * 128, (row - 8) * 128 + 127)
    return (pixel == wanted).astype(BF16)


def write_edges(field, last, columns, first=None):
    if first is not None:
        first[...] = field[:, pl.ds(0, 128)].astype(BF16)
    last[...] = field[:, pl.ds(896, 128)].astype(BF16)
    picked = lax.dot_general(
        column_selector(), field[...].astype(BF16), (((1,), (1,)), ((), ())), preferred_element_type=F32
    )
    columns[...] = picked.astype(BF16)


def right_side(*refs):
    weight_parts, corrected_parts = refs[:8], refs[8:16]
    design_t, field, weights, *edges = refs[16:]
    for part in range(8):
        weights[pl.ds(part * 64, 64), :] = weight_parts[part][...]

    def one_chunk(chunk, _):
        lanes = pl.ds(pl.multiple_of(chunk * 256, 256), 256)
        scaled = jnp.concatenate(
            [
                weight_parts[part][:, lanes].astype(F32) * corrected_parts[part][:, lanes].astype(F32)
                for part in range(8)
            ],
            axis=0,
        )
        high, low = split(scaled)
        field[:, lanes] = dot(design_t[...], high) + dot(design_t[...], low)
        return 0

    lax.fori_loop(0, 4, one_chunk, 0)
    write_edges(field, *edges)


def row_lanes(row):
    return pl.ds(pl.multiple_of(row * 128, 128), 128)


def local_image(field, weights, design, design_t, chunk):
    lanes = pl.ds(pl.multiple_of(chunk * 256, 256), 256)
    high, low = split(field[:, lanes])
    scaled = dot(design[...], jnp.concatenate([high, low], axis=0)) * weights[:, lanes].astype(F32)
    high, low = split(scaled)
    back = dot(design_t[...], high) + dot(design_t[...], low)
    lane = lax.broadcasted_iota(jnp.int32, (DP, 128), 1)
    parts = []
    for offset in range(2):
        row = 2 * chunk + offset
        here = field[:, row_lanes(row)]
        around = jnp.where(lane == 0, 0.0, pltpu.roll(here, 1, 1))
        around += jnp.where(lane == 127, 0.0, pltpu.roll(here, 127, 1))
        around += jnp.where(row > 0, field[:, row_lanes(jnp.maximum(row - 1, 0))], 0.0)
        around += jnp.where(row < 7, field[:, row_lanes(jnp.minimum(row + 1, 7))], 0.0)
        part = back[:, offset * 128 : offset * 128 + 128] + CENTRE * here - SMOOTHING_WEIGHT * around
        parts.append((row, part))
    return parts


def fold(values):
    return jnp.sum(values.reshape(DP // 8, 8, 128), axis=0)


def apply_local(with_before, with_image, *refs):
    field, weights, design, design_t = refs[:4]
    refs = refs[4:]
    before = None
    if with_before:
        before, refs = refs[0], refs[1:]
    image = None
    if with_image:
        image, refs = refs[0], refs[1:]
    moments = refs[0]

    def one_chunk(chunk, totals):
        square, cross, ahead = totals
        for row, part in local_image(field, weights, design, design_t, chunk):
            here = field[:, row_lanes(row)]
            square += fold(here * here)
            if with_before:
                cross += fold(here * before[:, row_lanes(row)])
            if with_image:
                image[:, row_lanes(row)] = part
            else:
                ahead += fold(here * part)
        return square, cross, ahead

    zero = jnp.zeros((8, 128), F32)
    totals = lax.fori_loop(0, 4, one_chunk, (zero, zero, zero), unroll=True)
    for index in range(3):
        moments[index] = totals[index]


def spread_columns(columns, pixels):
    row = lax.broadcasted_iota(jnp.int32, (16, 128), 0)
    lane = lax.broadcasted_iota(jnp.int32, (16, 128), 1)
    wanted = jnp.where(row < 8, row, row - 8) == pixels
    place = (wanted & (lane == jnp.where(row < 8, 0, 127))).astype(BF16)
    return lax.dot_general(columns, place, (((0,), (0,)), ((), ())), preferred_element_type=F32)


def keep(flag, values):
    return jnp.where(flag, values.astype(F32), 0.0)


def inside():
    row, col = lax.axis_index("rows"), lax.axis_index("ifg")
    return row > 0, row < lax.axis_size("rows") - 1, col > 0, col < lax.axis_size("ifg") - 1


def add_halo(image, above, below, left, right, field, *edges):
    flags = inside()
    sides = jnp.concatenate([keep(flags[2], left[8:16, :]), keep(flags[3], right[0:8, :])], axis=0).astype(BF16)
    for row in range(8):
        lanes = pl.ds(row * 128, 128)
        halo = spread_columns(sides, row)
        if row == 0:
            halo += keep(flags[0], above[...])
        if row == 7:
            halo += keep(flags[1], below[...])
        field[:, lanes] = image[:, lanes] - SMOOTHING_WEIGHT * halo
    write_edges(field, *edges)


def all_moments(field, above, left, zero, one, two, out):
    flags = inside()
    sides = jnp.concatenate([keep(flags[2], left[8:16, :]), jnp.zeros((8, DP), F32)], axis=0).astype(BF16)
    ahead = two[2]
    for row in range(8):
        halo = spread_columns(sides, row)
        if row == 0:
            halo += keep(flags[0], above[...])
        ahead -= (2.0 * SMOOTHING_WEIGHT) * fold(field[:, pl.ds(row * 128, 128)] * halo)
    rows = [zero[0], one[1], one[0], two[1], two[0], ahead]
    lane = lax.broadcasted_iota(jnp.int32, (1, 128), 1)
    total = jnp.zeros((1, 128), F32)
    for index, values in enumerate(rows):
        line = jnp.sum(values, axis=0, keepdims=True)
        total += jnp.where(lane == index, jnp.sum(line, axis=1, keepdims=True), 0.0)
    out[...] = total


def add_and_spread(one, two, basis, out):
    out[...] = jnp.broadcast_to((one[...] + two[...])[None], out.shape)


def combine(parts, zero, one, two, out, field, sems):
    total = parts[0]
    for index in range(1, parts.shape[0]):
        total += parts[index]
    m0, m1, m2, m3, m4, m5 = (jnp.broadcast_to(total[:, i : i + 1], (1, 128)) for i in range(6))
    t00, t01, t11 = m1 + SHIFT * m0, m2 + SHIFT * m1, m3 + SHIFT * m2
    t12, t22 = m4 + SHIFT * m3, m5 + SHIFT * m4
    l10, l20 = t01 / t00, t11 / t00
    pivot = t11 - l10 * t01
    off = t12 - l20 * t01
    keep = pivot > 1e-6 * t11
    safe = jnp.where(keep, pivot, 1.0)
    l21 = jnp.where(keep, off / safe, 0.0)
    last = t22 - l20 * t11 - l21 * off
    keep_last = keep & (last > 1e-6 * t22)
    y1 = m1 - l10 * m0
    y2 = m2 - l20 * m0 - l21 * y1
    c2 = jnp.where(keep_last, y2 / jnp.where(keep_last, last, 1.0), 0.0)
    c1 = jnp.where(keep, y1 / safe, 0.0) - l21 * c2
    c0 = m0 / t00 - l10 * c1 - l20 * c2
    copies = []
    for part in range(4):
        count = min(80, DATES - part * 80)
        dates = pl.ds(part * 80, (count + 7) // 8 * 8)
        for row in range(8):
            lanes = pl.ds(row * 128, 128)
            value = c0 * zero[dates, lanes] + c1 * one[dates, lanes] + c2 * two[dates, lanes]
            field[pl.ds(part * 640 + row, count, stride=8), :] = value[:count, :]
        lines = pl.ds(part * 640, count * 8)
        copies.append(pltpu.make_async_copy(field.at[lines], out.at[lines], sems.at[part]))
        copies[-1].start()
    for copy in copies:
        copy.wait()


def per_device(phase, coherence, height, gap_mask, date_pairs):
    n_ifg, n_rows = lax.axis_size("ifg"), lax.axis_size("rows")
    me = lax.axis_index("ifg")

    def permute(values, axis, target):
        return lax.ppermute(values, axis, [(i, target(i)) for i in range(lax.axis_size(axis))])

    def forward(values, axis):
        return permute(values, axis, lambda i: (i + 1) % lax.axis_size(axis))

    def backward(values, axis):
        return permute(values, axis, lambda i: (i - 1) % lax.axis_size(axis))

    stacked = sds((8, 64, 1024), BF16)
    edge = sds((128, 1024), BF16)
    phase_t, coher_t, first, last = call(
        rows_first,
        (stacked, stacked, edge, edge),
        pltpu.with_memory_space_constraint(phase, pltpu.HBM),
        pltpu.with_memory_space_constraint(coherence, pltpu.HBM),
        specs=[pltpu.HBM] * 2,
        scratch=(
            pltpu.VMEM((64, 8, 1024), BF16),
            pltpu.VMEM((64, 8, 1024), BF16),
            pltpu.VMEM((2, 8, 128, 128), F32),
            pltpu.SemaphoreType.DMA((2, 4)),
        ),
        name="rows_first",
    )
    above, below = forward(last, "rows"), backward(first, "rows")
    mask = gap_mask.astype(F32)
    pieces = [in_hbm((64, 1024), BF16)] * 8
    smooth, totals, *weight_parts = call(
        inner_rows,
        [in_hbm((8, 64, 1024), F32), sds((128, 128), F32)] + pieces,
        phase_t,
        coher_t,
        mask,
        height,
        out_specs=[pltpu.HBM, pltpu.VMEM] + [pltpu.HBM] * 8,
        scratch=(
            pltpu.VMEM((8, 64, 768), BF16),
            pltpu.VMEM((6, 64, 1024), F32),
            pltpu.SemaphoreType.DMA((4, 9)),
        ),
        name="inner_rows",
    )
    smooth, sums, *weight_parts = call(
        border_rows,
        [in_hbm((8, 64, 1024), F32), sds((n_rows, 1, 128), F32)] + pieces,
        phase_t,
        coher_t,
        above,
        below,
        mask,
        height,
        totals,
        smooth,
        *weight_parts,
        specs=[pltpu.VMEM] * 7 + [pltpu.HBM] * 9,
        out_specs=[pltpu.HBM, pltpu.VMEM] + [pltpu.HBM] * 8,
        scratch=(
            pltpu.VMEM((2, 8, 64, 128), BF16),
            pltpu.VMEM((2, 64, 1024), F32),
            pltpu.VMEM((128, 128), F32),
            pltpu.SemaphoreType.DMA((2, 9)),
        ),
        aliases={7: 0, **{8 + step: 2 + step for step in range(8)}},
        name="border_rows",
    )

    def exchange(parts):
        return [parts[0]] + [
            permute(part, "ifg", lambda i: other(i, *offset))
            for part, offset in zip(parts[1:], OFFSETS[1:])
        ]

    weight_parts = exchange(weight_parts)
    sums, weight_parts[1] = lax.optimization_barrier((sums, weight_parts[1]))
    sums = lax.all_to_all(sums, "rows", 0, 0, tiled=True)
    sums, *weight_parts[2:5] = lax.optimization_barrier((sums, *weight_parts[2:5]))
    smooth = call(
        stage,
        sds((8, 64, 1024), F32),
        pltpu.with_memory_space_constraint(smooth, pltpu.HBM),
        specs=[pltpu.HBM],
        scratch=(pltpu.SemaphoreType.DMA((4,)),),
        name="stage",
    )
    slope_row, *corrected_parts = call(
        correction,
        [sds((1, 128), F32)] + [sds((64, 1024), BF16)] * 8,
        sums,
        smooth,
        height,
        scratch=(pltpu.VMEM((8, 64, 1024), BF16),),
        name="correction",
    )
    slope, corrected_parts[0] = lax.optimization_barrier((slope_row[0, :64], corrected_parts[0]))
    corrected_parts = exchange(corrected_parts)
    sources = jnp.stack([other(me, 4 - chips, core) for chips, core in OFFSETS])
    pairs = date_pairs.reshape(n_ifg, -1, 2)[sources].reshape(-1, 2)
    dates = jnp.arange(DP, dtype=jnp.int32)
    design = ((dates[None] == pairs[:, 1:2]).astype(F32) - (dates[None] == pairs[:, 0:1]).astype(F32)).astype(BF16)
    design_t = design.T
    design = jnp.concatenate([design, design], axis=1)

    field = sds((DP, 1024), F32)
    edges = (sds((DP, 128), BF16), sds((16, DP), BF16), sds((DP, 128), BF16))
    moments = sds((3, 8, 128), F32)
    k0, weights, *sides = call(
        right_side,
        (field, sds((512, 1024), BF16)) + edges,
        *weight_parts,
        *corrected_parts,
        design_t,
        name="right_side",
    )

    def halos(last, columns, first):
        return (
            forward(last, "rows"),
            backward(first, "rows"),
            forward(columns, "ifg"),
            backward(columns, "ifg"),
        )

    def local(with_before, with_image, name, *args):
        outs = ((field,) if with_image else ()) + (moments,)
        body = lambda *refs: apply_local(with_before, with_image, *refs)
        return call(body, outs, *args, name=name)

    def joined(image, around, count, name):
        return call(add_halo, (field,) + edges[:count], image, *around, name=name)

    around = halos(*sides)
    image, mom0 = local(False, True, "apply0", k0, weights, design, design_t)
    k1, *sides = joined(image, around, 3, "add_halo1")
    around = halos(*sides)
    image, mom1 = local(True, True, "apply1", k1, weights, design, design_t, k0)
    k2, last, columns = joined(image, around, 2, "add_halo2")
    above, left = forward(last, "rows"), forward(columns, "ifg")
    (mom2,) = local(True, False, "apply2", k2, weights, design, design_t, k1)
    part = call(
        all_moments,
        sds((1, 128), F32),
        k2,
        above,
        left,
        mom0,
        mom1,
        mom2,
        name="all_moments",
    )
    for step in (1, 2):
        part = part + permute(part, "ifg", lambda i: i ^ step)
    parts = call(
        add_and_spread,
        sds((n_rows, 1, 128), F32),
        part,
        permute(part, "ifg", lambda i: i ^ 4),
        k0,
        name="add_and_spread",
    )
    parts = lax.all_to_all(parts, "rows", 0, 0, tiled=True)
    displacement = call(
        combine,
        sds((DATES * 8, 128), F32),
        parts,
        k0,
        k1,
        k2,
        out_specs=[pltpu.HBM],
        scratch=(pltpu.VMEM((DATES * 8, 128), F32), pltpu.SemaphoreType.DMA((4,))),
        name="combine",
    )
    return displacement.reshape(DATES, 8, 128), slope


def solution(mesh):
    placed = (
        P("ifg", "rows", None),
        P("ifg", "rows", None),
        P("rows", None),
        P("ifg", "rows"),
        P(),
    )
    return jax.shard_map(
        per_device,
        mesh=mesh,
        in_specs=placed,
        out_specs=(P(None, "rows", "ifg"), P("ifg")),
        check_vma=False,
    )
```

```python
import jax
import jax.numpy as jnp
from jax import lax
from jax.experimental import pallas as pl
from jax.experimental.pallas import tpu as pltpu
from jax.sharding import PartitionSpec as P

DATES = 300
DP = 304
SHIFT = 4.0
SMOOTHING_WEIGHT = 0.5
RIDGE_WEIGHT = 0.05
CENTRE = 4.0 * SMOOTHING_WEIGHT + RIDGE_WEIGHT - SHIFT
F32 = jnp.float32
BF16 = jnp.bfloat16


def sds(shape, dtype):
    return jax.ShapeDtypeStruct(shape, dtype)


def in_hbm(shape, dtype):
    return pltpu.HBM(shape, dtype)


def call(body, outs, *args, specs=None, out_specs=None, scratch=(), aliases=None, name=None):
    flat = outs if isinstance(outs, (list, tuple)) else [outs]
    places = specs or [pltpu.VMEM] * len(args)
    out_places = [pl.BlockSpec(memory_space=place) for place in out_specs or [pltpu.VMEM] * len(flat)]
    return pl.pallas_call(
        body,
        out_shape=outs,
        in_specs=[pl.BlockSpec(memory_space=place) for place in places],
        out_specs=out_places if isinstance(outs, (list, tuple)) else out_places[0],
        scratch_shapes=list(scratch),
        input_output_aliases=aliases or {},
        compiler_params=pltpu.CompilerParams(vmem_limit_bytes=16 * 1024 * 1024),
        name=name,
    )(*args)


def dot(a, b):
    return jnp.dot(a, b, preferred_element_type=F32)


def split(values):
    high = values.astype(BF16)
    return high, (values - high.astype(F32)).astype(BF16)


def rows_first(phase, coher, phase_t, coher_t, first, last, phase_in, coher_in, wide, sems):
    pairs = ((phase, phase_in, phase_t), (coher, coher_in, coher_t))

    def fetch(part, block):
        ifgs, _ = block_of(block)
        return pltpu.make_async_copy(pairs[part][0].at[ifgs], pairs[part][1].at[ifgs], sems.at[part, block])

    for block in range(4):
        for part in range(2):
            fetch(part, block).start()

    def group(block, _):
        ifgs, _ = block_of(block)
        for part, (_, source, target) in enumerate(pairs):
            fetch(part, block).wait()
            for tile in range(8):
                lanes = pl.ds(tile * 128, 128)
                wide[part, tile] = source[ifgs, :, lanes].astype(F32).reshape(128, 128)
                for row in range(8):
                    target[row, ifgs, lanes] = wide[part, tile, pl.ds(row, 16, stride=8), :].astype(BF16)
        return 0

    lax.fori_loop(0, 4, group, 0)
    for part, target in enumerate((phase_t, coher_t)):
        first[pl.ds(part * 64, 64), :] = target[0]
        last[pl.ds(part * 64, 64), :] = target[7]


def shifted_sum(values, lane, last):
    left = jnp.where(lane == 0, 0.0, pltpu.roll(values, 1, 1))
    right = jnp.where(lane == last, 0.0, pltpu.roll(values, last, 1))
    return values + left + right


def regression_sums(phase_t, coher_t, height, above, below, out, box_one, box_two, totals):
    lane = lax.broadcasted_iota(jnp.int32, (8, 1024), 1)
    sub = lax.broadcasted_iota(jnp.int32, (8, 1024), 0)
    my_row = lax.axis_index("rows")
    here = height[...]
    upper = jnp.where(my_row > 0, above[...], 0.0)
    lower = jnp.where(my_row < lax.axis_size("rows") - 1, below[...], 0.0)
    up = jnp.where(sub == 0, upper, pltpu.roll(here, 1, 0))
    down = jnp.where(sub == 7, lower, pltpu.roll(here, 7, 0))
    box_one[...] = shifted_sum(here + up + down, lane, 1023)
    box_two[...] = shifted_sum(here * here + up * up + down * down, lane, 1023)

    def group(block, _):
        ifgs, lows = block_of(block)
        top = jnp.zeros((16, 128), F32)
        low = jnp.zeros((16, 128), F32)
        for row in range(8):
            for tile in range(8):
                lanes = pl.ds(tile * 128, 128)
                coher = coher_t[row, ifgs, lanes].astype(F32)
                phase = phase_t[row, ifgs, lanes].astype(F32)
                top += coher * phase * box_one[pl.ds(row, 1), lanes]
                low += coher * box_two[pl.ds(row, 1), lanes]
        totals[ifgs, :] = top
        totals[lows, :] = low
        return 0

    lax.fori_loop(0, 4, group, 0)
    out[...] = jnp.broadcast_to(jnp.sum(totals[...].T, axis=0)[None, None, :], out.shape)


def add_parts(parts):
    total = parts[0]
    for index in range(1, parts.shape[0]):
        total += parts[index]
    return total


def sum_and_spread(parts, out):
    out[...] = jnp.broadcast_to(add_parts(parts)[None], out.shape)


OFFSETS = ((0, 0), (0, 1), (2, 0), (2, 1), (1, 0), (1, 1), (3, 0), (3, 1))


def other(index, chips, core):
    return (((index >> 1) + chips) & 3) * 2 + ((index & 1) ^ core)


def owner(step):
    return other(lax.axis_index("ifg"), *OFFSETS[step])


def smooth_row(rows, lane, mask):
    denom = shifted_sum(rows[0][0] + rows[1][0] + rows[2][0], lane, 1023)
    numer = shifted_sum(rows[0][1] + rows[1][1] + rows[2][1], lane, 1023)
    return numer / denom, (mask * (denom / 9.0)).astype(BF16)


def load_row(phase_t, coher_t, row, ifgs):
    coher = coher_t[row, ifgs, :].astype(F32)
    return coher, coher * phase_t[row, ifgs, :].astype(F32)


def block_of(block):
    return pl.ds(pl.multiple_of(block * 16, 16), 16), pl.ds(pl.multiple_of(block * 16 + 64, 16), 16)


def inner_rows(phase_t, coher_t, mask, smooth_out, *rest):
    outs, weights, smooth, sems = rest[:8], *rest[8:]
    lane = lax.broadcasted_iota(jnp.int32, (16, 1024), 1)

    def copies(block):
        ifgs, _ = block_of(block)
        return [
            pltpu.make_async_copy(
                weights.at[owner(step), ifgs], out.at[ifgs, pl.ds(128, 768)], sems.at[block, step]
            )
            for step, out in enumerate(outs)
        ] + [pltpu.make_async_copy(smooth.at[:, ifgs], smooth_out.at[pl.ds(1, 6), ifgs], sems.at[block, 8])]

    def group(block, _):
        ifgs, _ = block_of(block)
        masks = mask[ifgs, :]
        rows = [load_row(phase_t, coher_t, row, ifgs) for row in (0, 1)]
        for row in range(1, 7):
            rows.append(load_row(phase_t, coher_t, row + 1, ifgs))
            value, weight = smooth_row(rows, lane, masks[:, row : row + 1])
            rows = rows[1:]
            smooth[row - 1, ifgs, :] = value
            for tile in range(8):
                weights[tile, ifgs, pl.ds((row - 1) * 128, 128)] = weight[:, tile * 128 : tile * 128 + 128]
        for copy in copies(block):
            copy.start()
        return 0

    lax.fori_loop(0, 4, group, 0)
    for block in range(4):
        for copy in copies(block):
            copy.wait()


def border_rows(phase_t, coher_t, above, below, mask, *rest):
    smooth_out, outs = rest[9], rest[10:18]
    weights, smooth, sems = rest[18:]
    lane = lax.broadcasted_iota(jnp.int32, (16, 1024), 1)
    my_row = lax.axis_index("rows")
    valid = (my_row > 0, my_row < lax.axis_size("rows") - 1)

    def group(block, _):
        ifgs, lows = block_of(block)
        masks = mask[ifgs, :]
        for side, (edge, row) in enumerate(((above, 0), (below, 7))):
            coher = jnp.where(valid[side], edge[lows, :].astype(F32), 0.0)
            rows = [(coher, coher * edge[ifgs, :].astype(F32))]
            rows += [load_row(phase_t, coher_t, near, ifgs) for near in (row, 1 if row == 0 else 6)]
            value, weight = smooth_row(rows, lane, masks[:, row : row + 1])
            smooth[side, ifgs, :] = value
            for tile in range(8):
                weights[side, tile, ifgs, :] = weight[:, tile * 128 : tile * 128 + 128]
        return 0

    lax.fori_loop(0, 4, group, 0)
    copies = []
    for side, row in ((0, 0), (1, 7)):
        copies.append(pltpu.make_async_copy(smooth.at[side], smooth_out.at[row], sems.at[side, 8]))
        for step, out in enumerate(outs):
            lanes = pl.ds(row * 128, 128)
            copies.append(
                pltpu.make_async_copy(weights.at[side, owner(step)], out.at[:, lanes], sems.at[side, step])
            )
    for copy in copies:
        copy.start()
    for copy in copies:
        copy.wait()


def stage(source, out, sems):
    copies = [
        pltpu.make_async_copy(source.at[pl.ds(part * 2, 2)], out.at[pl.ds(part * 2, 2)], sems.at[part])
        for part in range(4)
    ]
    for copy in copies:
        copy.start()
    for copy in copies:
        copy.wait()


def correction(sums, smooth, height, slope_row, *rest):
    outs, blocks = rest[:8], rest[8]
    total = add_parts(sums)
    slope_row[...] = total / pltpu.roll(total, 64, 1)
    column = jnp.broadcast_to(total, (128, 128)).T
    slope = column[:64, :] / column[64:, :]

    def one_tile(tile, _):
        lanes = pl.ds(pl.multiple_of(tile * 128, 128), 128)
        for row in range(8):
            value = smooth[row, :, lanes] - slope * height[pl.ds(row, 1), lanes]
            blocks[tile, :, pl.ds(row * 128, 128)] = value.astype(BF16)
        return 0

    lax.fori_loop(0, 8, one_tile, 0)
    for step, out in enumerate(outs):
        out[...] = blocks[owner(step)]


def column_selector():
    row = lax.broadcasted_iota(jnp.int32, (16, 1024), 0)
    pixel = lax.broadcasted_iota(jnp.int32, (16, 1024), 1)
    wanted = jnp.where(row < 8, row * 128, (row - 8) * 128 + 127)
    return (pixel == wanted).astype(BF16)


def write_edges(field, last, columns, first=None):
    if first is not None:
        first[...] = field[:, pl.ds(0, 128)].astype(BF16)
    last[...] = field[:, pl.ds(896, 128)].astype(BF16)
    picked = lax.dot_general(
        column_selector(), field[...].astype(BF16), (((1,), (1,)), ((), ())), preferred_element_type=F32
    )
    columns[...] = picked.astype(BF16)


def right_side(*refs):
    weight_parts, corrected_parts = refs[:8], refs[8:16]
    design_t, field, weights, *edges = refs[16:]
    for part in range(8):
        weights[pl.ds(part * 64, 64), :] = weight_parts[part][...]

    def one_chunk(chunk, _):
        lanes = pl.ds(pl.multiple_of(chunk * 256, 256), 256)
        scaled = jnp.concatenate(
            [
                weight_parts[part][:, lanes].astype(F32) * corrected_parts[part][:, lanes].astype(F32)
                for part in range(8)
            ],
            axis=0,
        )
        high, low = split(scaled)
        field[:, lanes] = dot(design_t[...], high) + dot(design_t[...], low)
        return 0

    lax.fori_loop(0, 4, one_chunk, 0)
    write_edges(field, *edges)


def row_lanes(row):
    return pl.ds(pl.multiple_of(row * 128, 128), 128)


def local_image(field, weights, design, design_t, chunk):
    lanes = pl.ds(pl.multiple_of(chunk * 256, 256), 256)
    high, low = split(field[:, lanes])
    scaled = dot(design[...], jnp.concatenate([high, low], axis=0)) * weights[:, lanes].astype(F32)
    high, low = split(scaled)
    back = dot(design_t[...], high) + dot(design_t[...], low)
    lane = lax.broadcasted_iota(jnp.int32, (DP, 128), 1)
    parts = []
    for offset in range(2):
        row = 2 * chunk + offset
        here = field[:, row_lanes(row)]
        around = jnp.where(lane == 0, 0.0, pltpu.roll(here, 1, 1))
        around += jnp.where(lane == 127, 0.0, pltpu.roll(here, 127, 1))
        around += jnp.where(row > 0, field[:, row_lanes(jnp.maximum(row - 1, 0))], 0.0)
        around += jnp.where(row < 7, field[:, row_lanes(jnp.minimum(row + 1, 7))], 0.0)
        part = back[:, offset * 128 : offset * 128 + 128] + CENTRE * here - SMOOTHING_WEIGHT * around
        parts.append((row, part))
    return parts


def fold(values):
    return jnp.sum(values.reshape(DP // 8, 8, 128), axis=0)


def apply_local(with_before, with_image, *refs):
    field, weights, design, design_t = refs[:4]
    refs = refs[4:]
    before = None
    if with_before:
        before, refs = refs[0], refs[1:]
    image = None
    if with_image:
        image, refs = refs[0], refs[1:]
    moments = refs[0]

    def one_chunk(chunk, totals):
        square, cross, ahead = totals
        for row, part in local_image(field, weights, design, design_t, chunk):
            here = field[:, row_lanes(row)]
            square += fold(here * here)
            if with_before:
                cross += fold(here * before[:, row_lanes(row)])
            if with_image:
                image[:, row_lanes(row)] = part
            else:
                ahead += fold(here * part)
        return square, cross, ahead

    zero = jnp.zeros((8, 128), F32)
    totals = lax.fori_loop(0, 4, one_chunk, (zero, zero, zero), unroll=True)
    for index in range(3):
        moments[index] = totals[index]


def spread_columns(columns, pixels):
    row = lax.broadcasted_iota(jnp.int32, (16, 128), 0)
    lane = lax.broadcasted_iota(jnp.int32, (16, 128), 1)
    wanted = jnp.where(row < 8, row, row - 8) == pixels
    place = (wanted & (lane == jnp.where(row < 8, 0, 127))).astype(BF16)
    return lax.dot_general(columns, place, (((0,), (0,)), ((), ())), preferred_element_type=F32)


def keep(flag, values):
    return jnp.where(flag, values.astype(F32), 0.0)


def inside():
    row, col = lax.axis_index("rows"), lax.axis_index("ifg")
    return row > 0, row < lax.axis_size("rows") - 1, col > 0, col < lax.axis_size("ifg") - 1


def add_halo(image, above, below, left, right, field, *edges):
    flags = inside()
    sides = jnp.concatenate([keep(flags[2], left[8:16, :]), keep(flags[3], right[0:8, :])], axis=0).astype(BF16)
    for row in range(8):
        lanes = pl.ds(row * 128, 128)
        halo = spread_columns(sides, row)
        if row == 0:
            halo += keep(flags[0], above[...])
        if row == 7:
            halo += keep(flags[1], below[...])
        field[:, lanes] = image[:, lanes] - SMOOTHING_WEIGHT * halo
    write_edges(field, *edges)


def all_moments(field, above, left, zero, one, two, out):
    flags = inside()
    sides = jnp.concatenate([keep(flags[2], left[8:16, :]), jnp.zeros((8, DP), F32)], axis=0).astype(BF16)
    ahead = two[2]
    for row in range(8):
        halo = spread_columns(sides, row)
        if row == 0:
            halo += keep(flags[0], above[...])
        ahead -= (2.0 * SMOOTHING_WEIGHT) * fold(field[:, pl.ds(row * 128, 128)] * halo)
    rows = [zero[0], one[1], one[0], two[1], two[0], ahead]
    lane = lax.broadcasted_iota(jnp.int32, (1, 128), 1)
    total = jnp.zeros((1, 128), F32)
    for index, values in enumerate(rows):
        line = jnp.sum(values, axis=0, keepdims=True)
        total += jnp.where(lane == index, jnp.sum(line, axis=1, keepdims=True), 0.0)
    out[...] = total


def add_and_spread(one, two, basis, out):
    out[...] = jnp.broadcast_to((one[...] + two[...])[None], out.shape)


def combine(parts, zero, one, two, out, field, sems):
    total = add_parts(parts)
    m0, m1, m2, m3, m4, m5 = (jnp.broadcast_to(total[:, i : i + 1], (1, 128)) for i in range(6))
    t00, t01, t11 = m1 + SHIFT * m0, m2 + SHIFT * m1, m3 + SHIFT * m2
    t12, t22 = m4 + SHIFT * m3, m5 + SHIFT * m4
    l10, l20 = t01 / t00, t11 / t00
    pivot = t11 - l10 * t01
    off = t12 - l20 * t01
    keep = pivot > 1e-6 * t11
    safe = jnp.where(keep, pivot, 1.0)
    l21 = jnp.where(keep, off / safe, 0.0)
    last = t22 - l20 * t11 - l21 * off
    keep_last = keep & (last > 1e-6 * t22)
    y1 = m1 - l10 * m0
    y2 = m2 - l20 * m0 - l21 * y1
    c2 = jnp.where(keep_last, y2 / jnp.where(keep_last, last, 1.0), 0.0)
    c1 = jnp.where(keep, y1 / safe, 0.0) - l21 * c2
    c0 = m0 / t00 - l10 * c1 - l20 * c2
    copies = []
    for part in range(4):
        count = min(80, DATES - part * 80)
        dates = pl.ds(part * 80, (count + 7) // 8 * 8)
        for row in range(8):
            lanes = pl.ds(row * 128, 128)
            value = c0 * zero[dates, lanes] + c1 * one[dates, lanes] + c2 * two[dates, lanes]
            field[pl.ds(part * 640 + row, count, stride=8), :] = value[:count, :]
        lines = pl.ds(part * 640, count * 8)
        copies.append(pltpu.make_async_copy(field.at[lines], out.at[lines], sems.at[part]))
        copies[-1].start()
    for copy in copies:
        copy.wait()


def per_device(phase, coherence, height, gap_mask, date_pairs):
    n_ifg, n_rows = lax.axis_size("ifg"), lax.axis_size("rows")
    me = lax.axis_index("ifg")

    def permute(values, axis, target):
        return lax.ppermute(values, axis, [(i, target(i)) for i in range(lax.axis_size(axis))])

    def forward(values, axis):
        return permute(values, axis, lambda i: (i + 1) % lax.axis_size(axis))

    def backward(values, axis):
        return permute(values, axis, lambda i: (i - 1) % lax.axis_size(axis))

    height_above, height_below = forward(height[7:8], "rows"), backward(height[0:1], "rows")
    stacked = sds((8, 64, 1024), BF16)
    edge = sds((128, 1024), BF16)
    phase_t, coher_t, first, last = call(
        rows_first,
        (stacked, stacked, edge, edge),
        pltpu.with_memory_space_constraint(phase, pltpu.HBM),
        pltpu.with_memory_space_constraint(coherence, pltpu.HBM),
        specs=[pltpu.HBM] * 2,
        scratch=(
            pltpu.VMEM((64, 8, 1024), BF16),
            pltpu.VMEM((64, 8, 1024), BF16),
            pltpu.VMEM((2, 8, 128, 128), F32),
            pltpu.SemaphoreType.DMA((2, 4)),
        ),
        name="rows_first",
    )
    above, below = forward(last, "rows"), backward(first, "rows")
    mask = gap_mask.astype(F32)
    sums = call(
        regression_sums,
        sds((8, 1, 128), F32),
        phase_t,
        coher_t,
        height,
        height_above,
        height_below,
        scratch=(pltpu.VMEM((8, 1024), F32), pltpu.VMEM((8, 1024), F32), pltpu.VMEM((128, 128), F32)),
        name="regression_sums",
    )
    near = [[8 * y + z for z in range(8)] for y in range(4)]
    far = [[8 * y + z for y in range(4)] for z in range(8)]
    sums = lax.all_to_all(sums, "rows", 0, 0, tiled=True, axis_index_groups=near)
    sums = call(sum_and_spread, sds((4, 1, 128), F32), sums, name="sum_and_spread")
    pieces = [in_hbm((64, 1024), BF16)] * 8
    smooth, *weight_parts = call(
        inner_rows,
        [in_hbm((8, 64, 1024), F32)] + pieces,
        phase_t,
        coher_t,
        mask,
        out_specs=[pltpu.HBM] * 9,
        scratch=(
            pltpu.VMEM((8, 64, 768), BF16),
            pltpu.VMEM((6, 64, 1024), F32),
            pltpu.SemaphoreType.DMA((4, 9)),
        ),
        name="inner_rows",
    )
    smooth, *weight_parts = call(
        border_rows,
        [in_hbm((8, 64, 1024), F32)] + pieces,
        phase_t,
        coher_t,
        above,
        below,
        mask,
        smooth,
        *weight_parts,
        specs=[pltpu.VMEM] * 5 + [pltpu.HBM] * 9,
        out_specs=[pltpu.HBM] * 9,
        scratch=(
            pltpu.VMEM((2, 8, 64, 128), BF16),
            pltpu.VMEM((2, 64, 1024), F32),
            pltpu.SemaphoreType.DMA((2, 9)),
        ),
        aliases={5 + step: step for step in range(9)},
        name="border_rows",
    )

    def exchange(parts):
        return [parts[0]] + [
            permute(part, "ifg", lambda i: other(i, *offset))
            for part, offset in zip(parts[1:], OFFSETS[1:])
        ]

    weight_parts = exchange(weight_parts)
    sums, weight_parts[1] = lax.optimization_barrier((sums, weight_parts[1]))
    sums = lax.all_to_all(sums, "rows", 0, 0, tiled=True, axis_index_groups=far)
    sums, *weight_parts[2:5] = lax.optimization_barrier((sums, *weight_parts[2:5]))
    smooth = call(
        stage,
        sds((8, 64, 1024), F32),
        pltpu.with_memory_space_constraint(smooth, pltpu.HBM),
        specs=[pltpu.HBM],
        scratch=(pltpu.SemaphoreType.DMA((4,)),),
        name="stage",
    )
    slope_row, *corrected_parts = call(
        correction,
        [sds((1, 128), F32)] + [sds((64, 1024), BF16)] * 8,
        sums,
        smooth,
        height,
        scratch=(pltpu.VMEM((8, 64, 1024), BF16),),
        name="correction",
    )
    slope, corrected_parts[0] = lax.optimization_barrier((slope_row[0, :64], corrected_parts[0]))
    corrected_parts = exchange(corrected_parts)
    sources = jnp.stack([other(me, 4 - chips, core) for chips, core in OFFSETS])
    pairs = date_pairs.reshape(n_ifg, -1, 2)[sources].reshape(-1, 2)
    dates = jnp.arange(DP, dtype=jnp.int32)
    design = ((dates[None] == pairs[:, 1:2]).astype(F32) - (dates[None] == pairs[:, 0:1]).astype(F32)).astype(BF16)
    design_t = design.T
    design = jnp.concatenate([design, design], axis=1)

    field = sds((DP, 1024), F32)
    edges = (sds((DP, 128), BF16), sds((16, DP), BF16), sds((DP, 128), BF16))
    moments = sds((3, 8, 128), F32)
    k0, weights, *sides = call(
        right_side,
        (field, sds((512, 1024), BF16)) + edges,
        *weight_parts,
        *corrected_parts,
        design_t,
        name="right_side",
    )

    def halos(last, columns, first):
        return (
            forward(last, "rows"),
            backward(first, "rows"),
            forward(columns, "ifg"),
            backward(columns, "ifg"),
        )

    def local(with_before, with_image, name, *args):
        outs = ((field,) if with_image else ()) + (moments,)
        body = lambda *refs: apply_local(with_before, with_image, *refs)
        return call(body, outs, *args, name=name)

    def joined(image, around, count, name):
        return call(add_halo, (field,) + edges[:count], image, *around, name=name)

    around = halos(*sides)
    image, mom0 = local(False, True, "apply0", k0, weights, design, design_t)
    k1, *sides = joined(image, around, 3, "add_halo1")
    around = halos(*sides)
    image, mom1 = local(True, True, "apply1", k1, weights, design, design_t, k0)
    k2, last, columns = joined(image, around, 2, "add_halo2")
    above, left = forward(last, "rows"), forward(columns, "ifg")
    (mom2,) = local(True, False, "apply2", k2, weights, design, design_t, k1)
    part = call(
        all_moments,
        sds((1, 128), F32),
        k2,
        above,
        left,
        mom0,
        mom1,
        mom2,
        name="all_moments",
    )
    for step in (1, 2):
        part = part + permute(part, "ifg", lambda i: i ^ step)
    parts = call(
        add_and_spread,
        sds((n_rows, 1, 128), F32),
        part,
        permute(part, "ifg", lambda i: i ^ 4),
        k0,
        name="add_and_spread",
    )
    parts = lax.all_to_all(parts, "rows", 0, 0, tiled=True)
    displacement = call(
        combine,
        sds((DATES * 8, 128), F32),
        parts,
        k0,
        k1,
        k2,
        out_specs=[pltpu.HBM],
        scratch=(pltpu.VMEM((DATES * 8, 128), F32), pltpu.SemaphoreType.DMA((4,))),
        name="combine",
    )
    return displacement.reshape(DATES, 8, 128), slope


def solution(mesh):
    placed = (
        P("ifg", "rows", None),
        P("ifg", "rows", None),
        P("rows", None),
        P("ifg", "rows"),
        P(),
    )
    return jax.shard_map(
        per_device,
        mesh=mesh,
        in_specs=placed,
        out_specs=(P(None, "rows", "ifg"), P("ifg")),
        check_vma=False,
    )
```

```python
import jax
import jax.numpy as jnp
from jax import lax
from jax.experimental import pallas as pl
from jax.experimental.pallas import tpu as pltpu
from jax.sharding import PartitionSpec as P

DATES = 300
DP = 304
SHIFT = 4.0
SMOOTHING_WEIGHT = 0.5
RIDGE_WEIGHT = 0.05
CENTRE = 4.0 * SMOOTHING_WEIGHT + RIDGE_WEIGHT - SHIFT
F32 = jnp.float32
BF16 = jnp.bfloat16


def sds(shape, dtype):
    return jax.ShapeDtypeStruct(shape, dtype)


def in_hbm(shape, dtype):
    return pltpu.HBM(shape, dtype)


def call(body, outs, *args, specs=None, out_specs=None, scratch=(), aliases=None, name=None):
    flat = outs if isinstance(outs, (list, tuple)) else [outs]
    places = specs or [pltpu.VMEM] * len(args)
    out_places = [pl.BlockSpec(memory_space=place) for place in out_specs or [pltpu.VMEM] * len(flat)]
    return pl.pallas_call(
        body,
        out_shape=outs,
        in_specs=[pl.BlockSpec(memory_space=place) for place in places],
        out_specs=out_places if isinstance(outs, (list, tuple)) else out_places[0],
        scratch_shapes=list(scratch),
        input_output_aliases=aliases or {},
        compiler_params=pltpu.CompilerParams(vmem_limit_bytes=16 * 1024 * 1024),
        name=name,
    )(*args)


def dot(a, b):
    return jnp.dot(a, b, preferred_element_type=F32)


def split(values):
    high = values.astype(BF16)
    return high, (values - high.astype(F32)).astype(BF16)


def rows_first(phase, coher, phase_t, coher_t, first, last, phase_in, coher_in, wide, sems):
    pairs = ((phase, phase_in, phase_t), (coher, coher_in, coher_t))

    def fetch(part, block):
        ifgs, _ = block_of(block)
        return pltpu.make_async_copy(pairs[part][0].at[ifgs], pairs[part][1].at[ifgs], sems.at[part, block])

    for block in range(4):
        for part in range(2):
            fetch(part, block).start()

    def group(block, _):
        ifgs, _ = block_of(block)
        for part, (_, source, target) in enumerate(pairs):
            fetch(part, block).wait()
            for tile in range(8):
                lanes = pl.ds(tile * 128, 128)
                wide[part, tile] = source[ifgs, :, lanes].astype(F32).reshape(128, 128)
                for row in range(8):
                    target[row, ifgs, lanes] = wide[part, tile, pl.ds(row, 16, stride=8), :].astype(BF16)
        return 0

    lax.fori_loop(0, 4, group, 0)
    for part, target in enumerate((phase_t, coher_t)):
        first[pl.ds(part * 64, 64), :] = target[0]
        last[pl.ds(part * 64, 64), :] = target[7]


def shifted_sum(values, lane, last):
    left = jnp.where(lane == 0, 0.0, pltpu.roll(values, 1, 1))
    right = jnp.where(lane == last, 0.0, pltpu.roll(values, last, 1))
    return values + left + right


def fold_lanes(values):
    total = values[:, :128]
    for tile in range(1, 8):
        total += values[:, tile * 128 : tile * 128 + 128]
    return total


OFFSETS = ((0, 0), (0, 1), (2, 0), (1, 0), (3, 0), (2, 1), (1, 1), (3, 1))


def other(index, chips, core):
    return (((index >> 1) + chips) & 3) * 2 + ((index & 1) ^ core)


def owner(step):
    return other(lax.axis_index("ifg"), *OFFSETS[step])


def smooth_row(rows, lane, mask, terrain):
    denom = shifted_sum(rows[0][0] + rows[1][0] + rows[2][0], lane, 1023)
    numer = shifted_sum(rows[0][1] + rows[1][1] + rows[2][1], lane, 1023)
    top = fold_lanes(numer * terrain)
    low = fold_lanes(denom * (terrain * terrain))
    return numer / denom, (mask * (denom / 9.0)).astype(BF16), top, low


def load_row(phase_t, coher_t, row, ifgs):
    coher = coher_t[row, ifgs, :].astype(F32)
    return coher, coher * phase_t[row, ifgs, :].astype(F32)


def block_of(block):
    return pl.ds(pl.multiple_of(block * 16, 16), 16), pl.ds(pl.multiple_of(block * 16 + 64, 16), 16)


def inner_rows(phase_t, coher_t, mask, height, smooth_out, totals, *rest):
    outs, weights, smooth, sems = rest[:8], *rest[8:]
    lane = lax.broadcasted_iota(jnp.int32, (16, 1024), 1)

    def copies(block):
        ifgs, _ = block_of(block)
        return [
            pltpu.make_async_copy(
                weights.at[owner(step), ifgs], out.at[ifgs, pl.ds(128, 768)], sems.at[block, step]
            )
            for step, out in enumerate(outs)
        ] + [pltpu.make_async_copy(smooth.at[:, ifgs], smooth_out.at[pl.ds(1, 6), ifgs], sems.at[block, 8])]

    def group(block, _):
        ifgs, lows = block_of(block)
        masks = mask[ifgs, :]
        rows = [load_row(phase_t, coher_t, row, ifgs) for row in (0, 1)]
        top = jnp.zeros((16, 128), F32)
        low = jnp.zeros((16, 128), F32)
        for row in range(1, 7):
            rows.append(load_row(phase_t, coher_t, row + 1, ifgs))
            value, weight, more_top, more_low = smooth_row(
                rows, lane, masks[:, row : row + 1], height[pl.ds(row, 1), :]
            )
            rows = rows[1:]
            top += more_top
            low += more_low
            smooth[row - 1, ifgs, :] = value
            for tile in range(8):
                weights[tile, ifgs, pl.ds((row - 1) * 128, 128)] = weight[:, tile * 128 : tile * 128 + 128]
        totals[ifgs, :] = top
        totals[lows, :] = low
        for copy in copies(block):
            copy.start()
        return 0

    lax.fori_loop(0, 4, group, 0)
    for block in range(4):
        for copy in copies(block):
            copy.wait()


def border_rows(phase_t, coher_t, above, below, mask, height, totals, *rest):
    smooth_out, sums, outs = rest[9], rest[10], rest[11:19]
    weights, smooth, added, sems = rest[19:]
    lane = lax.broadcasted_iota(jnp.int32, (16, 1024), 1)
    my_row = lax.axis_index("rows")
    valid = (my_row > 0, my_row < lax.axis_size("rows") - 1)

    def group(block, _):
        ifgs, lows = block_of(block)
        masks = mask[ifgs, :]
        top = totals[ifgs, :]
        low = totals[lows, :]
        for side, (edge, row) in enumerate(((above, 0), (below, 7))):
            coher = jnp.where(valid[side], edge[lows, :].astype(F32), 0.0)
            rows = [(coher, coher * edge[ifgs, :].astype(F32))]
            rows += [load_row(phase_t, coher_t, near, ifgs) for near in (row, 1 if row == 0 else 6)]
            value, weight, more_top, more_low = smooth_row(
                rows, lane, masks[:, row : row + 1], height[pl.ds(row, 1), :]
            )
            top += more_top
            low += more_low
            smooth[side, ifgs, :] = value
            for tile in range(8):
                weights[side, tile, ifgs, :] = weight[:, tile * 128 : tile * 128 + 128]
        added[ifgs, :] = top
        added[lows, :] = low
        return 0

    lax.fori_loop(0, 4, group, 0)
    copies = []
    for side, row in ((0, 0), (1, 7)):
        copies.append(pltpu.make_async_copy(smooth.at[side], smooth_out.at[row], sems.at[side, 8]))
        for step, out in enumerate(outs):
            lanes = pl.ds(row * 128, 128)
            copies.append(
                pltpu.make_async_copy(weights.at[side, owner(step)], out.at[:, lanes], sems.at[side, step])
            )
    for copy in copies:
        copy.start()
    sums[...] = jnp.broadcast_to(jnp.sum(added[...].T, axis=0)[None, None, :], sums.shape)
    for copy in copies:
        copy.wait()


def stage(source, out, sems):
    copies = [
        pltpu.make_async_copy(source.at[pl.ds(part * 2, 2)], out.at[pl.ds(part * 2, 2)], sems.at[part])
        for part in range(4)
    ]
    for copy in copies:
        copy.start()
    for copy in copies:
        copy.wait()


def correction(sums, smooth, height, slope_row, *rest):
    outs, blocks = rest[:8], rest[8]
    total = sums[0]
    for index in range(1, sums.shape[0]):
        total += sums[index]
    slope_row[...] = total / pltpu.roll(total, 64, 1)
    column = jnp.broadcast_to(total, (128, 128)).T
    slope = column[:64, :] / column[64:, :]

    def one_tile(tile, _):
        lanes = pl.ds(pl.multiple_of(tile * 128, 128), 128)
        for row in range(8):
            value = smooth[row, :, lanes] - slope * height[pl.ds(row, 1), lanes]
            blocks[tile, :, pl.ds(row * 128, 128)] = value.astype(BF16)
        return 0

    lax.fori_loop(0, 8, one_tile, 0)
    for step, out in enumerate(outs):
        out[...] = blocks[owner(step)]


def column_selector():
    row = lax.broadcasted_iota(jnp.int32, (16, 1024), 0)
    pixel = lax.broadcasted_iota(jnp.int32, (16, 1024), 1)
    wanted = jnp.where(row < 8, row * 128, (row - 8) * 128 + 127)
    return (pixel == wanted).astype(BF16)


def write_edges(field, last, columns, first=None):
    if first is not None:
        first[...] = field[:, pl.ds(0, 128)].astype(BF16)
    last[...] = field[:, pl.ds(896, 128)].astype(BF16)
    picked = lax.dot_general(
        column_selector(), field[...].astype(BF16), (((1,), (1,)), ((), ())), preferred_element_type=F32
    )
    columns[...] = picked.astype(BF16)


def right_side(*refs):
    weight_parts, corrected_parts = refs[:8], refs[8:16]
    design_t, field, weights, *edges = refs[16:]
    for part in range(8):
        weights[pl.ds(part * 64, 64), :] = weight_parts[part][...]

    def one_chunk(chunk, _):
        lanes = pl.ds(pl.multiple_of(chunk * 256, 256), 256)
        scaled = jnp.concatenate(
            [
                weight_parts[part][:, lanes].astype(F32) * corrected_parts[part][:, lanes].astype(F32)
                for part in range(8)
            ],
            axis=0,
        )
        high, low = split(scaled)
        field[:, lanes] = dot(design_t[...], high) + dot(design_t[...], low)
        return 0

    lax.fori_loop(0, 4, one_chunk, 0)
    write_edges(field, *edges)


def row_lanes(row):
    return pl.ds(pl.multiple_of(row * 128, 128), 128)


def local_image(field, weights, design, design_t, chunk):
    lanes = pl.ds(pl.multiple_of(chunk * 256, 256), 256)
    high, low = split(field[:, lanes])
    scaled = dot(design[...], jnp.concatenate([high, low], axis=0)) * weights[:, lanes].astype(F32)
    high, low = split(scaled)
    back = dot(design_t[...], high) + dot(design_t[...], low)
    lane = lax.broadcasted_iota(jnp.int32, (DP, 128), 1)
    parts = []
    for offset in range(2):
        row = 2 * chunk + offset
        here = field[:, row_lanes(row)]
        around = jnp.where(lane == 0, 0.0, pltpu.roll(here, 1, 1))
        around += jnp.where(lane == 127, 0.0, pltpu.roll(here, 127, 1))
        around += jnp.where(row > 0, field[:, row_lanes(jnp.maximum(row - 1, 0))], 0.0)
        around += jnp.where(row < 7, field[:, row_lanes(jnp.minimum(row + 1, 7))], 0.0)
        part = back[:, offset * 128 : offset * 128 + 128] + CENTRE * here - SMOOTHING_WEIGHT * around
        parts.append((row, part))
    return parts


def fold(values):
    return jnp.sum(values.reshape(DP // 8, 8, 128), axis=0)


def apply_local(with_before, with_image, *refs):
    field, weights, design, design_t = refs[:4]
    refs = refs[4:]
    before = None
    if with_before:
        before, refs = refs[0], refs[1:]
    image = None
    if with_image:
        image, refs = refs[0], refs[1:]
    moments = refs[0]

    def one_chunk(chunk, totals):
        square, cross, ahead = totals
        for row, part in local_image(field, weights, design, design_t, chunk):
            here = field[:, row_lanes(row)]
            square += fold(here * here)
            if with_before:
                cross += fold(here * before[:, row_lanes(row)])
            if with_image:
                image[:, row_lanes(row)] = part
            else:
                ahead += fold(here * part)
        return square, cross, ahead

    zero = jnp.zeros((8, 128), F32)
    totals = lax.fori_loop(0, 4, one_chunk, (zero, zero, zero), unroll=True)
    for index in range(3):
        moments[index] = totals[index]


def spread_columns(columns, pixels):
    row = lax.broadcasted_iota(jnp.int32, (16, 128), 0)
    lane = lax.broadcasted_iota(jnp.int32, (16, 128), 1)
    wanted = jnp.where(row < 8, row, row - 8) == pixels
    place = (wanted & (lane == jnp.where(row < 8, 0, 127))).astype(BF16)
    return lax.dot_general(columns, place, (((0,), (0,)), ((), ())), preferred_element_type=F32)


def keep(flag, values):
    return jnp.where(flag, values.astype(F32), 0.0)


def inside():
    row, col = lax.axis_index("rows"), lax.axis_index("ifg")
    return row > 0, row < lax.axis_size("rows") - 1, col > 0, col < lax.axis_size("ifg") - 1


def add_halo(image, above, below, left, right, field, *edges):
    flags = inside()
    sides = jnp.concatenate([keep(flags[2], left[8:16, :]), keep(flags[3], right[0:8, :])], axis=0).astype(BF16)
    for row in range(8):
        lanes = pl.ds(row * 128, 128)
        halo = spread_columns(sides, row)
        if row == 0:
            halo += keep(flags[0], above[...])
        if row == 7:
            halo += keep(flags[1], below[...])
        field[:, lanes] = image[:, lanes] - SMOOTHING_WEIGHT * halo
    write_edges(field, *edges)


def all_moments(field, above, left, zero, one, two, out):
    flags = inside()
    sides = jnp.concatenate([keep(flags[2], left[8:16, :]), jnp.zeros((8, DP), F32)], axis=0).astype(BF16)
    ahead = two[2]
    for row in range(8):
        halo = spread_columns(sides, row)
        if row == 0:
            halo += keep(flags[0], above[...])
        ahead -= (2.0 * SMOOTHING_WEIGHT) * fold(field[:, pl.ds(row * 128, 128)] * halo)
    rows = [zero[0], one[1], one[0], two[1], two[0], ahead]
    lane = lax.broadcasted_iota(jnp.int32, (1, 128), 1)
    total = jnp.zeros((1, 128), F32)
    for index, values in enumerate(rows):
        line = jnp.sum(values, axis=0, keepdims=True)
        total += jnp.where(lane == index, jnp.sum(line, axis=1, keepdims=True), 0.0)
    out[...] = total


def add_and_spread(one, two, basis, out):
    out[...] = jnp.broadcast_to((one[...] + two[...])[None], out.shape)


def combine(parts, zero, one, two, out, field, sems):
    total = parts[0]
    for index in range(1, parts.shape[0]):
        total += parts[index]
    m0, m1, m2, m3, m4, m5 = (jnp.broadcast_to(total[:, i : i + 1], (1, 128)) for i in range(6))
    t00, t01, t11 = m1 + SHIFT * m0, m2 + SHIFT * m1, m3 + SHIFT * m2
    t12, t22 = m4 + SHIFT * m3, m5 + SHIFT * m4
    l10, l20 = t01 / t00, t11 / t00
    pivot = t11 - l10 * t01
    off = t12 - l20 * t01
    keep = pivot > 1e-6 * t11
    safe = jnp.where(keep, pivot, 1.0)
    l21 = jnp.where(keep, off / safe, 0.0)
    last = t22 - l20 * t11 - l21 * off
    keep_last = keep & (last > 1e-6 * t22)
    y1 = m1 - l10 * m0
    y2 = m2 - l20 * m0 - l21 * y1
    c2 = jnp.where(keep_last, y2 / jnp.where(keep_last, last, 1.0), 0.0)
    c1 = jnp.where(keep, y1 / safe, 0.0) - l21 * c2
    c0 = m0 / t00 - l10 * c1 - l20 * c2
    copies = []
    for part in range(4):
        count = min(80, DATES - part * 80)
        dates = pl.ds(part * 80, (count + 7) // 8 * 8)
        for row in range(8):
            lanes = pl.ds(row * 128, 128)
            value = c0 * zero[dates, lanes] + c1 * one[dates, lanes] + c2 * two[dates, lanes]
            field[pl.ds(part * 640 + row, count, stride=8), :] = value[:count, :]
        lines = pl.ds(part * 640, count * 8)
        copies.append(pltpu.make_async_copy(field.at[lines], out.at[lines], sems.at[part]))
        copies[-1].start()
    for copy in copies:
        copy.wait()


def per_device(phase, coherence, height, gap_mask, date_pairs):
    n_ifg, n_rows = lax.axis_size("ifg"), lax.axis_size("rows")
    me = lax.axis_index("ifg")

    def permute(values, axis, target):
        return lax.ppermute(values, axis, [(i, target(i)) for i in range(lax.axis_size(axis))])

    def forward(values, axis):
        return permute(values, axis, lambda i: (i + 1) % lax.axis_size(axis))

    def backward(values, axis):
        return permute(values, axis, lambda i: (i - 1) % lax.axis_size(axis))

    stacked = sds((8, 64, 1024), BF16)
    edge = sds((128, 1024), BF16)
    phase_t, coher_t, first, last = call(
        rows_first,
        (stacked, stacked, edge, edge),
        pltpu.with_memory_space_constraint(phase, pltpu.HBM),
        pltpu.with_memory_space_constraint(coherence, pltpu.HBM),
        specs=[pltpu.HBM] * 2,
        scratch=(
            pltpu.VMEM((64, 8, 1024), BF16),
            pltpu.VMEM((64, 8, 1024), BF16),
            pltpu.VMEM((2, 8, 128, 128), F32),
            pltpu.SemaphoreType.DMA((2, 4)),
        ),
        name="rows_first",
    )
    above, below = forward(last, "rows"), backward(first, "rows")
    mask = gap_mask.astype(F32)
    pieces = [in_hbm((64, 1024), BF16)] * 8
    smooth, totals, *weight_parts = call(
        inner_rows,
        [in_hbm((8, 64, 1024), F32), sds((128, 128), F32)] + pieces,
        phase_t,
        coher_t,
        mask,
        height,
        out_specs=[pltpu.HBM, pltpu.VMEM] + [pltpu.HBM] * 8,
        scratch=(
            pltpu.VMEM((8, 64, 768), BF16),
            pltpu.VMEM((6, 64, 1024), F32),
            pltpu.SemaphoreType.DMA((4, 9)),
        ),
        name="inner_rows",
    )
    smooth, sums, *weight_parts = call(
        border_rows,
        [in_hbm((8, 64, 1024), F32), sds((n_rows, 1, 128), F32)] + pieces,
        phase_t,
        coher_t,
        above,
        below,
        mask,
        height,
        totals,
        smooth,
        *weight_parts,
        specs=[pltpu.VMEM] * 7 + [pltpu.HBM] * 9,
        out_specs=[pltpu.HBM, pltpu.VMEM] + [pltpu.HBM] * 8,
        scratch=(
            pltpu.VMEM((2, 8, 64, 128), BF16),
            pltpu.VMEM((2, 64, 1024), F32),
            pltpu.VMEM((128, 128), F32),
            pltpu.SemaphoreType.DMA((2, 9)),
        ),
        aliases={7: 0, **{8 + step: 2 + step for step in range(8)}},
        name="border_rows",
    )

    def exchange(parts):
        return [parts[0]] + [
            permute(part, "ifg", lambda i: other(i, *offset))
            for part, offset in zip(parts[1:], OFFSETS[1:])
        ]

    weight_parts = exchange(weight_parts)
    sums, weight_parts[1] = lax.optimization_barrier((sums, weight_parts[1]))
    sums = lax.all_to_all(sums, "rows", 0, 0, tiled=True)
    sums, *weight_parts[2:5] = lax.optimization_barrier((sums, *weight_parts[2:5]))
    smooth = call(
        stage,
        sds((8, 64, 1024), F32),
        pltpu.with_memory_space_constraint(smooth, pltpu.HBM),
        specs=[pltpu.HBM],
        scratch=(pltpu.SemaphoreType.DMA((4,)),),
        name="stage",
    )
    slope_row, *corrected_parts = call(
        correction,
        [sds((1, 128), F32)] + [sds((64, 1024), BF16)] * 8,
        sums,
        smooth,
        height,
        scratch=(pltpu.VMEM((8, 64, 1024), BF16),),
        name="correction",
    )
    slope, corrected_parts[0] = lax.optimization_barrier((slope_row[0, :64], corrected_parts[0]))
    corrected_parts = exchange(corrected_parts)
    sources = jnp.stack([other(me, 4 - chips, core) for chips, core in OFFSETS])
    pairs = date_pairs.reshape(n_ifg, -1, 2)[sources].reshape(-1, 2)
    dates = jnp.arange(DP, dtype=jnp.int32)
    design = ((dates[None] == pairs[:, 1:2]).astype(F32) - (dates[None] == pairs[:, 0:1]).astype(F32)).astype(BF16)
    design_t = design.T
    design = jnp.concatenate([design, design], axis=1)

    field = sds((DP, 1024), F32)
    edges = (sds((DP, 128), BF16), sds((16, DP), BF16), sds((DP, 128), BF16))
    moments = sds((3, 8, 128), F32)
    k0, weights, *sides = call(
        right_side,
        (field, sds((512, 1024), BF16)) + edges,
        *weight_parts,
        *corrected_parts,
        design_t,
        name="right_side",
    )

    def halos(last, columns, first):
        return (
            forward(last, "rows"),
            backward(first, "rows"),
            forward(columns, "ifg"),
            backward(columns, "ifg"),
        )

    def local(with_before, with_image, name, *args):
        outs = ((field,) if with_image else ()) + (moments,)
        body = lambda *refs: apply_local(with_before, with_image, *refs)
        return call(body, outs, *args, name=name)

    def joined(image, around, count, name):
        return call(add_halo, (field,) + edges[:count], image, *around, name=name)

    around = halos(*sides)
    image, mom0 = local(False, True, "apply0", k0, weights, design, design_t)
    k1, *sides = joined(image, around, 3, "add_halo1")
    around = halos(*sides)
    image, mom1 = local(True, True, "apply1", k1, weights, design, design_t, k0)
    k2, last, columns = joined(image, around, 2, "add_halo2")
    above, left = forward(last, "rows"), forward(columns, "ifg")
    (mom2,) = local(True, False, "apply2", k2, weights, design, design_t, k1)
    part = call(
        all_moments,
        sds((1, 128), F32),
        k2,
        above,
        left,
        mom0,
        mom1,
        mom2,
        name="all_moments",
    )
    for step in (1, 2):
        part = part + permute(part, "ifg", lambda i: i ^ step)
    parts = call(
        add_and_spread,
        sds((n_rows, 1, 128), F32),
        part,
        permute(part, "ifg", lambda i: i ^ 4),
        k0,
        name="add_and_spread",
    )
    parts = lax.all_to_all(parts, "rows", 0, 0, tiled=True)
    displacement = call(
        combine,
        sds((DATES * 8, 128), F32),
        parts,
        k0,
        k1,
        k2,
        out_specs=[pltpu.HBM],
        scratch=(pltpu.VMEM((DATES * 8, 128), F32), pltpu.SemaphoreType.DMA((4,))),
        name="combine",
    )
    return displacement.reshape(DATES, 8, 128), slope


def solution(mesh):
    placed = (
        P("ifg", "rows", None),
        P("ifg", "rows", None),
        P("rows", None),
        P("ifg", "rows"),
        P(),
    )
    return jax.shard_map(
        per_device,
        mesh=mesh,
        in_specs=placed,
        out_specs=(P(None, "rows", "ifg"), P("ifg")),
        check_vma=False,
    )
```

```python
import jax
import jax.numpy as jnp
from jax import lax
from jax.experimental import pallas as pl
from jax.experimental.pallas import tpu as pltpu
from jax.sharding import PartitionSpec as P

DATES = 300
DP = 304
SHIFT = 4.0
SMOOTHING_WEIGHT = 0.5
RIDGE_WEIGHT = 0.05
CENTRE = 4.0 * SMOOTHING_WEIGHT + RIDGE_WEIGHT - SHIFT
F32 = jnp.float32
BF16 = jnp.bfloat16


def sds(shape, dtype):
    return jax.ShapeDtypeStruct(shape, dtype)


def in_hbm(shape, dtype):
    return pltpu.HBM(shape, dtype)


def call(body, outs, *args, specs=None, out_specs=None, scratch=(), aliases=None, name=None):
    flat = outs if isinstance(outs, (list, tuple)) else [outs]
    places = specs or [pltpu.VMEM] * len(args)
    out_places = [pl.BlockSpec(memory_space=place) for place in out_specs or [pltpu.VMEM] * len(flat)]
    return pl.pallas_call(
        body,
        out_shape=outs,
        in_specs=[pl.BlockSpec(memory_space=place) for place in places],
        out_specs=out_places if isinstance(outs, (list, tuple)) else out_places[0],
        scratch_shapes=list(scratch),
        input_output_aliases=aliases or {},
        compiler_params=pltpu.CompilerParams(vmem_limit_bytes=16 * 1024 * 1024),
        name=name,
    )(*args)


def dot(a, b):
    return jnp.dot(a, b, preferred_element_type=F32)


def split(values):
    high = values.astype(BF16)
    return high, (values - high.astype(F32)).astype(BF16)


def rows_first(phase, coher, phase_t, coher_t, first, last, phase_in, coher_in, wide, sems):
    pairs = ((phase, phase_in, phase_t), (coher, coher_in, coher_t))

    def fetch(part, block):
        ifgs, _ = block_of(block)
        return pltpu.make_async_copy(pairs[part][0].at[ifgs], pairs[part][1].at[ifgs], sems.at[part, block])

    for block in range(4):
        for part in range(2):
            fetch(part, block).start()

    def group(block, _):
        ifgs, _ = block_of(block)
        for part, (_, source, target) in enumerate(pairs):
            fetch(part, block).wait()
            for tile in range(8):
                lanes = pl.ds(tile * 128, 128)
                wide[part, tile] = source[ifgs, :, lanes].astype(F32).reshape(128, 128)
                for row in range(8):
                    target[row, ifgs, lanes] = wide[part, tile, pl.ds(row, 16, stride=8), :].astype(BF16)
        return 0

    lax.fori_loop(0, 4, group, 0)
    for part, target in enumerate((phase_t, coher_t)):
        first[pl.ds(part * 64, 64), :] = target[0]
        last[pl.ds(part * 64, 64), :] = target[7]


def shifted_sum(values, lane, last):
    left = jnp.where(lane == 0, 0.0, pltpu.roll(values, 1, 1))
    right = jnp.where(lane == last, 0.0, pltpu.roll(values, last, 1))
    return values + left + right


def fold_lanes(values):
    total = values[:, :128]
    for tile in range(1, 8):
        total += values[:, tile * 128 : tile * 128 + 128]
    return total


OFFSETS = ((0, 0), (0, 1), (2, 0), (1, 0), (3, 0), (2, 1), (1, 1), (3, 1))


def other(index, chips, core):
    return (((index >> 1) + chips) & 3) * 2 + ((index & 1) ^ core)


def owner(step):
    return other(lax.axis_index("ifg"), *OFFSETS[step])


def smooth_row(rows, lane, mask, terrain):
    denom = shifted_sum(rows[0][0] + rows[1][0] + rows[2][0], lane, 1023)
    numer = shifted_sum(rows[0][1] + rows[1][1] + rows[2][1], lane, 1023)
    top = fold_lanes(numer * terrain)
    low = fold_lanes(denom * (terrain * terrain))
    return numer / denom, (mask * (denom / 9.0)).astype(BF16), top, low


def load_row(phase_t, coher_t, row, ifgs):
    coher = coher_t[row, ifgs, :].astype(F32)
    return coher, coher * phase_t[row, ifgs, :].astype(F32)


def block_of(block):
    return pl.ds(pl.multiple_of(block * 16, 16), 16), pl.ds(pl.multiple_of(block * 16 + 64, 16), 16)


def inner_rows(phase_t, coher_t, mask, height, smooth_out, totals, *rest):
    outs, weights, smooth, sems = rest[:8], *rest[8:]
    lane = lax.broadcasted_iota(jnp.int32, (16, 1024), 1)

    def copies(block):
        ifgs, _ = block_of(block)
        return [
            pltpu.make_async_copy(
                weights.at[owner(step), ifgs], out.at[ifgs, pl.ds(128, 768)], sems.at[block, step]
            )
            for step, out in enumerate(outs)
        ] + [pltpu.make_async_copy(smooth.at[:, ifgs], smooth_out.at[pl.ds(1, 6), ifgs], sems.at[block, 8])]

    def group(block, _):
        ifgs, lows = block_of(block)
        masks = mask[ifgs, :]
        rows = [load_row(phase_t, coher_t, row, ifgs) for row in (0, 1)]
        top = jnp.zeros((16, 128), F32)
        low = jnp.zeros((16, 128), F32)
        for row in range(1, 7):
            rows.append(load_row(phase_t, coher_t, row + 1, ifgs))
            value, weight, more_top, more_low = smooth_row(
                rows, lane, masks[:, row : row + 1], height[pl.ds(row, 1), :]
            )
            rows = rows[1:]
            top += more_top
            low += more_low
            smooth[row - 1, ifgs, :] = value
            for tile in range(8):
                weights[tile, ifgs, pl.ds((row - 1) * 128, 128)] = weight[:, tile * 128 : tile * 128 + 128]
        totals[ifgs, :] = top
        totals[lows, :] = low
        for copy in copies(block):
            copy.start()
        return 0

    lax.fori_loop(0, 4, group, 0)
    for block in range(4):
        for copy in copies(block):
            copy.wait()


def border_rows(phase_t, coher_t, above, below, mask, height, totals, *rest):
    smooth_out, sums, outs = rest[9], rest[10], rest[11:19]
    weights, smooth, added, sems = rest[19:]
    lane = lax.broadcasted_iota(jnp.int32, (16, 1024), 1)
    my_row = lax.axis_index("rows")
    valid = (my_row > 0, my_row < lax.axis_size("rows") - 1)

    def group(block, _):
        ifgs, lows = block_of(block)
        masks = mask[ifgs, :]
        top = totals[ifgs, :]
        low = totals[lows, :]
        for side, (edge, row) in enumerate(((above, 0), (below, 7))):
            coher = jnp.where(valid[side], edge[lows, :].astype(F32), 0.0)
            rows = [(coher, coher * edge[ifgs, :].astype(F32))]
            rows += [load_row(phase_t, coher_t, near, ifgs) for near in (row, 1 if row == 0 else 6)]
            value, weight, more_top, more_low = smooth_row(
                rows, lane, masks[:, row : row + 1], height[pl.ds(row, 1), :]
            )
            top += more_top
            low += more_low
            smooth[side, ifgs, :] = value
            for tile in range(8):
                weights[side, tile, ifgs, :] = weight[:, tile * 128 : tile * 128 + 128]
        added[ifgs, :] = top
        added[lows, :] = low
        return 0

    lax.fori_loop(0, 4, group, 0)
    copies = []
    for side, row in ((0, 0), (1, 7)):
        copies.append(pltpu.make_async_copy(smooth.at[side], smooth_out.at[row], sems.at[side, 8]))
        for step, out in enumerate(outs):
            lanes = pl.ds(row * 128, 128)
            copies.append(
                pltpu.make_async_copy(weights.at[side, owner(step)], out.at[:, lanes], sems.at[side, step])
            )
    for copy in copies:
        copy.start()
    sums[...] = jnp.broadcast_to(jnp.sum(added[...].T, axis=0)[None, None, :], sums.shape)
    for copy in copies:
        copy.wait()


def stage(source, out, sems):
    copies = [
        pltpu.make_async_copy(source.at[pl.ds(part * 2, 2)], out.at[pl.ds(part * 2, 2)], sems.at[part])
        for part in range(4)
    ]
    for copy in copies:
        copy.start()
    for copy in copies:
        copy.wait()


def correction(sums, smooth, height, slope_row, *rest):
    outs, blocks = rest[:8], rest[8]
    total = sums[0]
    for index in range(1, sums.shape[0]):
        total += sums[index]
    slope_row[...] = total / pltpu.roll(total, 64, 1)
    column = jnp.broadcast_to(total, (128, 128)).T
    slope = column[:64, :] / column[64:, :]

    def one_tile(tile, _):
        lanes = pl.ds(pl.multiple_of(tile * 128, 128), 128)
        for row in range(8):
            value = smooth[row, :, lanes] - slope * height[pl.ds(row, 1), lanes]
            blocks[tile, :, pl.ds(row * 128, 128)] = value.astype(BF16)
        return 0

    lax.fori_loop(0, 8, one_tile, 0)
    for step, out in enumerate(outs):
        out[...] = blocks[owner(step)]


def column_selector():
    row = lax.broadcasted_iota(jnp.int32, (16, 1024), 0)
    pixel = lax.broadcasted_iota(jnp.int32, (16, 1024), 1)
    wanted = jnp.where(row < 8, row * 128, (row - 8) * 128 + 127)
    return (pixel == wanted).astype(BF16)


def write_edges(field, last, columns, first=None):
    if first is not None:
        first[...] = field[:, pl.ds(0, 128)].astype(BF16)
    last[...] = field[:, pl.ds(896, 128)].astype(BF16)
    picked = lax.dot_general(
        column_selector(), field[...].astype(BF16), (((1,), (1,)), ((), ())), preferred_element_type=F32
    )
    columns[...] = picked.astype(BF16)


def right_side(*refs):
    weight_parts, corrected_parts = refs[:8], refs[8:16]
    design_t, field, weights, *edges = refs[16:]
    for part in range(8):
        weights[pl.ds(part * 64, 64), :] = weight_parts[part][...]

    def one_chunk(chunk, _):
        lanes = pl.ds(pl.multiple_of(chunk * 256, 256), 256)
        scaled = jnp.concatenate(
            [
                weight_parts[part][:, lanes].astype(F32) * corrected_parts[part][:, lanes].astype(F32)
                for part in range(8)
            ],
            axis=0,
        )
        high, low = split(scaled)
        field[:, lanes] = dot(design_t[...], high) + dot(design_t[...], low)
        return 0

    lax.fori_loop(0, 4, one_chunk, 0)
    write_edges(field, *edges)


def row_lanes(row):
    return pl.ds(pl.multiple_of(row * 128, 128), 128)


def local_image(field, weights, design, design_t, chunk, with_image):
    lanes = pl.ds(pl.multiple_of(chunk * 256, 256), 256)
    high, low = split(field[:, lanes])
    across = dot(design[...], jnp.concatenate([high, low], axis=0))
    scaled = across * weights[:, lanes].astype(F32)
    back, square = None, None
    if with_image:
        high, low = split(scaled)
        back = dot(design_t[...], high) + dot(design_t[...], low)
    else:
        square = across * scaled
    lane = lax.broadcasted_iota(jnp.int32, (DP, 128), 1)
    parts = []
    for offset in range(2):
        row = 2 * chunk + offset
        here = field[:, row_lanes(row)]
        around = jnp.where(lane == 0, 0.0, pltpu.roll(here, 1, 1))
        around += jnp.where(lane == 127, 0.0, pltpu.roll(here, 127, 1))
        around += jnp.where(row > 0, field[:, row_lanes(jnp.maximum(row - 1, 0))], 0.0)
        around += jnp.where(row < 7, field[:, row_lanes(jnp.minimum(row + 1, 7))], 0.0)
        part = CENTRE * here - SMOOTHING_WEIGHT * around
        if with_image:
            part = back[:, offset * 128 : offset * 128 + 128] + part
        parts.append((row, part))
    return parts, square


def fold(values):
    return jnp.sum(values.reshape(-1, 8, 128), axis=0)


def apply_local(with_before, with_image, *refs):
    field, weights, design, design_t = refs[:4]
    refs = refs[4:]
    before = None
    if with_before:
        before, refs = refs[0], refs[1:]
    image = None
    if with_image:
        image, refs = refs[0], refs[1:]
    moments = refs[0]

    def one_chunk(chunk, totals):
        square, cross, ahead = totals
        parts, across = local_image(field, weights, design, design_t, chunk, with_image)
        if not with_image:
            ahead += fold(across[:, :128]) + fold(across[:, 128:])
        for row, part in parts:
            here = field[:, row_lanes(row)]
            square += fold(here * here)
            if with_before:
                cross += fold(here * before[:, row_lanes(row)])
            if with_image:
                image[:, row_lanes(row)] = part
            else:
                ahead += fold(here * part)
        return square, cross, ahead

    zero = jnp.zeros((8, 128), F32)
    totals = lax.fori_loop(0, 4, one_chunk, (zero, zero, zero), unroll=True)
    for index in range(3):
        moments[index] = totals[index]


def spread_columns(columns, pixels):
    row = lax.broadcasted_iota(jnp.int32, (16, 128), 0)
    lane = lax.broadcasted_iota(jnp.int32, (16, 128), 1)
    wanted = jnp.where(row < 8, row, row - 8) == pixels
    place = (wanted & (lane == jnp.where(row < 8, 0, 127))).astype(BF16)
    return lax.dot_general(columns, place, (((0,), (0,)), ((), ())), preferred_element_type=F32)


def keep(flag, values):
    return jnp.where(flag, values.astype(F32), 0.0)


def inside():
    row, col = lax.axis_index("rows"), lax.axis_index("ifg")
    return row > 0, row < lax.axis_size("rows") - 1, col > 0, col < lax.axis_size("ifg") - 1


def add_halo(image, above, below, left, right, field, *edges):
    flags = inside()
    sides = jnp.concatenate([keep(flags[2], left[8:16, :]), keep(flags[3], right[0:8, :])], axis=0).astype(BF16)
    for row in range(8):
        lanes = pl.ds(row * 128, 128)
        halo = spread_columns(sides, row)
        if row == 0:
            halo += keep(flags[0], above[...])
        if row == 7:
            halo += keep(flags[1], below[...])
        field[:, lanes] = image[:, lanes] - SMOOTHING_WEIGHT * halo
    write_edges(field, *edges)


def all_moments(field, above, left, zero, one, two, out):
    flags = inside()
    sides = jnp.concatenate([keep(flags[2], left[8:16, :]), jnp.zeros((8, DP), F32)], axis=0).astype(BF16)
    ahead = two[2]
    for row in range(8):
        halo = spread_columns(sides, row)
        if row == 0:
            halo += keep(flags[0], above[...])
        ahead -= (2.0 * SMOOTHING_WEIGHT) * fold(field[:, pl.ds(row * 128, 128)] * halo)
    rows = [zero[0], one[1], one[0], two[1], two[0], ahead]
    lane = lax.broadcasted_iota(jnp.int32, (1, 128), 1)
    total = jnp.zeros((1, 128), F32)
    for index, values in enumerate(rows):
        line = jnp.sum(values, axis=0, keepdims=True)
        total += jnp.where(lane == index, jnp.sum(line, axis=1, keepdims=True), 0.0)
    out[...] = total


def add_and_spread(one, two, basis, out):
    out[...] = jnp.broadcast_to((one[...] + two[...])[None], out.shape)


def combine(parts, zero, one, two, out, field, sems):
    total = parts[0]
    for index in range(1, parts.shape[0]):
        total += parts[index]
    m0, m1, m2, m3, m4, m5 = (jnp.broadcast_to(total[:, i : i + 1], (1, 128)) for i in range(6))
    t00, t01, t11 = m1 + SHIFT * m0, m2 + SHIFT * m1, m3 + SHIFT * m2
    t12, t22 = m4 + SHIFT * m3, m5 + SHIFT * m4
    l10, l20 = t01 / t00, t11 / t00
    pivot = t11 - l10 * t01
    off = t12 - l20 * t01
    keep = pivot > 1e-6 * t11
    safe = jnp.where(keep, pivot, 1.0)
    l21 = jnp.where(keep, off / safe, 0.0)
    last = t22 - l20 * t11 - l21 * off
    keep_last = keep & (last > 1e-6 * t22)
    y1 = m1 - l10 * m0
    y2 = m2 - l20 * m0 - l21 * y1
    c2 = jnp.where(keep_last, y2 / jnp.where(keep_last, last, 1.0), 0.0)
    c1 = jnp.where(keep, y1 / safe, 0.0) - l21 * c2
    c0 = m0 / t00 - l10 * c1 - l20 * c2
    copies = []
    for part in range(4):
        count = min(80, DATES - part * 80)
        dates = pl.ds(part * 80, (count + 7) // 8 * 8)
        for row in range(8):
            lanes = pl.ds(row * 128, 128)
            value = c0 * zero[dates, lanes] + c1 * one[dates, lanes] + c2 * two[dates, lanes]
            field[pl.ds(part * 640 + row, count, stride=8), :] = value[:count, :]
        lines = pl.ds(part * 640, count * 8)
        copies.append(pltpu.make_async_copy(field.at[lines], out.at[lines], sems.at[part]))
        copies[-1].start()
    for copy in copies:
        copy.wait()


def per_device(phase, coherence, height, gap_mask, date_pairs):
    n_ifg, n_rows = lax.axis_size("ifg"), lax.axis_size("rows")
    me = lax.axis_index("ifg")

    def permute(values, axis, target):
        return lax.ppermute(values, axis, [(i, target(i)) for i in range(lax.axis_size(axis))])

    def forward(values, axis):
        return permute(values, axis, lambda i: (i + 1) % lax.axis_size(axis))

    def backward(values, axis):
        return permute(values, axis, lambda i: (i - 1) % lax.axis_size(axis))

    stacked = sds((8, 64, 1024), BF16)
    edge = sds((128, 1024), BF16)
    phase_t, coher_t, first, last = call(
        rows_first,
        (stacked, stacked, edge, edge),
        pltpu.with_memory_space_constraint(phase, pltpu.HBM),
        pltpu.with_memory_space_constraint(coherence, pltpu.HBM),
        specs=[pltpu.HBM] * 2,
        scratch=(
            pltpu.VMEM((64, 8, 1024), BF16),
            pltpu.VMEM((64, 8, 1024), BF16),
            pltpu.VMEM((2, 8, 128, 128), F32),
            pltpu.SemaphoreType.DMA((2, 4)),
        ),
        name="rows_first",
    )
    above, below = forward(last, "rows"), backward(first, "rows")
    mask = gap_mask.astype(F32)
    pieces = [in_hbm((64, 1024), BF16)] * 8
    smooth, totals, *weight_parts = call(
        inner_rows,
        [in_hbm((8, 64, 1024), F32), sds((128, 128), F32)] + pieces,
        phase_t,
        coher_t,
        mask,
        height,
        out_specs=[pltpu.HBM, pltpu.VMEM] + [pltpu.HBM] * 8,
        scratch=(
            pltpu.VMEM((8, 64, 768), BF16),
            pltpu.VMEM((6, 64, 1024), F32),
            pltpu.SemaphoreType.DMA((4, 9)),
        ),
        name="inner_rows",
    )
    smooth, sums, *weight_parts = call(
        border_rows,
        [in_hbm((8, 64, 1024), F32), sds((n_rows, 1, 128), F32)] + pieces,
        phase_t,
        coher_t,
        above,
        below,
        mask,
        height,
        totals,
        smooth,
        *weight_parts,
        specs=[pltpu.VMEM] * 7 + [pltpu.HBM] * 9,
        out_specs=[pltpu.HBM, pltpu.VMEM] + [pltpu.HBM] * 8,
        scratch=(
            pltpu.VMEM((2, 8, 64, 128), BF16),
            pltpu.VMEM((2, 64, 1024), F32),
            pltpu.VMEM((128, 128), F32),
            pltpu.SemaphoreType.DMA((2, 9)),
        ),
        aliases={7: 0, **{8 + step: 2 + step for step in range(8)}},
        name="border_rows",
    )

    def exchange(parts):
        return [parts[0]] + [
            permute(part, "ifg", lambda i: other(i, *offset))
            for part, offset in zip(parts[1:], OFFSETS[1:])
        ]

    weight_parts = exchange(weight_parts)
    sums, weight_parts[1] = lax.optimization_barrier((sums, weight_parts[1]))
    sums = lax.all_to_all(sums, "rows", 0, 0, tiled=True)
    sums, *weight_parts[2:5] = lax.optimization_barrier((sums, *weight_parts[2:5]))
    smooth = call(
        stage,
        sds((8, 64, 1024), F32),
        pltpu.with_memory_space_constraint(smooth, pltpu.HBM),
        specs=[pltpu.HBM],
        scratch=(pltpu.SemaphoreType.DMA((4,)),),
        name="stage",
    )
    slope_row, *corrected_parts = call(
        correction,
        [sds((1, 128), F32)] + [sds((64, 1024), BF16)] * 8,
        sums,
        smooth,
        height,
        scratch=(pltpu.VMEM((8, 64, 1024), BF16),),
        name="correction",
    )
    slope, corrected_parts[0] = lax.optimization_barrier((slope_row[0, :64], corrected_parts[0]))
    corrected_parts = exchange(corrected_parts)
    sources = jnp.stack([other(me, 4 - chips, core) for chips, core in OFFSETS])
    pairs = date_pairs.reshape(n_ifg, -1, 2)[sources].reshape(-1, 2)
    dates = jnp.arange(DP, dtype=jnp.int32)
    design = ((dates[None] == pairs[:, 1:2]).astype(F32) - (dates[None] == pairs[:, 0:1]).astype(F32)).astype(BF16)
    design_t = design.T
    design = jnp.concatenate([design, design], axis=1)

    field = sds((DP, 1024), F32)
    edges = (sds((DP, 128), BF16), sds((16, DP), BF16), sds((DP, 128), BF16))
    moments = sds((3, 8, 128), F32)
    k0, weights, *sides = call(
        right_side,
        (field, sds((512, 1024), BF16)) + edges,
        *weight_parts,
        *corrected_parts,
        design_t,
        name="right_side",
    )

    def halos(last, columns, first):
        return (
            forward(last, "rows"),
            backward(first, "rows"),
            forward(columns, "ifg"),
            backward(columns, "ifg"),
        )

    def local(with_before, with_image, name, *args):
        outs = ((field,) if with_image else ()) + (moments,)
        body = lambda *refs: apply_local(with_before, with_image, *refs)
        return call(body, outs, *args, name=name)

    def joined(image, around, count, name):
        return call(add_halo, (field,) + edges[:count], image, *around, name=name)

    around = halos(*sides)
    image, mom0 = local(False, True, "apply0", k0, weights, design, design_t)
    k1, *sides = joined(image, around, 3, "add_halo1")
    around = halos(*sides)
    image, mom1 = local(True, True, "apply1", k1, weights, design, design_t, k0)
    k2, last, columns = joined(image, around, 2, "add_halo2")
    above, left = forward(last, "rows"), forward(columns, "ifg")
    (mom2,) = local(True, False, "apply2", k2, weights, design, design_t, k1)
    part = call(
        all_moments,
        sds((1, 128), F32),
        k2,
        above,
        left,
        mom0,
        mom1,
        mom2,
        name="all_moments",
    )
    for step in (1, 2):
        part = part + permute(part, "ifg", lambda i: i ^ step)
    parts = call(
        add_and_spread,
        sds((n_rows, 1, 128), F32),
        part,
        permute(part, "ifg", lambda i: i ^ 4),
        k0,
        name="add_and_spread",
    )
    parts = lax.all_to_all(parts, "rows", 0, 0, tiled=True)
    displacement = call(
        combine,
        sds((DATES * 8, 128), F32),
        parts,
        k0,
        k1,
        k2,
        out_specs=[pltpu.HBM],
        scratch=(pltpu.VMEM((DATES * 8, 128), F32), pltpu.SemaphoreType.DMA((4,))),
        name="combine",
    )
    return displacement.reshape(DATES, 8, 128), slope


def solution(mesh):
    placed = (
        P("ifg", "rows", None),
        P("ifg", "rows", None),
        P("rows", None),
        P("ifg", "rows"),
        P(),
    )
    return jax.shard_map(
        per_device,
        mesh=mesh,
        in_specs=placed,
        out_specs=(P(None, "rows", "ifg"), P("ifg")),
        check_vma=False,
    )
```

```python
import jax
import jax.numpy as jnp
from jax import lax
from jax.experimental import pallas as pl
from jax.experimental.pallas import tpu as pltpu
from jax.sharding import PartitionSpec as P

DATES = 300
DP = 304
SHIFT = 4.0
SMOOTHING_WEIGHT = 0.5
RIDGE_WEIGHT = 0.05
CENTRE = 4.0 * SMOOTHING_WEIGHT + RIDGE_WEIGHT - SHIFT
F32 = jnp.float32
BF16 = jnp.bfloat16


def sds(shape, dtype):
    return jax.ShapeDtypeStruct(shape, dtype)


def in_hbm(shape, dtype):
    return pltpu.HBM(shape, dtype)


def call(body, outs, *args, specs=None, out_specs=None, scratch=(), aliases=None, name=None):
    flat = outs if isinstance(outs, (list, tuple)) else [outs]
    places = specs or [pltpu.VMEM] * len(args)
    out_places = [pl.BlockSpec(memory_space=place) for place in out_specs or [pltpu.VMEM] * len(flat)]
    return pl.pallas_call(
        body,
        out_shape=outs,
        in_specs=[pl.BlockSpec(memory_space=place) for place in places],
        out_specs=out_places if isinstance(outs, (list, tuple)) else out_places[0],
        scratch_shapes=list(scratch),
        input_output_aliases=aliases or {},
        compiler_params=pltpu.CompilerParams(vmem_limit_bytes=16 * 1024 * 1024),
        name=name,
    )(*args)


def dot(a, b):
    return jnp.dot(a, b, preferred_element_type=F32)


def split(values):
    high = values.astype(BF16)
    return high, (values - high.astype(F32)).astype(BF16)


def rows_first(phase, coher, phase_t, coher_t, first, last, phase_in, coher_in, wide, sems):
    pairs = ((phase, phase_in, phase_t), (coher, coher_in, coher_t))

    def fetch(part, block):
        ifgs, _ = block_of(block)
        return pltpu.make_async_copy(pairs[part][0].at[ifgs], pairs[part][1].at[ifgs], sems.at[part, block])

    for block in range(4):
        for part in range(2):
            fetch(part, block).start()

    def group(block, _):
        ifgs, _ = block_of(block)
        for part, (_, source, target) in enumerate(pairs):
            fetch(part, block).wait()
            for tile in range(8):
                lanes = pl.ds(tile * 128, 128)
                wide[part, tile] = source[ifgs, :, lanes].astype(F32).reshape(128, 128)
                for row in range(8):
                    target[row, ifgs, lanes] = wide[part, tile, pl.ds(row, 16, stride=8), :].astype(BF16)
        return 0

    lax.fori_loop(0, 4, group, 0)
    for part, target in enumerate((phase_t, coher_t)):
        first[pl.ds(part * 64, 64), :] = target[0]
        last[pl.ds(part * 64, 64), :] = target[7]


def shifted_sum(values, lane, last):
    left = jnp.where(lane == 0, 0.0, pltpu.roll(values, 1, 1))
    right = jnp.where(lane == last, 0.0, pltpu.roll(values, last, 1))
    return values + left + right


def fold_lanes(values):
    total = values[:, :128]
    for tile in range(1, 8):
        total += values[:, tile * 128 : tile * 128 + 128]
    return total


OFFSETS = ((0, 0), (0, 1), (2, 0), (1, 0), (3, 0), (2, 1), (1, 1), (3, 1))


def other(index, chips, core):
    return (((index >> 1) + chips) & 3) * 2 + ((index & 1) ^ core)


def owner(step):
    return other(lax.axis_index("ifg"), *OFFSETS[step])


def smooth_row(rows, lane, mask, terrain):
    denom = shifted_sum(rows[0][0] + rows[1][0] + rows[2][0], lane, 1023)
    numer = shifted_sum(rows[0][1] + rows[1][1] + rows[2][1], lane, 1023)
    top = fold_lanes(numer * terrain)
    low = fold_lanes(denom * (terrain * terrain))
    return numer / denom, (mask * (denom / 9.0)).astype(BF16), top, low


def load_row(phase_t, coher_t, row, ifgs):
    coher = coher_t[row, ifgs, :].astype(F32)
    return coher, coher * phase_t[row, ifgs, :].astype(F32)


def block_of(block):
    return pl.ds(pl.multiple_of(block * 16, 16), 16), pl.ds(pl.multiple_of(block * 16 + 64, 16), 16)


def inner_rows(phase_t, coher_t, mask, height, smooth_out, totals, *rest):
    outs, weights, smooth, sems = rest[:8], *rest[8:]
    lane = lax.broadcasted_iota(jnp.int32, (16, 1024), 1)

    def copies(block):
        ifgs, _ = block_of(block)
        return [
            pltpu.make_async_copy(
                weights.at[owner(step), ifgs], out.at[ifgs, pl.ds(128, 768)], sems.at[block, step]
            )
            for step, out in enumerate(outs)
        ] + [pltpu.make_async_copy(smooth.at[:, ifgs], smooth_out.at[pl.ds(1, 6), ifgs], sems.at[block, 8])]

    def group(block, _):
        ifgs, lows = block_of(block)
        masks = mask[ifgs, :]
        rows = [load_row(phase_t, coher_t, row, ifgs) for row in (0, 1)]
        top = jnp.zeros((16, 128), F32)
        low = jnp.zeros((16, 128), F32)
        for row in range(1, 7):
            rows.append(load_row(phase_t, coher_t, row + 1, ifgs))
            value, weight, more_top, more_low = smooth_row(
                rows, lane, masks[:, row : row + 1], height[pl.ds(row, 1), :]
            )
            rows = rows[1:]
            top += more_top
            low += more_low
            smooth[row - 1, ifgs, :] = value
            for tile in range(8):
                weights[tile, ifgs, pl.ds((row - 1) * 128, 128)] = weight[:, tile * 128 : tile * 128 + 128]
        totals[ifgs, :] = top
        totals[lows, :] = low
        for copy in copies(block):
            copy.start()
        return 0

    lax.fori_loop(0, 4, group, 0)
    for block in range(4):
        for copy in copies(block):
            copy.wait()


def border_rows(phase_t, coher_t, above, below, mask, height, totals, *rest):
    smooth_out, sums, outs = rest[9], rest[10], rest[11:19]
    weights, smooth, added, sems = rest[19:]
    lane = lax.broadcasted_iota(jnp.int32, (16, 1024), 1)
    my_row = lax.axis_index("rows")
    valid = (my_row > 0, my_row < lax.axis_size("rows") - 1)

    def group(block, _):
        ifgs, lows = block_of(block)
        masks = mask[ifgs, :]
        top = totals[ifgs, :]
        low = totals[lows, :]
        for side, (edge, row) in enumerate(((above, 0), (below, 7))):
            coher = jnp.where(valid[side], edge[lows, :].astype(F32), 0.0)
            rows = [(coher, coher * edge[ifgs, :].astype(F32))]
            rows += [load_row(phase_t, coher_t, near, ifgs) for near in (row, 1 if row == 0 else 6)]
            value, weight, more_top, more_low = smooth_row(
                rows, lane, masks[:, row : row + 1], height[pl.ds(row, 1), :]
            )
            top += more_top
            low += more_low
            smooth[side, ifgs, :] = value
            for tile in range(8):
                weights[side, tile, ifgs, :] = weight[:, tile * 128 : tile * 128 + 128]
        added[ifgs, :] = top
        added[lows, :] = low
        return 0

    lax.fori_loop(0, 4, group, 0)
    copies = []
    for side, row in ((0, 0), (1, 7)):
        copies.append(pltpu.make_async_copy(smooth.at[side], smooth_out.at[row], sems.at[side, 8]))
        for step, out in enumerate(outs):
            lanes = pl.ds(row * 128, 128)
            copies.append(
                pltpu.make_async_copy(weights.at[side, owner(step)], out.at[:, lanes], sems.at[side, step])
            )
    for copy in copies:
        copy.start()
    sums[...] = jnp.broadcast_to(jnp.sum(added[...].T, axis=0)[None, None, :], sums.shape)
    for copy in copies:
        copy.wait()


def stage(source, out, sems):
    copies = [
        pltpu.make_async_copy(source.at[pl.ds(part * 2, 2)], out.at[pl.ds(part * 2, 2)], sems.at[part])
        for part in range(4)
    ]
    for copy in copies:
        copy.start()
    for copy in copies:
        copy.wait()


def correction(sums, smooth, height, slope_row, *rest):
    outs, blocks = rest[:8], rest[8]
    total = sums[0]
    for index in range(1, sums.shape[0]):
        total += sums[index]
    slope_row[...] = total / pltpu.roll(total, 64, 1)
    column = jnp.broadcast_to(total, (128, 128)).T
    slope = column[:64, :] / column[64:, :]

    def one_tile(tile, _):
        lanes = pl.ds(pl.multiple_of(tile * 128, 128), 128)
        for row in range(8):
            value = smooth[row, :, lanes] - slope * height[pl.ds(row, 1), lanes]
            blocks[tile, :, pl.ds(row * 128, 128)] = value.astype(BF16)
        return 0

    lax.fori_loop(0, 8, one_tile, 0)
    for step, out in enumerate(outs):
        out[...] = blocks[owner(step)]


def column_selector():
    row = lax.broadcasted_iota(jnp.int32, (16, 1024), 0)
    pixel = lax.broadcasted_iota(jnp.int32, (16, 1024), 1)
    wanted = jnp.where(row < 8, row * 128, (row - 8) * 128 + 127)
    return (pixel == wanted).astype(BF16)


def write_edges(field, last, columns, first=None):
    if first is not None:
        first[...] = field[:, pl.ds(0, 128)].astype(BF16)
    last[...] = field[:, pl.ds(896, 128)].astype(BF16)
    picked = lax.dot_general(
        column_selector(), field[...].astype(BF16), (((1,), (1,)), ((), ())), preferred_element_type=F32
    )
    columns[...] = picked.astype(BF16)


def right_side(*refs):
    weight_parts, corrected_parts = refs[:8], refs[8:16]
    design_t, field, weights, *edges = refs[16:]
    for part in range(8):
        weights[pl.ds(part * 64, 64), :] = weight_parts[part][...]

    def one_chunk(chunk, _):
        lanes = pl.ds(pl.multiple_of(chunk * 256, 256), 256)
        scaled = jnp.concatenate(
            [
                weight_parts[part][:, lanes].astype(F32) * corrected_parts[part][:, lanes].astype(F32)
                for part in range(8)
            ],
            axis=0,
        )
        high, low = split(scaled)
        field[:, lanes] = dot(design_t[...], high) + dot(design_t[...], low)
        return 0

    lax.fori_loop(0, 4, one_chunk, 0, unroll=True)
    write_edges(field, *edges)


def row_lanes(row):
    return pl.ds(pl.multiple_of(row * 128, 128), 128)


def local_image(field, weights, design, design_t, chunk, with_image):
    lanes = pl.ds(pl.multiple_of(chunk * 256, 256), 256)
    high, low = split(field[:, lanes])
    across = dot(design[...], jnp.concatenate([high, low], axis=0))
    scaled = across * weights[:, lanes].astype(F32)
    back, square = None, None
    if with_image:
        high, low = split(scaled)
        back = dot(design_t[...], high) + dot(design_t[...], low)
    else:
        square = across * scaled
    lane = lax.broadcasted_iota(jnp.int32, (DP, 128), 1)
    parts = []
    for offset in range(2):
        row = 2 * chunk + offset
        here = field[:, row_lanes(row)]
        around = jnp.where(lane == 0, 0.0, pltpu.roll(here, 1, 1))
        around += jnp.where(lane == 127, 0.0, pltpu.roll(here, 127, 1))
        around += jnp.where(row > 0, field[:, row_lanes(jnp.maximum(row - 1, 0))], 0.0)
        around += jnp.where(row < 7, field[:, row_lanes(jnp.minimum(row + 1, 7))], 0.0)
        part = CENTRE * here - SMOOTHING_WEIGHT * around
        if with_image:
            part = back[:, offset * 128 : offset * 128 + 128] + part
        parts.append((row, part))
    return parts, square


def fold(values):
    return jnp.sum(values.reshape(-1, 8, 128), axis=0)


def apply_local(with_before, with_image, *refs):
    field, weights, design, design_t = refs[:4]
    refs = refs[4:]
    before = None
    if with_before:
        before, refs = refs[0], refs[1:]
    image = None
    if with_image:
        image, refs = refs[0], refs[1:]
    moments = refs[0]

    def one_chunk(chunk, totals):
        square, cross, ahead = totals
        parts, across = local_image(field, weights, design, design_t, chunk, with_image)
        if not with_image:
            ahead += fold(across[:, :128]) + fold(across[:, 128:])
        for row, part in parts:
            here = field[:, row_lanes(row)]
            square += fold(here * here)
            if with_before:
                cross += fold(here * before[:, row_lanes(row)])
            if with_image:
                image[:, row_lanes(row)] = part
            else:
                ahead += fold(here * part)
        return square, cross, ahead

    zero = jnp.zeros((8, 128), F32)
    totals = lax.fori_loop(0, 4, one_chunk, (zero, zero, zero), unroll=True)
    for index in range(3):
        moments[index] = totals[index]


def spread_columns(columns, pixels):
    row = lax.broadcasted_iota(jnp.int32, (16, 128), 0)
    lane = lax.broadcasted_iota(jnp.int32, (16, 128), 1)
    wanted = jnp.where(row < 8, row, row - 8) == pixels
    place = (wanted & (lane == jnp.where(row < 8, 0, 127))).astype(BF16)
    return lax.dot_general(columns, place, (((0,), (0,)), ((), ())), preferred_element_type=F32)


def keep(flag, values):
    return jnp.where(flag, values.astype(F32), 0.0)


def inside():
    row, col = lax.axis_index("rows"), lax.axis_index("ifg")
    return row > 0, row < lax.axis_size("rows") - 1, col > 0, col < lax.axis_size("ifg") - 1


def add_halo(image, above, below, left, right, field, *edges):
    flags = inside()
    sides = jnp.concatenate([keep(flags[2], left[8:16, :]), keep(flags[3], right[0:8, :])], axis=0).astype(BF16)
    for row in range(8):
        lanes = pl.ds(row * 128, 128)
        halo = spread_columns(sides, row)
        if row == 0:
            halo += keep(flags[0], above[...])
        if row == 7:
            halo += keep(flags[1], below[...])
        field[:, lanes] = image[:, lanes] - SMOOTHING_WEIGHT * halo
    write_edges(field, *edges)


def all_moments(field, above, left, zero, one, two, out):
    flags = inside()
    sides = jnp.concatenate([keep(flags[2], left[8:16, :]), jnp.zeros((8, DP), F32)], axis=0).astype(BF16)
    ahead = two[2]
    for row in range(8):
        halo = spread_columns(sides, row)
        if row == 0:
            halo += keep(flags[0], above[...])
        ahead -= (2.0 * SMOOTHING_WEIGHT) * fold(field[:, pl.ds(row * 128, 128)] * halo)
    rows = [zero[0], one[1], one[0], two[1], two[0], ahead]
    lane = lax.broadcasted_iota(jnp.int32, (1, 128), 1)
    total = jnp.zeros((1, 128), F32)
    for index, values in enumerate(rows):
        line = jnp.sum(values, axis=0, keepdims=True)
        total += jnp.where(lane == index, jnp.sum(line, axis=1, keepdims=True), 0.0)
    out[...] = total


def add_and_spread(one, two, basis, out):
    out[...] = jnp.broadcast_to((one[...] + two[...])[None], out.shape)


def combine(parts, zero, one, two, out, field, sems):
    total = parts[0]
    for index in range(1, parts.shape[0]):
        total += parts[index]
    m0, m1, m2, m3, m4, m5 = (jnp.broadcast_to(total[:, i : i + 1], (1, 128)) for i in range(6))
    t00, t01, t11 = m1 + SHIFT * m0, m2 + SHIFT * m1, m3 + SHIFT * m2
    t12, t22 = m4 + SHIFT * m3, m5 + SHIFT * m4
    l10, l20 = t01 / t00, t11 / t00
    pivot = t11 - l10 * t01
    off = t12 - l20 * t01
    keep = pivot > 1e-6 * t11
    safe = jnp.where(keep, pivot, 1.0)
    l21 = jnp.where(keep, off / safe, 0.0)
    last = t22 - l20 * t11 - l21 * off
    keep_last = keep & (last > 1e-6 * t22)
    y1 = m1 - l10 * m0
    y2 = m2 - l20 * m0 - l21 * y1
    c2 = jnp.where(keep_last, y2 / jnp.where(keep_last, last, 1.0), 0.0)
    c1 = jnp.where(keep, y1 / safe, 0.0) - l21 * c2
    c0 = m0 / t00 - l10 * c1 - l20 * c2
    copies = []
    for part in range(4):
        count = min(80, DATES - part * 80)
        dates = pl.ds(part * 80, (count + 7) // 8 * 8)
        for row in range(8):
            lanes = pl.ds(row * 128, 128)
            value = c0 * zero[dates, lanes] + c1 * one[dates, lanes] + c2 * two[dates, lanes]
            field[pl.ds(part * 640 + row, count, stride=8), :] = value[:count, :]
        lines = pl.ds(part * 640, count * 8)
        copies.append(pltpu.make_async_copy(field.at[lines], out.at[lines], sems.at[part]))
        copies[-1].start()
    for copy in copies:
        copy.wait()


def per_device(phase, coherence, height, gap_mask, date_pairs):
    n_ifg, n_rows = lax.axis_size("ifg"), lax.axis_size("rows")
    me = lax.axis_index("ifg")

    def permute(values, axis, target):
        return lax.ppermute(values, axis, [(i, target(i)) for i in range(lax.axis_size(axis))])

    def forward(values, axis):
        return permute(values, axis, lambda i: (i + 1) % lax.axis_size(axis))

    def backward(values, axis):
        return permute(values, axis, lambda i: (i - 1) % lax.axis_size(axis))

    stacked = sds((8, 64, 1024), BF16)
    edge = sds((128, 1024), BF16)
    phase_t, coher_t, first, last = call(
        rows_first,
        (stacked, stacked, edge, edge),
        pltpu.with_memory_space_constraint(phase, pltpu.HBM),
        pltpu.with_memory_space_constraint(coherence, pltpu.HBM),
        specs=[pltpu.HBM] * 2,
        scratch=(
            pltpu.VMEM((64, 8, 1024), BF16),
            pltpu.VMEM((64, 8, 1024), BF16),
            pltpu.VMEM((2, 8, 128, 128), F32),
            pltpu.SemaphoreType.DMA((2, 4)),
        ),
        name="rows_first",
    )
    above, below = forward(last, "rows"), backward(first, "rows")
    mask = gap_mask.astype(F32)
    pieces = [in_hbm((64, 1024), BF16)] * 8
    smooth, totals, *weight_parts = call(
        inner_rows,
        [in_hbm((8, 64, 1024), F32), sds((128, 128), F32)] + pieces,
        phase_t,
        coher_t,
        mask,
        height,
        out_specs=[pltpu.HBM, pltpu.VMEM] + [pltpu.HBM] * 8,
        scratch=(
            pltpu.VMEM((8, 64, 768), BF16),
            pltpu.VMEM((6, 64, 1024), F32),
            pltpu.SemaphoreType.DMA((4, 9)),
        ),
        name="inner_rows",
    )
    smooth, sums, *weight_parts = call(
        border_rows,
        [in_hbm((8, 64, 1024), F32), sds((n_rows, 1, 128), F32)] + pieces,
        phase_t,
        coher_t,
        above,
        below,
        mask,
        height,
        totals,
        smooth,
        *weight_parts,
        specs=[pltpu.VMEM] * 7 + [pltpu.HBM] * 9,
        out_specs=[pltpu.HBM, pltpu.VMEM] + [pltpu.HBM] * 8,
        scratch=(
            pltpu.VMEM((2, 8, 64, 128), BF16),
            pltpu.VMEM((2, 64, 1024), F32),
            pltpu.VMEM((128, 128), F32),
            pltpu.SemaphoreType.DMA((2, 9)),
        ),
        aliases={7: 0, **{8 + step: 2 + step for step in range(8)}},
        name="border_rows",
    )

    def exchange(parts):
        return [parts[0]] + [
            permute(part, "ifg", lambda i: other(i, *offset))
            for part, offset in zip(parts[1:], OFFSETS[1:])
        ]

    weight_parts = exchange(weight_parts)
    sums, weight_parts[1] = lax.optimization_barrier((sums, weight_parts[1]))
    sums = lax.all_to_all(sums, "rows", 0, 0, tiled=True)
    sums, *weight_parts[2:5] = lax.optimization_barrier((sums, *weight_parts[2:5]))
    smooth = call(
        stage,
        sds((8, 64, 1024), F32),
        pltpu.with_memory_space_constraint(smooth, pltpu.HBM),
        specs=[pltpu.HBM],
        scratch=(pltpu.SemaphoreType.DMA((4,)),),
        name="stage",
    )
    slope_row, *corrected_parts = call(
        correction,
        [sds((1, 128), F32)] + [sds((64, 1024), BF16)] * 8,
        sums,
        smooth,
        height,
        scratch=(pltpu.VMEM((8, 64, 1024), BF16),),
        name="correction",
    )
    slope, corrected_parts[0] = lax.optimization_barrier((slope_row[0, :64], corrected_parts[0]))
    corrected_parts = exchange(corrected_parts)
    sources = jnp.stack([other(me, 4 - chips, core) for chips, core in OFFSETS])
    pairs = date_pairs.reshape(n_ifg, -1, 2)[sources].reshape(-1, 2)
    dates = jnp.arange(DP, dtype=jnp.int32)
    design = ((dates[None] == pairs[:, 1:2]).astype(F32) - (dates[None] == pairs[:, 0:1]).astype(F32)).astype(BF16)
    design_t = design.T
    design = jnp.concatenate([design, design], axis=1)

    field = sds((DP, 1024), F32)
    edges = (sds((DP, 128), BF16), sds((16, DP), BF16), sds((DP, 128), BF16))
    moments = sds((3, 8, 128), F32)
    k0, weights, *sides = call(
        right_side,
        (field, sds((512, 1024), BF16)) + edges,
        *weight_parts,
        *corrected_parts,
        design_t,
        name="right_side",
    )

    def halos(last, columns, first):
        return (
            forward(last, "rows"),
            backward(first, "rows"),
            forward(columns, "ifg"),
            backward(columns, "ifg"),
        )

    def local(with_before, with_image, name, *args):
        outs = ((field,) if with_image else ()) + (moments,)
        body = lambda *refs: apply_local(with_before, with_image, *refs)
        return call(body, outs, *args, name=name)

    def joined(image, around, count, name):
        return call(add_halo, (field,) + edges[:count], image, *around, name=name)

    around = halos(*sides)
    image, mom0 = local(False, True, "apply0", k0, weights, design, design_t)
    k1, *sides = joined(image, around, 3, "add_halo1")
    around = halos(*sides)
    image, mom1 = local(True, True, "apply1", k1, weights, design, design_t, k0)
    k2, last, columns = joined(image, around, 2, "add_halo2")
    above, left = forward(last, "rows"), forward(columns, "ifg")
    (mom2,) = local(True, False, "apply2", k2, weights, design, design_t, k1)
    part = call(
        all_moments,
        sds((1, 128), F32),
        k2,
        above,
        left,
        mom0,
        mom1,
        mom2,
        name="all_moments",
    )
    for step in (1, 2):
        part = part + permute(part, "ifg", lambda i: i ^ step)
    parts = call(
        add_and_spread,
        sds((n_rows, 1, 128), F32),
        part,
        permute(part, "ifg", lambda i: i ^ 4),
        k0,
        name="add_and_spread",
    )
    parts = lax.all_to_all(parts, "rows", 0, 0, tiled=True)
    displacement = call(
        combine,
        sds((DATES * 8, 128), F32),
        parts,
        k0,
        k1,
        k2,
        out_specs=[pltpu.HBM],
        scratch=(pltpu.VMEM((DATES * 8, 128), F32), pltpu.SemaphoreType.DMA((4,))),
        name="combine",
    )
    return displacement.reshape(DATES, 8, 128), slope


def solution(mesh):
    placed = (
        P("ifg", "rows", None),
        P("ifg", "rows", None),
        P("rows", None),
        P("ifg", "rows"),
        P(),
    )
    return jax.shard_map(
        per_device,
        mesh=mesh,
        in_specs=placed,
        out_specs=(P(None, "rows", "ifg"), P("ifg")),
        check_vma=False,
    )
```
